32 devices in a mesh: dp: 2 (over y), tok: 8 (over z, core), col: 2 (over x).
Axes of the slice: x: 2, y: 2, z: 4, core: 2. Of those that a mesh axis runs over, the one named last changes fastest.
Arguments:
- tokens: bfloat16 [2, 4096, 1024], P('dp', 'tok'), may hold values from -6 to 6
- ln_gain: bfloat16 [1024], replicated, may hold values from 0.099609375 to 1.8984375
- qkv_weight: bfloat16 [3, 1024, 512], P(None, None, 'col'), may hold values from -0.375 to 0.375
- out_weight: bfloat16 [512, 1024], P('col'), may hold values from -0.25 to 0.25
- readout_weight: bfloat16 [1024, 64], replicated, may hold values from -0.1875 to 0.1875
- conv_weight: bfloat16 [2, 64, 576], replicated, may hold values from -0.25 to 0.25
- head_weight: bfloat16 [2, 64], replicated, may hold values from -0.75 to 0.75
- holo_cot: float32 [2, 2, 16, 256], P('dp', None, 'tok', 'col'), may hold values from -2.5 to 2.5
Outputs:
- hologram: float32 [2, 2, 16, 256], P('dp', None, 'tok', 'col')
- conv_grad: float32 [2, 64, 576], replicated
- out_grad: float32 [512, 1024], P('col')
The draws below stay inside these ranges and needn't reach their ends.
All inputs are finite; a program needn't handle non-finite values.
Results may differ from the reference program's by a relative error of at most 0.017.
The reference program's roundings to bfloat16 on the way count: a program that leaves them out, or rounds other values in their place, can miss the bound.
Values may be sent and summed in bfloat16 or wider, within the bound.
No kernel may reach another device: no remote copies, remote signals or barrier semaphores. Data moves between devices by JAX's collectives and lax.ppermute only.
A program may use at most 128 MiB of HBM per device.

```python
import jax
import jax.numpy as jnp
from jax import lax

D = 1024
HEAD = 64
HEADS = 8
CH = 64
COLS = 256
LAYERS = 2
LENGTH = 4096
FRAMES = 2
ROWS = 16
HW = 512


def draw_tokens(key, part):
    noise = jax.random.normal(jax.random.fold_in(key, 11), (FRAMES, LENGTH, D), jnp.float32)
    return jnp.clip(noise, -6.0, 6.0).astype(jnp.bfloat16)


def draw_qkv_weight(key, part):
    factors = jnp.array([2.0, 2.0, 1.0], jnp.float32).reshape(3, 1, 1)
    drawn = jax.random.normal(jax.random.fold_in(key, 21), (3, D, HW), jnp.float32) * factors / jnp.sqrt(D * 1.0)
    bound = 12.0 / jnp.sqrt(D * 1.0)
    return jnp.clip(drawn, -bound, bound).astype(jnp.bfloat16)


def block_scale(stream_key, extent, cuts, least, largest):
    gain = 1.0
    for axis_at, blocks in cuts:
        heights = jax.random.uniform(jax.random.fold_in(jax.random.fold_in(stream_key, 6), axis_at), (blocks,), jnp.float32, least / len(cuts), largest / len(cuts))
        gain = gain * jnp.repeat(jnp.exp(heights), extent[axis_at] // blocks).reshape((-1,) + (1,) * (len(extent) - 1 - axis_at))
    return gain


def bell_draw(key, shape, scale, reach, cuts=(), kind=jnp.bfloat16):
    entries = jax.random.normal(key, shape, jnp.float32) * scale
    if len(cuts) > 0:
        entries = block_scale(key, shape, cuts, -0.22, 0.18) * entries
    return jnp.clip(entries, min=-reach, max=reach).astype(kind)


def setup_inputs(seed: int = 0) -> dict:
    arg_keys = jax.random.split(jax.random.key(seed), 9)
    return {
        "tokens": draw_tokens(jax.random.fold_in(arg_keys[8], 71), 0),
        "ln_gain": jnp.clip(1.0 + 0.18 * jax.random.normal(arg_keys[1], (D,), jnp.float32), 0.099609375, 1.8984375).astype(jnp.bfloat16),
        "qkv_weight": draw_qkv_weight(jax.random.fold_in(arg_keys[8], 71), 0),
        "out_weight": bell_draw(arg_keys[3], (HW, D), HW ** -0.5, 0.25, ((0, 2),)),
        "readout_weight": bell_draw(arg_keys[4], (D, CH), D ** -0.5, 0.1875),
        "conv_weight": bell_draw(arg_keys[5], (LAYERS, CH, 9 * CH), (9 * CH) ** -0.5, 0.25),
        "head_weight": bell_draw(arg_keys[6], (2, CH), CH ** -0.5, 0.75),
        "holo_cot": bell_draw(arg_keys[7], (FRAMES, 2, ROWS, COLS), (16.0 / (FRAMES * LENGTH) ** 0.5), 2.5, ((0, 2), (2, 8), (3, 2)), jnp.float32),
    }


EPSILON = 1e-05

def normalize(rows_in, ln_gain):
    values = rows_in.astype(jnp.float32)
    center = values - lax.optimization_barrier(jnp.mean(values, axis=-1, keepdims=True))
    spread = lax.optimization_barrier(jnp.mean(center * center, axis=-1, keepdims=True))
    return (center * lax.rsqrt(spread + EPSILON) * ln_gain.astype(jnp.float32)).astype(jnp.bfloat16)

def attend(queries, key_rows, value_rows):
    length = queries.shape[0]
    block_rows = min(512, length)
    query_blocks = queries.reshape(length // block_rows, block_rows, HEADS, HEAD)
    key_view = key_rows.reshape(length, HEADS, HEAD).astype(jnp.float32)
    value_view = value_rows.reshape(length, HEADS, HEAD)

    def one_block(query_block):
        scores = jnp.einsum('qhd,khd->hqk', query_block.astype(jnp.float32), key_view) * (1.0 / HEAD ** 0.5)
        row_top = lax.optimization_barrier(jnp.max(scores, axis=-1, keepdims=True))
        raised = jnp.exp(scores - row_top)
        row_total = lax.optimization_barrier(jnp.sum(raised, axis=-1))
        weights = raised.astype(jnp.bfloat16)
        weighted = jnp.einsum('hqk,khd->qhd', weights.astype(jnp.float32), value_view.astype(jnp.float32))
        return (weighted / jnp.transpose(row_total)[:, :, None]).astype(jnp.bfloat16)
    context = lax.map(one_block, query_blocks)
    return context.reshape(length, HEADS * HEAD)

def neighbourhood(padded, grid_rows, grid_cols):
    pieces = [padded[:, row_off:row_off + grid_rows, col_off:col_off + grid_cols] for row_off in range(3) for col_off in range(3)]
    return jnp.concatenate(pieces, axis=0).reshape(9 * padded.shape[0], grid_rows * grid_cols)

def flipped(padded, grid_rows, grid_cols):
    pieces = [padded[:, 2 - row_off:2 - row_off + grid_rows, 2 - col_off:2 - col_off + grid_cols] for row_off in range(3) for col_off in range(3)]
    return jnp.concatenate(pieces, axis=0).reshape(9 * padded.shape[0], grid_rows * grid_cols)

def transposed(weight):
    channels = weight.shape[0]
    return jnp.transpose(weight.reshape(channels, 9, channels), (2, 1, 0)).reshape(channels, 9 * channels)

def frame_network(first_map, conv_weight, head_weight, cotangent):
    channels, grid_rows, grid_cols = first_map.shape
    hidden = first_map
    inputs = []
    pre_acts = []
    for layer_at in range(LAYERS):
        padded = jnp.pad(hidden, ((0, 0), (1, 1), (1, 1)))
        stacked = neighbourhood(padded, grid_rows, grid_cols)
        pre_act = jnp.dot(conv_weight[layer_at], stacked, preferred_element_type=jnp.float32)
        inputs.append(stacked)
        pre_acts.append(pre_act)
        hidden = jax.nn.silu(pre_act).astype(jnp.bfloat16).reshape(channels, grid_rows, grid_cols)
    hologram = jnp.dot(head_weight, hidden.reshape(channels, -1), preferred_element_type=jnp.float32)
    grad_hidden = jnp.dot(jnp.transpose(head_weight.astype(jnp.float32)), cotangent.reshape(cotangent.shape[0], -1), precision=lax.Precision.HIGHEST).astype(jnp.bfloat16)
    conv_terms = [None] * LAYERS
    for layer_at in reversed(range(LAYERS)):
        pre_act = pre_acts[layer_at]
        sigmoid_pre = jax.nn.sigmoid(pre_act)
        grad_pre = (grad_hidden.reshape(channels, -1).astype(jnp.float32) * sigmoid_pre * (1.0 + pre_act * (1.0 - sigmoid_pre))).astype(jnp.bfloat16)
        conv_terms[layer_at] = lax.dot_general(grad_pre, inputs[layer_at], (((1,), (1,)), ((), ())), preferred_element_type=jnp.float32)
        padded = jnp.pad(grad_pre.reshape(channels, grid_rows, grid_cols), ((0, 0), (1, 1), (1, 1)))
        grad_hidden = jnp.dot(transposed(conv_weight[layer_at]), flipped(padded, grid_rows, grid_cols), preferred_element_type=jnp.float32).astype(jnp.bfloat16)
    return (hologram.reshape(cotangent.shape), jnp.stack(conv_terms), grad_hidden)

def reference(tokens, ln_gain, qkv_weight, out_weight, readout_weight, conv_weight, head_weight, holo_cot):

    def one_frame(inputs_pair):
        rows_in, cotangent = inputs_pair
        normed = normalize(rows_in, ln_gain)
        queries = jnp.dot(normed, qkv_weight[0], preferred_element_type=jnp.float32).astype(jnp.bfloat16)
        key_rows = jnp.dot(normed, qkv_weight[1], preferred_element_type=jnp.float32).astype(jnp.bfloat16)
        value_rows = jnp.dot(normed, qkv_weight[2], preferred_element_type=jnp.float32).astype(jnp.bfloat16)
        context = attend(queries, key_rows, value_rows)
        mixed = rows_in.astype(jnp.float32) + jnp.dot(context, out_weight, preferred_element_type=jnp.float32)
        readout = jnp.dot(mixed, readout_weight.astype(jnp.float32), precision=lax.Precision.HIGHEST).astype(jnp.bfloat16)
        first_map = jnp.transpose(readout).reshape(CH, ROWS, COLS)
        hologram, conv_terms, grad_readout = frame_network(first_map, conv_weight, head_weight, cotangent)
        small_term = lax.dot_general(context, grad_readout, (((0,), (1,)), ((), ())), preferred_element_type=jnp.float32)
        return (hologram, conv_terms, small_term)
    holograms, conv_all, small_all = lax.map(one_frame, (tokens, holo_cot))
    grad_small = lax.optimization_barrier(jnp.sum(small_all, axis=0))
    out_grad = jnp.dot(grad_small, jnp.transpose(readout_weight.astype(jnp.float32)), precision=lax.Precision.HIGHEST)
    return (holograms, lax.optimization_barrier(jnp.sum(conv_all, axis=0)), out_grad)
```

```python
import functools

import jax
import jax.numpy as jnp
from jax import lax
from jax.experimental import pallas as pl
from jax.experimental.pallas import tpu as pltpu
from jax.sharding import PartitionSpec as P

HEAD = 64
EPSILON = 1e-05
BF16 = jnp.bfloat16
F32 = jnp.float32
VMEM = pl.BlockSpec(memory_space=pltpu.VMEM)
SMEM = pl.BlockSpec(memory_space=pltpu.SMEM)
PARAMS = pltpu.CompilerParams(vmem_limit_bytes=48 * 2**20)
NT = (((1,), (1,)), ((), ()))
TN = (((0,), (0,)), ((), ()))


def dot(a, b):
    return jnp.dot(a, b, preferred_element_type=F32)


def split3(values):
    high = values.astype(BF16)
    rest = values - high.astype(F32)
    mid = rest.astype(BF16)
    low = (rest - mid.astype(F32)).astype(BF16)
    return high, mid, low


def project_kernel(place, tokens, gain, weight, mine, theirs):
    core = place[0]
    values = tokens[...].astype(F32)
    center = values - jnp.mean(values, axis=-1, keepdims=True)
    spread = jnp.mean(center * center, axis=-1, keepdims=True)
    normed = (center * lax.rsqrt(spread + EPSILON) * gain[...].astype(F32)).astype(BF16)
    kept = mine.shape[0] * HEAD
    for which, out in ((core, mine), (1 - core, theirs)):
        for member in range(3):
            part = weight[member, :, pl.ds(pl.multiple_of(which * kept, 128), kept)]
            rows = dot(normed, part).astype(BF16)
            if member == 0:
                rows = rows * jnp.asarray(1.0 / HEAD**0.5, BF16)
            turned = rows.T
            for head in range(mine.shape[0]):
                out[head, member * HEAD : (member + 1) * HEAD, :] = turned[head * HEAD : (head + 1) * HEAD, :]


def project(place, tokens, gain, weight):
    count, length = weight.shape[2] // HEAD // 2, tokens.shape[0]
    shape = jax.ShapeDtypeStruct((count, 3 * HEAD, length), BF16)
    return pl.pallas_call(
        project_kernel,
        out_shape=(shape, shape),
        in_specs=[SMEM, VMEM, VMEM, VMEM],
        out_specs=(VMEM, VMEM),
        compiler_params=PARAMS,
        name="project",
    )(place, tokens, gain, weight)


def absorb_kernel(first, *refs):
    if first:
        queries, block, out, top = refs
    else:
        queries, block, carried, carried_top, out, top = refs
    keys = block[:HEAD, :].T
    length = block.shape[1]
    values = jnp.concatenate([block[HEAD:, :], jnp.ones((16, length), BF16)], axis=0)
    width = min(512, queries.shape[1])
    depth = min(512, length)
    for at in range(0, queries.shape[1], width):
        part = queries[:, at : at + width]
        running = None if first else carried[:, at : at + width]
        best = None if first else carried_top[0:1, at : at + width]
        for below in range(0, length, depth):
            scores = dot(keys[below : below + depth], part)
            raised_top = jnp.max(scores, axis=0, keepdims=True)
            if best is not None:
                raised_top = jnp.maximum(best, raised_top)
            weights = jnp.exp(scores - raised_top).astype(BF16)
            added = dot(values[:, below : below + depth], weights)
            running = added if best is None else running * jnp.exp(best - raised_top) + added
            best = raised_top
        out[:, at : at + width] = running
        top[:, at : at + width] = jnp.broadcast_to(best, (8, width))


def absorb(queries, block, state):
    count = queries.shape[1]
    shapes = (jax.ShapeDtypeStruct((HEAD + 16, count), F32), jax.ShapeDtypeStruct((8, count), F32))
    first = state is None
    return pl.pallas_call(
        functools.partial(absorb_kernel, first),
        out_shape=shapes,
        in_specs=[VMEM] * (2 if first else 4),
        out_specs=(VMEM, VMEM),
        input_output_aliases={} if first else {2: 0, 3: 1},
        compiler_params=PARAMS,
        name="absorb",
    )(queries, block, *(() if first else state))


def finish_kernel(*refs):
    states, (folded, context, share) = refs[:-3], refs[-3:]
    for head, state in enumerate(states):
        context[head * HEAD : (head + 1) * HEAD, :] = (state[:HEAD, :] / state[HEAD : HEAD + 1, :]).astype(BF16)
    whole = context[...]
    share[...] = sum(dot(part, whole) for part in split3(folded[...]))


def finish(states, folded):
    count = states[0].shape[1]
    return pl.pallas_call(
        finish_kernel,
        out_shape=(
            jax.ShapeDtypeStruct((len(states) * HEAD, count), BF16),
            jax.ShapeDtypeStruct((folded.shape[0], count), F32),
        ),
        in_specs=[VMEM] * (len(states) + 1),
        out_specs=(VMEM, VMEM),
        compiler_params=PARAMS,
        name="finish",
    )(*states, folded)


def turned(values, step):
    return pltpu.roll(values, step % values.shape[1], 1)


def three_columns(values, cols):
    cells = values.shape[1]
    column = lax.rem(lax.broadcasted_iota(jnp.int32, (1, cells), 1), cols)
    wide = values.astype(F32)
    left = jnp.where(column == 0, 0.0, turned(wide, 1)).astype(BF16)
    right = jnp.where(column == cols - 1, 0.0, turned(wide, -1)).astype(BF16)
    return jnp.concatenate([left, values.astype(BF16), right], axis=0)


def three_rows(weights, columns, cols):
    cells = columns.shape[1] - 2 * cols
    return sum(dot(weights[a], columns[:, a * cols : a * cols + cells]) for a in range(3))


def network_kernel(
    cols, frame_rows, place, hidden, cotangent, forward, backward, head, context, holo, sums, gradient, pre_one, pre_two
):
    core, half, row_at = place[0], place[1], place[2]
    own = context.shape[1]
    cells = hidden.shape[1]
    rim = (cells - own) // 2
    row_count = cells // cols
    above = rim // cols
    first_row = row_at - above

    def inside(start_row, rows):
        lane = lax.broadcasted_iota(jnp.int32, (1, rows * cols), 1)
        frame_lane = lane + (first_row + start_row) * cols
        return jnp.logical_and(frame_lane >= 0, frame_lane < frame_rows * cols)

    columns_zero = three_columns(hidden[...], cols)
    first = three_rows(forward[0], columns_zero, cols)
    rows_one = row_count - 2
    one = jnp.where(inside(1, rows_one), first * jax.nn.sigmoid(first), 0.0)
    columns_one = three_columns(one, cols)
    second = three_rows(forward[1], columns_one, cols)
    rows_two = row_count - 4
    sigmoid_two = jax.nn.sigmoid(second)
    two = (second * sigmoid_two).astype(BF16)
    holo[...] = dot(head[...], two[:, rim - 2 * cols : rim - 2 * cols + own])
    grad_two = lax.dot_general(
        head[...].astype(F32), cotangent[...], TN, precision=lax.Precision.HIGHEST, preferred_element_type=F32
    ).astype(BF16)
    slope = grad_two.astype(F32) * sigmoid_two * (1.0 + second * (1.0 - sigmoid_two))
    pre_grad_two = jnp.where(inside(2, rows_two), slope, 0.0)
    grad_one = three_rows(backward[1], three_columns(pre_grad_two, cols), cols).astype(BF16)
    rows_grad = row_count - 6
    middle = first[:, 2 * cols : 2 * cols + rows_grad * cols]
    sigmoid_one = jax.nn.sigmoid(middle)
    slope = grad_one.astype(F32) * sigmoid_one * (1.0 + middle * (1.0 - sigmoid_one))
    pre_grad_one = jnp.where(inside(3, rows_grad), slope, 0.0)
    grad_zero = three_rows(backward[0], three_columns(pre_grad_one, cols), cols).astype(BF16)
    pre_one[...] = pre_grad_one[:, rim - 3 * cols : rim - 3 * cols + own].astype(BF16)
    pre_two[...] = pre_grad_two[:, rim - 2 * cols : rim - 2 * cols + own].astype(BF16)

    share = sums.shape[0]
    taps = 9 * hidden.shape[0]
    for layer, (pre, columns, offset) in enumerate(((pre_one, columns_zero, rim), (pre_two, columns_one, rim - cols))):

        @pl.when(core == layer)
        def _(pre=pre, columns=columns, offset=offset):
            stacked = jnp.concatenate(
                [columns[:, offset + (a - 1) * cols : offset + (a - 1) * cols + own] for a in range(3)], axis=0
            )
            rows = pre[pl.ds(pl.multiple_of(half * share, 16), share), :]
            sums[:, :taps] = lax.dot_general(rows, stacked, NT, preferred_element_type=F32)

    piece = own // 2
    total = None
    for side in range(2):
        where = lax.rem(core + side, 2)
        seen = context[:, pl.ds(pl.multiple_of(where * piece, 128), piece)]
        term = lax.dot_general(
            grad_zero[:, side * piece : (side + 1) * piece], seen, NT, preferred_element_type=F32
        )
        total = term if total is None else total + term
    gradient[...] = total


def network(place, hidden, cotangent, forward, backward, head, context, cols, frame_rows, col_count):
    own = context.shape[1]
    channels = hidden.shape[0]
    return pl.pallas_call(
        functools.partial(network_kernel, cols, frame_rows),
        out_shape=(
            jax.ShapeDtypeStruct((head.shape[0], own), F32),
            jax.ShapeDtypeStruct((channels // col_count, 9 * channels), F32),
            jax.ShapeDtypeStruct((channels, context.shape[0]), F32),
        ),
        in_specs=[SMEM] + [VMEM] * 6,
        out_specs=(VMEM,) * 3,
        scratch_shapes=[pltpu.VMEM((channels, own), BF16)] * 2,
        compiler_params=PARAMS,
        name="network",
    )(place, hidden, cotangent, forward, backward, head, context)


def swapped(values, axis):
    size = lax.axis_size(axis)
    return lax.ppermute(values, axis, [(i, i ^ 1) for i in range(size)])


def passed(values, axis, step, wrap):
    size = lax.axis_size(axis)
    pairs = [(i, (i + step) % size) for i in range(size) if wrap or 0 <= i + step < size]
    return lax.ppermute(values, axis, pairs)


def in_order(core, mine, theirs, axis):
    return jnp.where(
        core == 0, jnp.concatenate([mine, theirs], axis=axis), jnp.concatenate([theirs, mine], axis=axis)
    )


def shards(
    tokens, ln_gain, qkv_weight, out_weight, readout_weight, conv_weight, head_weight, holo_cot
):
    frame_rows = tokens[0]
    cotangent = holo_cot[0]
    rows_dev, cols_dev = cotangent.shape[1:]
    tok_count, col_count, dp_count = (lax.axis_size(axis) for axis in ("tok", "col", "dp"))
    chips = tok_count // 2
    tok_at, half = lax.axis_index("tok"), lax.axis_index("col")
    core = lax.rem(tok_at, 2)
    chip_row = (tok_at - core) * rows_dev
    place = jnp.stack([core, half, chip_row]).astype(jnp.int32)
    layers, channels = conv_weight.shape[:2]
    cols = cols_dev * col_count
    length = frame_rows.shape[0]

    mine, theirs = project(place, frame_rows, ln_gain.reshape(1, -1), qkv_weight)
    joined = jnp.concatenate([mine, swapped(theirs, "tok")], axis=2)
    count = joined.shape[0]
    queries = [joined[head, :HEAD] for head in range(count)]
    blocks = [joined[head, HEAD:] for head in range(count)]
    states = [None] * count
    for turn in range(chips):
        arriving = [passed(block, "tok", 2, True) for block in blocks] if turn < chips - 1 else None
        states = [absorb(queries[head], blocks[head], states[head]) for head in range(count)]
        blocks = arriving

    kept = count * HEAD
    own_out = lax.dynamic_slice_in_dim(out_weight, core * kept, kept, 0)
    folded = lax.dot_general(readout_weight, own_out, (((0,), (1,)), ((), ())), preferred_element_type=F32)
    direct = lax.dot_general(readout_weight, frame_rows, (((0,), (1,)), ((), ())), preferred_element_type=F32)
    context, share = finish([state[0] for state in states], folded)
    partial = share[:, :length] + swapped(share[:, length:], "tok")
    own_map = (partial + swapped(partial, "col") + direct).astype(BF16)
    chip_map = in_order(core, own_map, swapped(own_map, "tok"), 1)
    rows_chip = 2 * rows_dev
    hidden = jnp.concatenate(
        [passed(chip_map, "tok", 2, False), chip_map, passed(chip_map, "tok", -2, False)], axis=1
    )

    wide_cot = in_order(half, cotangent, swapped(cotangent, "col"), 2)
    chip_cot = in_order(core, wide_cot, swapped(wide_cot, "tok"), 1)
    edge = chip_cot.shape[1] - 2
    cot_rows = jnp.concatenate(
        [passed(chip_cot[:, edge:], "tok", 2, False), chip_cot, passed(chip_cot[:, :2], "tok", -2, False)], axis=1
    )
    taps = conv_weight.reshape(layers, channels, 3, 3, channels)
    forward = jnp.transpose(taps.reshape(layers, channels, 3, 3 * channels), (0, 2, 1, 3))
    backward = jnp.transpose(taps[:, :, ::-1, ::-1, :], (0, 2, 4, 3, 1)).reshape(layers, 3, channels, 3 * channels)
    holo, sums, gradient = network(
        place, hidden, cot_rows.reshape(cot_rows.shape[0], -1), forward, backward, head_weight, context, cols,
        tok_count * rows_dev, col_count,
    )
    holo = holo.reshape(-1, rows_chip, cols)
    hologram = lax.dynamic_slice(
        holo, (0, core * rows_dev, half * cols_dev), (holo.shape[0], rows_dev, cols_dev)
    )

    taps_wide = sums.shape[1]
    lanes = 128 * ((taps_wide + 127) // 128)
    rows = sums.shape[0]
    pieces = gradient.shape[0] // rows
    folded_gradient = [gradient[at * rows : (at + 1) * rows] for at in range(pieces)]
    sent = jnp.concatenate([jnp.pad(sums, ((0, 0), (0, lanes - taps_wide))), *folded_gradient], axis=1)
    summed = sent
    for step in range(1, dp_count):
        summed = summed + passed(sent, "dp", step, True)
    total = summed
    for step in range(1, chips):
        total = total + passed(summed, "tok", 2 * step, True)
    own_grad = total[:, :taps_wide]
    layer_grad = in_order(half, own_grad, swapped(own_grad, "col"), 0)
    other_grad = swapped(layer_grad, "tok")
    conv_grad = in_order(core, layer_grad[None], other_grad[None], 0)
    wide = gradient.shape[1]
    own_small = jnp.concatenate(
        [total[:, lanes + at * wide : lanes + (at + 1) * wide] for at in range(pieces)], axis=0
    )
    small = in_order(core, own_small, swapped(own_small, "tok"), 1)
    out_grad = lax.dot_general(
        small, readout_weight.astype(F32), (((0,), (1,)), ((), ())), precision=lax.Precision.HIGHEST
    )
    return (hologram[None], conv_grad, out_grad)


def solution(mesh):
    in_specs = (
        P("dp", "tok", None),
        P(),
        P(None, None, "col"),
        P("col", None),
        P(),
        P(),
        P(),
        P("dp", None, "tok", "col"),
    )
    out_specs = (P("dp", None, "tok", "col"), P(), P("col", None))
    return jax.shard_map(shards, mesh=mesh, in_specs=in_specs, out_specs=out_specs, check_vma=False)
```

```python
import functools

import jax
import jax.numpy as jnp
from jax import lax
from jax.experimental import pallas as pl
from jax.experimental.pallas import tpu as pltpu
from jax.sharding import PartitionSpec as P

HEAD = 64
EPSILON = 1e-05
BF16 = jnp.bfloat16
F32 = jnp.float32
VMEM = pl.BlockSpec(memory_space=pltpu.VMEM)
SMEM = pl.BlockSpec(memory_space=pltpu.SMEM)
PARAMS = pltpu.CompilerParams(vmem_limit_bytes=48 * 2**20)
NT = (((1,), (1,)), ((), ()))
TN = (((0,), (0,)), ((), ()))


def dot(a, b):
    return jnp.dot(a, b, preferred_element_type=F32)


def split3(values):
    high = values.astype(BF16)
    rest = values - high.astype(F32)
    mid = rest.astype(BF16)
    low = (rest - mid.astype(F32)).astype(BF16)
    return high, mid, low


def project_kernel(place, tokens, gain, weight, mine, theirs, rows, parts, normed, token_sems, weight_sems):
    core = place[0]
    pieces = token_sems.shape[0]
    size = rows.shape[0] // pieces
    token_copies = [
        pltpu.make_async_copy(
            tokens.at[pl.ds(at * size, size)], rows.at[pl.ds(at * size, size)], token_sems.at[at]
        )
        for at in range(pieces)
    ]
    weight_copies = [
        pltpu.make_async_copy(weight.at[member], parts.at[member], weight_sems.at[member]) for member in range(3)
    ]
    for copy in token_copies + weight_copies:
        copy.start()
    wide_gain = gain[...].astype(F32)
    for at, copy in enumerate(token_copies):
        copy.wait()
        values = rows[at * size : (at + 1) * size, :].astype(F32)
        center = values - jnp.mean(values, axis=-1, keepdims=True)
        spread = jnp.mean(center * center, axis=-1, keepdims=True)
        normed[at * size : (at + 1) * size, :] = (center * lax.rsqrt(spread + EPSILON) * wide_gain).astype(BF16)
    kept = mine.shape[0] * HEAD
    for member, copy in enumerate(weight_copies):
        copy.wait()
        for which, out in ((core, mine), (1 - core, theirs)):
            part = parts[member, :, pl.ds(pl.multiple_of(which * kept, 128), kept)]
            product = dot(normed[...], part).astype(BF16)
            if member == 0:
                product = product * jnp.asarray(1.0 / HEAD**0.5, BF16)
            turned = product.T
            for head in range(mine.shape[0]):
                out[head, member * HEAD : (member + 1) * HEAD, :] = turned[head * HEAD : (head + 1) * HEAD, :]


def project(place, tokens, gain, weight):
    count, length = weight.shape[2] // HEAD // 2, tokens.shape[0]
    shape = jax.ShapeDtypeStruct((count, 3 * HEAD, length), BF16)
    pieces = 4 if length % 64 == 0 else 1
    anywhere = pl.BlockSpec(memory_space=pltpu.HBM)
    return pl.pallas_call(
        project_kernel,
        out_shape=(shape, shape),
        in_specs=[SMEM, anywhere, VMEM, anywhere],
        out_specs=(VMEM, VMEM),
        scratch_shapes=[
            pltpu.VMEM(tokens.shape, BF16),
            pltpu.VMEM(weight.shape, BF16),
            pltpu.VMEM(tokens.shape, BF16),
            pltpu.SemaphoreType.DMA((pieces,)),
            pltpu.SemaphoreType.DMA((3,)),
        ],
        compiler_params=PARAMS,
        name="project",
    )(place, tokens, gain, weight)


def absorb_kernel(first, *refs):
    if first:
        queries, block, out, top = refs
    else:
        queries, block, carried, carried_top, out, top = refs
    keys = block[:HEAD, :].T
    length = block.shape[1]
    values = jnp.concatenate([block[HEAD:, :], jnp.ones((16, length), BF16)], axis=0)
    width = min(512, queries.shape[1])
    depth = min(512, length)
    for at in range(0, queries.shape[1], width):
        part = queries[:, at : at + width]
        running = None if first else carried[:, at : at + width]
        best = None if first else carried_top[0:1, at : at + width]
        for below in range(0, length, depth):
            scores = dot(keys[below : below + depth], part)
            raised_top = jnp.max(scores, axis=0, keepdims=True)
            if best is not None:
                raised_top = jnp.maximum(best, raised_top)
            weights = jnp.exp(scores - raised_top).astype(BF16)
            added = dot(values[:, below : below + depth], weights)
            running = added if best is None else running * jnp.exp(best - raised_top) + added
            best = raised_top
        out[:, at : at + width] = running
        top[:, at : at + width] = jnp.broadcast_to(best, (8, width))


def absorb(queries, block, state):
    count = queries.shape[1]
    shapes = (jax.ShapeDtypeStruct((HEAD + 16, count), F32), jax.ShapeDtypeStruct((8, count), F32))
    first = state is None
    return pl.pallas_call(
        functools.partial(absorb_kernel, first),
        out_shape=shapes,
        in_specs=[VMEM] * (2 if first else 4),
        out_specs=(VMEM, VMEM),
        input_output_aliases={} if first else {2: 0, 3: 1},
        compiler_params=PARAMS,
        name="absorb",
    )(queries, block, *(() if first else state))


def finish_kernel(*refs):
    states, (folded, context, share) = refs[:-3], refs[-3:]
    for head, state in enumerate(states):
        context[head * HEAD : (head + 1) * HEAD, :] = (state[:HEAD, :] / state[HEAD : HEAD + 1, :]).astype(BF16)
    whole = context[...]
    share[...] = sum(dot(part, whole) for part in split3(folded[...]))


def finish(states, folded):
    count = states[0].shape[1]
    return pl.pallas_call(
        finish_kernel,
        out_shape=(
            jax.ShapeDtypeStruct((len(states) * HEAD, count), BF16),
            jax.ShapeDtypeStruct((folded.shape[0], count), F32),
        ),
        in_specs=[VMEM] * (len(states) + 1),
        out_specs=(VMEM, VMEM),
        compiler_params=PARAMS,
        name="finish",
    )(*states, folded)


def turned(values, step):
    return pltpu.roll(values, step % values.shape[1], 1)


def three_columns(values, cols):
    cells = values.shape[1]
    column = lax.rem(lax.broadcasted_iota(jnp.int32, (1, cells), 1), cols)
    wide = values.astype(F32)
    left = jnp.where(column == 0, 0.0, turned(wide, 1)).astype(BF16)
    right = jnp.where(column == cols - 1, 0.0, turned(wide, -1)).astype(BF16)
    return jnp.concatenate([left, values.astype(BF16), right], axis=0)


def three_rows(weights, columns, cols):
    cells = columns.shape[1] - 2 * cols
    return sum(dot(weights[a], columns[:, a * cols : a * cols + cells]) for a in range(3))


def network_kernel(
    cols, frame_rows, place, hidden, cotangent, forward, backward, head, context, holo, sums, gradient, pre_one, pre_two
):
    core, half, row_at = place[0], place[1], place[2]
    own = context.shape[1]
    cells = hidden.shape[1]
    rim = (cells - own) // 2
    row_count = cells // cols
    above = rim // cols
    first_row = row_at - above

    def inside(start_row, rows):
        lane = lax.broadcasted_iota(jnp.int32, (1, rows * cols), 1)
        frame_lane = lane + (first_row + start_row) * cols
        return jnp.logical_and(frame_lane >= 0, frame_lane < frame_rows * cols)

    columns_zero = three_columns(hidden[...], cols)
    first = three_rows(forward[0], columns_zero, cols)
    rows_one = row_count - 2
    one = jnp.where(inside(1, rows_one), first * jax.nn.sigmoid(first), 0.0)
    columns_one = three_columns(one, cols)
    second = three_rows(forward[1], columns_one, cols)
    rows_two = row_count - 4
    sigmoid_two = jax.nn.sigmoid(second)
    two = (second * sigmoid_two).astype(BF16)
    holo[...] = dot(head[...], two[:, rim - 2 * cols : rim - 2 * cols + own])
    grad_two = lax.dot_general(
        head[...].astype(F32), cotangent[...], TN, precision=lax.Precision.HIGHEST, preferred_element_type=F32
    ).astype(BF16)
    slope = grad_two.astype(F32) * sigmoid_two * (1.0 + second * (1.0 - sigmoid_two))
    pre_grad_two = jnp.where(inside(2, rows_two), slope, 0.0)
    grad_one = three_rows(backward[1], three_columns(pre_grad_two, cols), cols).astype(BF16)
    rows_grad = row_count - 6
    middle = first[:, 2 * cols : 2 * cols + rows_grad * cols]
    sigmoid_one = jax.nn.sigmoid(middle)
    slope = grad_one.astype(F32) * sigmoid_one * (1.0 + middle * (1.0 - sigmoid_one))
    pre_grad_one = jnp.where(inside(3, rows_grad), slope, 0.0)
    grad_zero = three_rows(backward[0], three_columns(pre_grad_one, cols), cols).astype(BF16)
    pre_one[...] = pre_grad_one[:, rim - 3 * cols : rim - 3 * cols + own].astype(BF16)
    pre_two[...] = pre_grad_two[:, rim - 2 * cols : rim - 2 * cols + own].astype(BF16)

    share = sums.shape[0]
    taps = 9 * hidden.shape[0]
    for layer, (pre, columns, offset) in enumerate(((pre_one, columns_zero, rim), (pre_two, columns_one, rim - cols))):

        @pl.when(core == layer)
        def _(pre=pre, columns=columns, offset=offset):
            stacked = jnp.concatenate(
                [columns[:, offset + (a - 1) * cols : offset + (a - 1) * cols + own] for a in range(3)], axis=0
            )
            rows = pre[pl.ds(pl.multiple_of(half * share, 16), share), :]
            sums[:, :taps] = lax.dot_general(rows, stacked, NT, preferred_element_type=F32)

    piece = own // 2
    total = None
    for side in range(2):
        where = lax.rem(core + side, 2)
        seen = context[:, pl.ds(pl.multiple_of(where * piece, 128), piece)]
        term = lax.dot_general(
            grad_zero[:, side * piece : (side + 1) * piece], seen, NT, preferred_element_type=F32
        )
        total = term if total is None else total + term
    gradient[...] = total


def network(place, hidden, cotangent, forward, backward, head, context, cols, frame_rows, col_count):
    own = context.shape[1]
    channels = hidden.shape[0]
    return pl.pallas_call(
        functools.partial(network_kernel, cols, frame_rows),
        out_shape=(
            jax.ShapeDtypeStruct((head.shape[0], own), F32),
            jax.ShapeDtypeStruct((channels // col_count, 9 * channels), F32),
            jax.ShapeDtypeStruct((channels, context.shape[0]), F32),
        ),
        in_specs=[SMEM] + [VMEM] * 6,
        out_specs=(VMEM,) * 3,
        scratch_shapes=[pltpu.VMEM((channels, own), BF16)] * 2,
        compiler_params=PARAMS,
        name="network",
    )(place, hidden, cotangent, forward, backward, head, context)


def swapped(values, axis):
    size = lax.axis_size(axis)
    return lax.ppermute(values, axis, [(i, i ^ 1) for i in range(size)])


def passed(values, axis, step, wrap):
    size = lax.axis_size(axis)
    pairs = [(i, (i + step) % size) for i in range(size) if wrap or 0 <= i + step < size]
    return lax.ppermute(values, axis, pairs)


def in_order(core, mine, theirs, axis):
    return jnp.where(
        core == 0, jnp.concatenate([mine, theirs], axis=axis), jnp.concatenate([theirs, mine], axis=axis)
    )


def shards(
    tokens, ln_gain, qkv_weight, out_weight, readout_weight, conv_weight, head_weight, holo_cot
):
    frame_rows = tokens[0]
    cotangent = holo_cot[0]
    rows_dev, cols_dev = cotangent.shape[1:]
    tok_count, col_count, dp_count = (lax.axis_size(axis) for axis in ("tok", "col", "dp"))
    chips = tok_count // 2
    tok_at, half = lax.axis_index("tok"), lax.axis_index("col")
    core = lax.rem(tok_at, 2)
    chip_row = (tok_at - core) * rows_dev
    place = jnp.stack([core, half, chip_row]).astype(jnp.int32)
    layers, channels = conv_weight.shape[:2]
    cols = cols_dev * col_count
    length = frame_rows.shape[0]

    mine, theirs = project(place, frame_rows, ln_gain.reshape(1, -1), qkv_weight)
    joined = jnp.concatenate([mine, swapped(theirs, "tok")], axis=2)
    count = joined.shape[0]
    kept = count * HEAD
    queries = [joined[head, :HEAD] for head in range(count)]
    blocks = [joined[head, HEAD:] for head in range(count)]
    states = [None] * count

    def weights_stage(_):
        taps = conv_weight.reshape(layers, channels, 3, 3, channels)
        forward = jnp.transpose(taps.reshape(layers, channels, 3, 3 * channels), (0, 2, 1, 3))
        backward = jnp.transpose(taps[:, :, ::-1, ::-1, :], (0, 2, 4, 3, 1)).reshape(
            layers, 3, channels, 3 * channels
        )
        own_out = lax.dynamic_slice_in_dim(out_weight, core * kept, kept, 0)
        folded = lax.dot_general(readout_weight, own_out, (((0,), (1,)), ((), ())), preferred_element_type=F32)
        direct = lax.dot_general(readout_weight, frame_rows, (((0,), (1,)), ((), ())), preferred_element_type=F32)
        return (forward, backward, folded, direct)

    def cotangent_stage(_):
        wide = in_order(half, cotangent, swapped(cotangent, "col"), 2)
        return in_order(core, wide, swapped(wide, "tok"), 1)

    def rim_stage(chip_cot):
        edge = chip_cot.shape[1] - 2
        before, after = passed(chip_cot[:, edge:], "tok", 2, False), passed(chip_cot[:, :2], "tok", -2, False)
        return jnp.concatenate([before, chip_cot, after], axis=1)

    stages = [weights_stage, cotangent_stage, rim_stage]
    results, held = [], None
    for turn in range(chips):
        arriving = [passed(block, "tok", 2, True) for block in blocks] if turn < chips - 1 else None
        states = [absorb(queries[head], blocks[head], states[head]) for head in range(count)]
        if stages:
            held = stages.pop(0)(held)
            results.append(held)
        if arriving is not None:
            tied = [lax.optimization_barrier((arriving[head], states[head])) for head in range(count)]
            blocks, states = [pair[0] for pair in tied], [pair[1] for pair in tied]
            if held is not None and turn < len(results):
                blocks[-1], held = lax.optimization_barrier((blocks[-1], held))
                results[-1] = held
    for stage in stages:
        held = stage(held)
        results.append(held)
    forward, backward, folded, direct = results[0]
    cot_rows = results[2]

    context, share = finish([state[0] for state in states], folded)
    partial = share[:, :length] + swapped(share[:, length:], "tok")
    own_map = (partial + swapped(partial, "col") + direct).astype(BF16)
    chip_map = in_order(core, own_map, swapped(own_map, "tok"), 1)
    rows_chip = 2 * rows_dev
    hidden = jnp.concatenate(
        [passed(chip_map, "tok", 2, False), chip_map, passed(chip_map, "tok", -2, False)], axis=1
    )

    holo, sums, gradient = network(
        place, hidden, cot_rows.reshape(cot_rows.shape[0], -1), forward, backward, head_weight, context, cols,
        tok_count * rows_dev, col_count,
    )
    holo = holo.reshape(-1, rows_chip, cols)
    hologram = lax.dynamic_slice(
        holo, (0, core * rows_dev, half * cols_dev), (holo.shape[0], rows_dev, cols_dev)
    )

    taps_wide = sums.shape[1]
    lanes = 128 * ((taps_wide + 127) // 128)
    rows = sums.shape[0]
    pieces = gradient.shape[0] // rows
    folded_gradient = [gradient[at * rows : (at + 1) * rows] for at in range(pieces)]
    sent = jnp.concatenate([jnp.pad(sums, ((0, 0), (0, lanes - taps_wide))), *folded_gradient], axis=1)
    summed = sent
    for step in range(1, dp_count):
        summed = summed + passed(sent, "dp", step, True)
    total = summed
    for step in range(1, chips):
        total = total + passed(summed, "tok", 2 * step, True)
    own_grad = total[:, :taps_wide]
    col_grad = swapped(own_grad, "col")
    wide = gradient.shape[1]
    own_small = jnp.concatenate(
        [total[:, lanes + at * wide : lanes + (at + 1) * wide] for at in range(pieces)], axis=0
    )
    small = in_order(core, own_small, swapped(own_small, "tok"), 1)
    out_grad = lax.dot_general(
        small, readout_weight.astype(F32), (((0,), (1,)), ((), ())), precision=lax.Precision.HIGHEST
    )
    col_grad, out_grad = lax.optimization_barrier((col_grad, out_grad))
    layer_grad = in_order(half, own_grad, col_grad, 0)
    other_grad = swapped(layer_grad, "tok")
    conv_grad = in_order(core, layer_grad[None], other_grad[None], 0)
    return (hologram[None], conv_grad, out_grad)


def solution(mesh):
    in_specs = (
        P("dp", "tok", None),
        P(),
        P(None, None, "col"),
        P("col", None),
        P(),
        P(),
        P(),
        P("dp", None, "tok", "col"),
    )
    out_specs = (P("dp", None, "tok", "col"), P(), P("col", None))
    return jax.shard_map(shards, mesh=mesh, in_specs=in_specs, out_specs=out_specs, check_vma=False)
```

```python
import functools

import jax
import jax.numpy as jnp
from jax import lax
from jax.experimental import pallas as pl
from jax.experimental.pallas import tpu as pltpu
from jax.sharding import PartitionSpec as P

HEAD = 64
EPSILON = 1e-05
BF16 = jnp.bfloat16
F32 = jnp.float32
VMEM = pl.BlockSpec(memory_space=pltpu.VMEM)
SMEM = pl.BlockSpec(memory_space=pltpu.SMEM)
PARAMS = pltpu.CompilerParams(vmem_limit_bytes=48 * 2**20)
NT = (((1,), (1,)), ((), ()))
TN = (((0,), (0,)), ((), ()))


def dot(a, b):
    return jnp.dot(a, b, preferred_element_type=F32)


def split3(values):
    high = values.astype(BF16)
    rest = values - high.astype(F32)
    mid = rest.astype(BF16)
    low = (rest - mid.astype(F32)).astype(BF16)
    return high, mid, low


def normalize_kernel(tokens, gain, normed):
    values = tokens[...].astype(F32)
    center = values - jnp.mean(values, axis=-1, keepdims=True)
    spread = jnp.mean(center * center, axis=-1, keepdims=True)
    wide_gain = gain[...].astype(F32)[None, :]
    normed[...] = (center * lax.rsqrt(spread + EPSILON) * wide_gain).astype(BF16)


def normalize(tokens, gain):
    return pl.pallas_call(
        normalize_kernel,
        out_shape=jax.ShapeDtypeStruct(tokens.shape, BF16),
        in_specs=[VMEM, VMEM],
        out_specs=VMEM,
        compiler_params=PARAMS,
        name="normalize",
    )(tokens, gain)


def project_kernel(place, normed, weight, queries, keyed, theirs):
    core = place[0]
    kept = keyed.shape[0] * HEAD
    rows = normed[...]
    for which in range(2):
        start = core if which == 0 else 1 - core
        for member in range(3):
            part = weight[member, :, pl.ds(pl.multiple_of(start * kept, 128), kept)]
            product = dot(rows, part).astype(BF16)
            if member == 0:
                product = product * jnp.asarray(1.0 / HEAD**0.5, BF16)
            turned = product.T
            for head in range(keyed.shape[0]):
                piece = turned[head * HEAD : (head + 1) * HEAD, :]
                if which == 1:
                    theirs[head, member * HEAD : (member + 1) * HEAD, :] = piece
                elif member == 0:
                    queries[head] = piece
                else:
                    keyed[head, (member - 1) * HEAD : member * HEAD, :] = piece


def project(place, normed, weight):
    count, length = weight.shape[2] // HEAD // 2, normed.shape[0]
    return pl.pallas_call(
        project_kernel,
        out_shape=tuple(jax.ShapeDtypeStruct((count, many * HEAD, length), BF16) for many in (1, 2, 3)),
        in_specs=[SMEM, VMEM, VMEM],
        out_specs=(VMEM,) * 3,
        compiler_params=PARAMS,
        name="project",
    )(place, normed, weight)


def absorb_kernel(first, *refs):
    if first:
        queries, block, out, top = refs
    else:
        queries, block, carried, carried_top, out, top = refs
    keys = block[:HEAD, :].T
    length = block.shape[1]
    values = jnp.concatenate([block[HEAD:, :], jnp.ones((16, length), BF16)], axis=0)
    width = min(512, queries.shape[1])
    depth = min(512, length)
    for at in range(0, queries.shape[1], width):
        part = queries[:, at : at + width]
        running = None if first else carried[:, at : at + width]
        best = None if first else carried_top[0:1, at : at + width]
        for below in range(0, length, depth):
            scores = dot(keys[below : below + depth], part)
            raised_top = jnp.max(scores, axis=0, keepdims=True)
            if best is not None:
                raised_top = jnp.maximum(best, raised_top)
            weights = jnp.exp(scores - raised_top).astype(BF16)
            added = dot(values[:, below : below + depth], weights)
            running = added if best is None else running * jnp.exp(best - raised_top) + added
            best = raised_top
        out[:, at : at + width] = running
        top[:, at : at + width] = jnp.broadcast_to(best, (8, width))


def absorb(queries, block, state):
    count = queries.shape[1]
    shapes = (jax.ShapeDtypeStruct((HEAD + 16, count), F32), jax.ShapeDtypeStruct((8, count), F32))
    first = state is None
    return pl.pallas_call(
        functools.partial(absorb_kernel, first),
        out_shape=shapes,
        in_specs=[VMEM] * (2 if first else 4),
        out_specs=(VMEM, VMEM),
        input_output_aliases={} if first else {2: 0, 3: 1},
        compiler_params=PARAMS,
        name="absorb",
    )(queries, block, *(() if first else state))


def finish_kernel(*refs):
    states, (folded, context, share) = refs[:-3], refs[-3:]
    for head, state in enumerate(states):
        context[head * HEAD : (head + 1) * HEAD, :] = (state[:HEAD, :] / state[HEAD : HEAD + 1, :]).astype(BF16)
    whole = context[...]
    share[...] = sum(dot(part, whole) for part in split3(folded[...]))


def finish(states, folded):
    count = states[0].shape[1]
    return pl.pallas_call(
        finish_kernel,
        out_shape=(
            jax.ShapeDtypeStruct((len(states) * HEAD, count), BF16),
            jax.ShapeDtypeStruct((folded.shape[0], count), F32),
        ),
        in_specs=[VMEM] * (len(states) + 1),
        out_specs=(VMEM, VMEM),
        compiler_params=PARAMS,
        name="finish",
    )(*states, folded)


def turned(values, step):
    return pltpu.roll(values, step % values.shape[1], 1)


def three_columns(values, cols):
    cells = values.shape[1]
    column = lax.rem(lax.broadcasted_iota(jnp.int32, (1, cells), 1), cols)
    wide = values.astype(F32)
    left = jnp.where(column == 0, 0.0, turned(wide, 1)).astype(BF16)
    right = jnp.where(column == cols - 1, 0.0, turned(wide, -1)).astype(BF16)
    return jnp.concatenate([left, values.astype(BF16), right], axis=0)


def three_rows(weights, columns, cols):
    cells = columns.shape[1] - 2 * cols
    return sum(dot(weights[a], columns[:, a * cols : a * cols + cells]) for a in range(3))


def network_kernel(
    cols, frame_rows, place, hidden, forward, backward, head, context, holo, sums, gradient, pre_one, pre_two
):
    core, half, row_at = place[0], place[1], place[2]
    own = context.shape[1]
    cells = hidden.shape[1]
    rim = (cells - own) // 2
    row_count = cells // cols
    above = rim // cols
    first_row = row_at - above

    def inside(start_row, rows):
        lane = lax.broadcasted_iota(jnp.int32, (1, rows * cols), 1)
        frame_lane = lane + (first_row + start_row) * cols
        return jnp.logical_and(frame_lane >= 0, frame_lane < frame_rows * cols)

    channels, outputs = forward.shape[2], head.shape[0]
    columns_zero = three_columns(hidden[:channels, :], cols)
    first = three_rows(forward[0], columns_zero, cols)
    rows_one = row_count - 2
    one = jnp.where(inside(1, rows_one), first * jax.nn.sigmoid(first), 0.0)
    columns_one = three_columns(one, cols)
    second = three_rows(forward[1], columns_one, cols)
    rows_two = row_count - 4
    sigmoid_two = jax.nn.sigmoid(second)
    two = (second * sigmoid_two).astype(BF16)
    holo[...] = dot(head[...], two[:, rim - 2 * cols : rim - 2 * cols + own])
    pieces = hidden[channels:, 2 * cols : cells - 2 * cols].astype(F32)
    cotangent = pieces[:outputs] + pieces[outputs : 2 * outputs] + pieces[2 * outputs : 3 * outputs]
    grad_two = lax.dot_general(
        head[...].astype(F32), cotangent, TN, precision=lax.Precision.HIGHEST, preferred_element_type=F32
    ).astype(BF16)
    slope = grad_two.astype(F32) * sigmoid_two * (1.0 + second * (1.0 - sigmoid_two))
    pre_grad_two = jnp.where(inside(2, rows_two), slope, 0.0)
    grad_one = three_rows(backward[1], three_columns(pre_grad_two, cols), cols).astype(BF16)
    rows_grad = row_count - 6
    middle = first[:, 2 * cols : 2 * cols + rows_grad * cols]
    sigmoid_one = jax.nn.sigmoid(middle)
    slope = grad_one.astype(F32) * sigmoid_one * (1.0 + middle * (1.0 - sigmoid_one))
    pre_grad_one = jnp.where(inside(3, rows_grad), slope, 0.0)
    grad_zero = three_rows(backward[0], three_columns(pre_grad_one, cols), cols).astype(BF16)
    pre_one[...] = pre_grad_one[:, rim - 3 * cols : rim - 3 * cols + own].astype(BF16)
    pre_two[...] = pre_grad_two[:, rim - 2 * cols : rim - 2 * cols + own].astype(BF16)

    share = sums.shape[0]
    taps = 9 * channels
    for layer, (pre, columns, offset) in enumerate(((pre_one, columns_zero, rim), (pre_two, columns_one, rim - cols))):

        @pl.when(core == layer)
        def _(pre=pre, columns=columns, offset=offset):
            stacked = jnp.concatenate(
                [columns[:, offset + (a - 1) * cols : offset + (a - 1) * cols + own] for a in range(3)], axis=0
            )
            rows = pre[pl.ds(pl.multiple_of(half * share, 16), share), :]
            sums[:, :taps] = lax.dot_general(rows, stacked, NT, preferred_element_type=F32)

    piece = own // 2
    total = None
    for side in range(2):
        where = lax.rem(core + side, 2)
        seen = context[:, pl.ds(pl.multiple_of(where * piece, 128), piece)]
        term = lax.dot_general(
            grad_zero[:, side * piece : (side + 1) * piece], seen, NT, preferred_element_type=F32
        )
        total = term if total is None else total + term
    gradient[...] = total


def network(place, hidden, forward, backward, head, context, cols, frame_rows, col_count):
    own = context.shape[1]
    channels = forward.shape[2]
    return pl.pallas_call(
        functools.partial(network_kernel, cols, frame_rows),
        out_shape=(
            jax.ShapeDtypeStruct((head.shape[0], own), F32),
            jax.ShapeDtypeStruct((channels // col_count, 9 * channels), F32),
            jax.ShapeDtypeStruct((channels, context.shape[0]), F32),
        ),
        in_specs=[SMEM] + [VMEM] * 5,
        out_specs=(VMEM,) * 3,
        scratch_shapes=[pltpu.VMEM((channels, own), BF16)] * 2,
        compiler_params=PARAMS,
        name="network",
    )(place, hidden, forward, backward, head, context)


def swapped(values, axis):
    size = lax.axis_size(axis)
    return lax.ppermute(values, axis, [(i, i ^ 1) for i in range(size)])


def passed(values, axis, step, wrap):
    size = lax.axis_size(axis)
    pairs = [(i, (i + step) % size) for i in range(size) if wrap or 0 <= i + step < size]
    return lax.ppermute(values, axis, pairs)


def in_order(core, mine, theirs, axis):
    return jnp.where(
        core == 0, jnp.concatenate([mine, theirs], axis=axis), jnp.concatenate([theirs, mine], axis=axis)
    )


def shards(
    tokens, ln_gain, qkv_weight, out_weight, readout_weight, conv_weight, head_weight, holo_cot
):
    frame_rows = tokens[0]
    cotangent = holo_cot[0]
    rows_dev, cols_dev = cotangent.shape[1:]
    tok_count, col_count, dp_count = (lax.axis_size(axis) for axis in ("tok", "col", "dp"))
    chips = tok_count // 2
    tok_at, half = lax.axis_index("tok"), lax.axis_index("col")
    core = lax.rem(tok_at, 2)
    chip_row = (tok_at - core) * rows_dev
    place = jnp.stack([core, half, chip_row]).astype(jnp.int32)
    layers, channels = conv_weight.shape[:2]
    cols = cols_dev * col_count
    length = frame_rows.shape[0]

    own_queries, own_keyed, theirs = project(place, normalize(frame_rows, ln_gain), qkv_weight)
    received = swapped(theirs, "tok")
    count = received.shape[0]
    kept = count * HEAD
    blocks = [jnp.concatenate([own_keyed[head], received[head, HEAD:]], axis=1) for head in range(count)]
    queries = [jnp.concatenate([own_queries[head], received[head, :HEAD]], axis=1) for head in range(count)]
    states = [None] * count

    def prepare(conv_weight, out_weight, readout_weight, frame_rows, other_cot):
        taps = conv_weight.reshape(layers, channels, 3, 3, channels)
        forward = jnp.transpose(taps.reshape(layers, channels, 3, 3 * channels), (0, 2, 1, 3))
        backward = jnp.transpose(taps[:, :, ::-1, ::-1, :], (0, 2, 4, 3, 1)).reshape(
            layers, 3, channels, 3 * channels
        )
        own_out = lax.dynamic_slice_in_dim(out_weight, core * kept, kept, 0)
        folded = lax.dot_general(readout_weight, own_out, (((0,), (1,)), ((), ())), preferred_element_type=F32)
        direct = lax.dot_general(readout_weight, frame_rows, (((0,), (1,)), ((), ())), preferred_element_type=F32)
        wide_cot = in_order(half, cotangent, other_cot, 2)
        exact_cot = jnp.concatenate(split3(wide_cot.reshape(wide_cot.shape[0], -1)), axis=0)
        exact_cot = jnp.pad(exact_cot, ((0, -exact_cot.shape[0] % 16), (0, 0)))
        return (forward, backward, folded, direct, exact_cot)

    for turn in range(chips):
        arriving = [passed(block, "tok", 2, True) for block in blocks] if turn < chips - 1 else blocks
        for head in range(count):
            states[head] = absorb(queries[head], blocks[head], states[head])
            if turn == 0 and head == 0:
                states[head], given = lax.optimization_barrier(
                    (states[head], (conv_weight, out_weight, readout_weight, frame_rows, swapped(cotangent, "col")))
                )
                prepared = prepare(*given)
            if turn == min(1, chips - 1) and head == count - 1:
                states[head], prepared = lax.optimization_barrier((states[head], prepared))
            arriving[head], states[head] = lax.optimization_barrier((arriving[head], states[head]))
            if head + 1 < count:
                gate = arriving[head] if turn < chips - 1 else states[head]
                blocks[head + 1], gate = lax.optimization_barrier((blocks[head + 1], gate))
                if turn < chips - 1:
                    arriving[head] = gate
                else:
                    states[head] = gate
        blocks = arriving
    forward, backward, folded, direct, exact_cot = prepared

    context, share = finish([state[0] for state in states], folded)
    partial = share[:, :length] + swapped(share[:, length:], "tok")
    own_map = (partial + swapped(partial, "col") + direct).astype(BF16)
    own_map = jnp.concatenate([own_map, exact_cot], axis=0)
    chip_map = in_order(core, own_map, swapped(own_map, "tok"), 1)
    rows_chip = 2 * rows_dev
    hidden = jnp.concatenate(
        [passed(chip_map, "tok", 2, False), chip_map, passed(chip_map, "tok", -2, False)], axis=1
    )

    holo, sums, gradient = network(
        place, hidden, forward, backward, head_weight, context, cols, tok_count * rows_dev, col_count
    )
    holo = holo.reshape(-1, rows_chip, cols)
    hologram = lax.dynamic_slice(
        holo, (0, core * rows_dev, half * cols_dev), (holo.shape[0], rows_dev, cols_dev)
    )

    taps_wide = sums.shape[1]
    lanes = 128 * ((taps_wide + 127) // 128)
    rows = sums.shape[0]
    pieces = gradient.shape[0] // rows
    folded_gradient = [gradient[at * rows : (at + 1) * rows] for at in range(pieces)]
    sent = jnp.concatenate([jnp.pad(sums, ((0, 0), (0, lanes - taps_wide))), *folded_gradient], axis=1)
    summed = sent
    for step in range(1, dp_count):
        summed = summed + passed(sent, "dp", step, True)
    total = summed
    for step in range(1, chips):
        total = total + passed(summed, "tok", 2 * step, True)
    own_grad = total[:, :taps_wide]
    col_grad = swapped(own_grad, "col")
    wide = gradient.shape[1]
    own_small = jnp.concatenate(
        [total[:, lanes + at * wide : lanes + (at + 1) * wide] for at in range(pieces)], axis=0
    )
    small = in_order(core, own_small, swapped(own_small, "tok"), 1)
    out_grad = lax.dot_general(
        small, readout_weight.astype(F32), (((0,), (1,)), ((), ())), precision=lax.Precision.HIGHEST
    )
    col_grad, out_grad = lax.optimization_barrier((col_grad, out_grad))
    layer_grad = in_order(half, own_grad, col_grad, 0)
    other_grad = swapped(layer_grad, "tok")
    conv_grad = in_order(core, layer_grad[None], other_grad[None], 0)
    return (hologram[None], conv_grad, out_grad)


def solution(mesh):
    in_specs = (
        P("dp", "tok", None),
        P(),
        P(None, None, "col"),
        P("col", None),
        P(),
        P(),
        P(),
        P("dp", None, "tok", "col"),
    )
    out_specs = (P("dp", None, "tok", "col"), P(), P("col", None))
    return jax.shard_map(shards, mesh=mesh, in_specs=in_specs, out_specs=out_specs, check_vma=False)
```

```python
import functools

import jax
import jax.numpy as jnp
from jax import lax
from jax.experimental import pallas as pl
from jax.experimental.pallas import tpu as pltpu
from jax.sharding import PartitionSpec as P

HEAD = 64
EPSILON = 1e-05
BF16 = jnp.bfloat16
F32 = jnp.float32
VMEM = pl.BlockSpec(memory_space=pltpu.VMEM)
SMEM = pl.BlockSpec(memory_space=pltpu.SMEM)
PARAMS = pltpu.CompilerParams(vmem_limit_bytes=48 * 2**20)
NT = (((1,), (1,)), ((), ()))
TN = (((0,), (0,)), ((), ()))


def dot(a, b):
    return jnp.dot(a, b, preferred_element_type=F32)


def split3(values):
    high = values.astype(BF16)
    rest = values - high.astype(F32)
    mid = rest.astype(BF16)
    low = (rest - mid.astype(F32)).astype(BF16)
    return high, mid, low


def normalize_kernel(tokens, gain, normed):
    values = tokens[...].astype(F32)
    center = values - jnp.mean(values, axis=-1, keepdims=True)
    spread = jnp.mean(center * center, axis=-1, keepdims=True)
    wide_gain = gain[...].astype(F32)[None, :]
    normed[...] = (center * lax.rsqrt(spread + EPSILON) * wide_gain).astype(BF16)


def normalize(tokens, gain):
    return pl.pallas_call(
        normalize_kernel,
        out_shape=jax.ShapeDtypeStruct(tokens.shape, BF16),
        in_specs=[VMEM, VMEM],
        out_specs=VMEM,
        compiler_params=PARAMS,
        name="normalize",
    )(tokens, gain)


def project_kernel(members, place, normed, weight, mine, theirs):
    core = place[0]
    kept = mine.shape[0] * HEAD
    rows = normed[...]
    for which, out in ((1 - core, theirs), (core, mine)):
        for at, member in enumerate(members):
            part = weight[member, :, pl.ds(pl.multiple_of(which * kept, 128), kept)]
            product = dot(rows, part).astype(BF16)
            if member == 0:
                product = product * jnp.asarray(1.0 / HEAD**0.5, BF16)
            turned = product.T
            for head in range(mine.shape[0]):
                out[head, at * HEAD : (at + 1) * HEAD, :] = turned[head * HEAD : (head + 1) * HEAD, :]


def project(members, place, normed, weight):
    count, length = weight.shape[2] // HEAD // 2, normed.shape[0]
    shape = jax.ShapeDtypeStruct((count, len(members) * HEAD, length), BF16)
    return pl.pallas_call(
        functools.partial(project_kernel, members),
        out_shape=(shape, shape),
        in_specs=[SMEM, VMEM, VMEM],
        out_specs=(VMEM,) * 2,
        compiler_params=PARAMS,
        name="project",
    )(place, normed, weight)


def absorb_kernel(first, *refs):
    if first:
        queries, block, out, top = refs
    else:
        queries, block, carried, carried_top, out, top = refs
    keys = block[:HEAD, :].T
    length = block.shape[1]
    values = jnp.concatenate([block[HEAD:, :], jnp.ones((16, length), BF16)], axis=0)
    width = min(512, queries.shape[1])
    depth = min(512, length)
    for at in range(0, queries.shape[1], width):
        part = queries[:, at : at + width]
        running = None if first else carried[:, at : at + width]
        best = None if first else carried_top[0:1, at : at + width]
        for below in range(0, length, depth):
            scores = dot(keys[below : below + depth], part)
            raised_top = jnp.max(scores, axis=0, keepdims=True)
            if best is not None:
                raised_top = jnp.maximum(best, raised_top)
            weights = jnp.exp(scores - raised_top).astype(BF16)
            added = dot(values[:, below : below + depth], weights)
            running = added if best is None else running * jnp.exp(best - raised_top) + added
            best = raised_top
        out[:, at : at + width] = running
        top[:, at : at + width] = jnp.broadcast_to(best, (8, width))


def absorb(queries, block, state):
    count = queries.shape[1]
    shapes = (jax.ShapeDtypeStruct((HEAD + 16, count), F32), jax.ShapeDtypeStruct((8, count), F32))
    first = state is None
    return pl.pallas_call(
        functools.partial(absorb_kernel, first),
        out_shape=shapes,
        in_specs=[VMEM] * (2 if first else 4),
        out_specs=(VMEM, VMEM),
        input_output_aliases={} if first else {2: 0, 3: 1},
        compiler_params=PARAMS,
        name="absorb",
    )(queries, block, *(() if first else state))


def finish_kernel(*refs):
    states, (folded, context, share) = refs[:-3], refs[-3:]
    for head, state in enumerate(states):
        context[head * HEAD : (head + 1) * HEAD, :] = (state[:HEAD, :] / state[HEAD : HEAD + 1, :]).astype(BF16)
    whole = context[...]
    share[...] = sum(dot(part, whole) for part in split3(folded[...]))


def finish(states, folded):
    count = states[0].shape[1]
    return pl.pallas_call(
        finish_kernel,
        out_shape=(
            jax.ShapeDtypeStruct((len(states) * HEAD, count), BF16),
            jax.ShapeDtypeStruct((folded.shape[0], count), F32),
        ),
        in_specs=[VMEM] * (len(states) + 1),
        out_specs=(VMEM, VMEM),
        compiler_params=PARAMS,
        name="finish",
    )(*states, folded)


def turned(values, step):
    return pltpu.roll(values, step % values.shape[1], 1)


def three_columns(values, cols):
    cells = values.shape[1]
    column = lax.rem(lax.broadcasted_iota(jnp.int32, (1, cells), 1), cols)
    wide = values.astype(F32)
    left = jnp.where(column == 0, 0.0, turned(wide, 1)).astype(BF16)
    right = jnp.where(column == cols - 1, 0.0, turned(wide, -1)).astype(BF16)
    return jnp.concatenate([left, values.astype(BF16), right], axis=0)


def three_rows(weights, columns, cols):
    cells = columns.shape[1] - 2 * cols
    return sum(dot(weights[a], columns[:, a * cols : a * cols + cells]) for a in range(3))


def network_kernel(
    cols, frame_rows, place, own_map, other_map, rims, other_rims, forward, backward, head, context, holo, sums,
    gradient, hidden, pre_one, pre_two,
):
    core, half, row_at = place[0], place[1], place[2]
    own = context.shape[1]
    cells = hidden.shape[1]
    rim = (cells - own) // 2
    row_count = cells // cols
    above = rim // cols
    first_row = row_at - above
    piece = own // 2
    for order, (mine, theirs, at) in enumerate(
        ((rims, other_rims, 0), (own_map, other_map, 0), (rims, other_rims, piece))
    ):
        for which, source in ((core, mine), (1 - core, theirs)):
            start = pl.multiple_of(order * own + which * piece, 128)
            hidden[:, pl.ds(start, piece)] = source[:, at : at + piece]

    def inside(start_row, rows):
        lane = lax.broadcasted_iota(jnp.int32, (1, rows * cols), 1)
        frame_lane = lane + (first_row + start_row) * cols
        return jnp.logical_and(frame_lane >= 0, frame_lane < frame_rows * cols)

    channels, outputs = forward.shape[2], head.shape[0]
    columns_zero = three_columns(hidden[:channels, :], cols)
    first = three_rows(forward[0], columns_zero, cols)
    rows_one = row_count - 2
    one = jnp.where(inside(1, rows_one), first * jax.nn.sigmoid(first), 0.0)
    columns_one = three_columns(one, cols)
    second = three_rows(forward[1], columns_one, cols)
    rows_two = row_count - 4
    sigmoid_two = jax.nn.sigmoid(second)
    two = (second * sigmoid_two).astype(BF16)
    holo[...] = dot(head[...], two[:, rim - 2 * cols : rim - 2 * cols + own])
    pieces = hidden[channels:, 2 * cols : cells - 2 * cols].astype(F32)
    cotangent = pieces[:outputs] + pieces[outputs : 2 * outputs] + pieces[2 * outputs : 3 * outputs]
    grad_two = lax.dot_general(
        head[...].astype(F32), cotangent, TN, precision=lax.Precision.HIGHEST, preferred_element_type=F32
    ).astype(BF16)
    slope = grad_two.astype(F32) * sigmoid_two * (1.0 + second * (1.0 - sigmoid_two))
    pre_grad_two = jnp.where(inside(2, rows_two), slope, 0.0)
    grad_one = three_rows(backward[1], three_columns(pre_grad_two, cols), cols).astype(BF16)
    rows_grad = row_count - 6
    middle = first[:, 2 * cols : 2 * cols + rows_grad * cols]
    sigmoid_one = jax.nn.sigmoid(middle)
    slope = grad_one.astype(F32) * sigmoid_one * (1.0 + middle * (1.0 - sigmoid_one))
    pre_grad_one = jnp.where(inside(3, rows_grad), slope, 0.0)
    grad_zero = three_rows(backward[0], three_columns(pre_grad_one, cols), cols).astype(BF16)
    pre_one[...] = pre_grad_one[:, rim - 3 * cols : rim - 3 * cols + own].astype(BF16)
    pre_two[...] = pre_grad_two[:, rim - 2 * cols : rim - 2 * cols + own].astype(BF16)

    share = sums.shape[0]
    taps = 9 * channels
    for layer, (pre, columns, offset) in enumerate(((pre_one, columns_zero, rim), (pre_two, columns_one, rim - cols))):

        @pl.when(core == layer)
        def _(pre=pre, columns=columns, offset=offset):
            stacked = jnp.concatenate(
                [columns[:, offset + (a - 1) * cols : offset + (a - 1) * cols + own] for a in range(3)], axis=0
            )
            rows = pre[pl.ds(pl.multiple_of(half * share, 16), share), :]
            sums[:, :taps] = lax.dot_general(rows, stacked, NT, preferred_element_type=F32)

    total = None
    for side in range(2):
        where = lax.rem(core + side, 2)
        seen = context[:, pl.ds(pl.multiple_of(where * piece, 128), piece)]
        term = lax.dot_general(
            grad_zero[:, side * piece : (side + 1) * piece], seen, NT, preferred_element_type=F32
        )
        total = term if total is None else total + term
    gradient[...] = total


def network(place, maps, forward, backward, head, context, cols, frame_rows, col_count):
    own = context.shape[1]
    channels = forward.shape[2]
    return pl.pallas_call(
        functools.partial(network_kernel, cols, frame_rows),
        out_shape=(
            jax.ShapeDtypeStruct((head.shape[0], own), F32),
            jax.ShapeDtypeStruct((channels // col_count, 9 * channels), F32),
            jax.ShapeDtypeStruct((channels, context.shape[0]), F32),
        ),
        in_specs=[SMEM] + [VMEM] * 8,
        out_specs=(VMEM,) * 3,
        scratch_shapes=[pltpu.VMEM((maps[0].shape[0], 3 * own), BF16)] + [pltpu.VMEM((channels, own), BF16)] * 2,
        compiler_params=PARAMS,
        name="network",
    )(place, *maps, forward, backward, head, context)


def swapped(values, axis):
    size = lax.axis_size(axis)
    return lax.ppermute(values, axis, [(i, i ^ 1) for i in range(size)])


def passed(values, axis, step, wrap):
    size = lax.axis_size(axis)
    pairs = [(i, (i + step) % size) for i in range(size) if wrap or 0 <= i + step < size]
    return lax.ppermute(values, axis, pairs)


def everyone(values, axis, stride, count):
    sent = values.astype(BF16)
    total = sent.astype(F32)
    for step in range(1, count):
        total = total + passed(sent, axis, stride * step, True).astype(F32)
    return total


def in_order(core, mine, theirs, axis):
    return jnp.where(
        core == 0, jnp.concatenate([mine, theirs], axis=axis), jnp.concatenate([theirs, mine], axis=axis)
    )


def shards(
    tokens, ln_gain, qkv_weight, out_weight, readout_weight, conv_weight, head_weight, holo_cot
):
    frame_rows = tokens[0]
    cotangent = holo_cot[0]
    rows_dev, cols_dev = cotangent.shape[1:]
    tok_count, col_count, dp_count = (lax.axis_size(axis) for axis in ("tok", "col", "dp"))
    chips = tok_count // 2
    tok_at, half = lax.axis_index("tok"), lax.axis_index("col")
    core = lax.rem(tok_at, 2)
    chip_row = (tok_at - core) * rows_dev
    place = jnp.stack([core, half, chip_row]).astype(jnp.int32)
    layers, channels = conv_weight.shape[:2]
    cols = cols_dev * col_count
    length = frame_rows.shape[0]

    normed = normalize(frame_rows, ln_gain)
    own_keyed, their_keyed = project((1, 2), place, normed, qkv_weight)
    own_keyed, their_keyed, normed = lax.optimization_barrier((own_keyed, their_keyed, normed))
    got_keyed = swapped(their_keyed, "tok")
    own_queries, their_queries = project((0,), place, normed, qkv_weight)
    got_queries = swapped(their_queries, "tok")
    count = got_keyed.shape[0]
    kept = count * HEAD
    blocks = [jnp.concatenate([own_keyed[head], got_keyed[head]], axis=1) for head in range(count)]
    queries = [jnp.concatenate([own_queries[head], got_queries[head]], axis=1) for head in range(count)]
    states = [None] * count

    def prepare(conv_weight, out_weight, readout_weight, frame_rows, cotangent):
        taps = conv_weight.reshape(layers, channels, 3, 3, channels)
        forward = jnp.transpose(taps.reshape(layers, channels, 3, 3 * channels), (0, 2, 1, 3))
        backward = jnp.transpose(taps[:, :, ::-1, ::-1, :], (0, 2, 4, 3, 1)).reshape(
            layers, 3, channels, 3 * channels
        )
        own_out = lax.dynamic_slice_in_dim(out_weight, core * kept, kept, 0)
        folded = lax.dot_general(readout_weight, own_out, (((0,), (1,)), ((), ())), preferred_element_type=F32)
        direct = lax.dot_general(readout_weight, frame_rows, (((0,), (1,)), ((), ())), preferred_element_type=F32)
        wide_cot = in_order(half, cotangent, swapped(cotangent, "col"), 2)
        exact_cot = jnp.concatenate(split3(wide_cot.reshape(wide_cot.shape[0], -1)), axis=0)
        exact_cot = jnp.pad(exact_cot, ((0, -exact_cot.shape[0] % 16), (0, 0)))
        return (forward, backward, folded, direct, exact_cot)

    for turn in range(chips):
        arriving = [passed(block, "tok", 2, True) for block in blocks] if turn < chips - 1 else blocks
        for head in range(count):
            states[head] = absorb(queries[head], blocks[head], states[head])
            if turn == 0 and head == 0:
                states[head], given = lax.optimization_barrier(
                    (states[head], (conv_weight, out_weight, readout_weight, frame_rows, cotangent))
                )
                prepared = prepare(*given)
            if turn == min(1, chips - 1) and head == count - 1:
                states[head], prepared = lax.optimization_barrier((states[head], prepared))
            arriving[head], states[head] = lax.optimization_barrier((arriving[head], states[head]))
            if head + 1 < count:
                gate = arriving[head] if turn < chips - 1 else states[head]
                blocks[head + 1], gate = lax.optimization_barrier((blocks[head + 1], gate))
                if turn < chips - 1:
                    arriving[head] = gate
                else:
                    states[head] = gate
        blocks = arriving
    forward, backward, folded, direct, exact_cot = prepared

    context, share = finish([state[0] for state in states], folded)
    partial = share[:, :length] + swapped(share[:, length:], "tok")
    own_map = (partial + swapped(partial, "col") + direct).astype(BF16)
    own_map = jnp.concatenate([own_map, exact_cot], axis=0)
    rims = jnp.concatenate([passed(own_map, "tok", 2, False), passed(own_map, "tok", -2, False)], axis=1)
    rows_chip = 2 * rows_dev
    maps = (own_map, swapped(own_map, "tok"), rims, swapped(rims, "tok"))
    holo, sums, gradient = network(
        place, maps, forward, backward, head_weight, context, cols, tok_count * rows_dev, col_count
    )
    holo = holo.reshape(-1, rows_chip, cols)
    hologram = lax.dynamic_slice(
        holo, (0, core * rows_dev, half * cols_dev), (holo.shape[0], rows_dev, cols_dev)
    )

    taps_wide = sums.shape[1]
    lanes = 128 * ((taps_wide + 127) // 128)
    rows = sums.shape[0]
    pieces = gradient.shape[0] // rows
    folded_gradient = [gradient[at * rows : (at + 1) * rows] for at in range(pieces)]
    sent = jnp.concatenate([jnp.pad(sums, ((0, 0), (0, lanes - taps_wide))), *folded_gradient], axis=1)
    summed = everyone(sent, "dp", 1, dp_count)
    total = everyone(summed, "tok", 2, chips)
    own_grad = total[:, :taps_wide]
    col_grad = swapped(own_grad, "col")
    wide = gradient.shape[1]
    own_small = jnp.concatenate(
        [total[:, lanes + at * wide : lanes + (at + 1) * wide] for at in range(pieces)], axis=0
    )
    small = in_order(core, own_small, swapped(own_small, "tok"), 1)
    out_grad = lax.dot_general(
        small, readout_weight.astype(F32), (((0,), (1,)), ((), ())), precision=lax.Precision.HIGHEST
    )
    core_grad = swapped(own_grad, "tok")
    col_grad, out_grad, core_grad = lax.optimization_barrier((col_grad, out_grad, core_grad))
    far_grad = swapped(col_grad, "tok")
    layer_grad = in_order(half, own_grad, col_grad, 0)
    other_grad = in_order(half, core_grad, far_grad, 0)
    conv_grad = in_order(core, layer_grad[None], other_grad[None], 0)
    return (hologram[None], conv_grad, out_grad)


def solution(mesh):
    in_specs = (
        P("dp", "tok", None),
        P(),
        P(None, None, "col"),
        P("col", None),
        P(),
        P(),
        P(),
        P("dp", None, "tok", "col"),
    )
    out_specs = (P("dp", None, "tok", "col"), P(), P("col", None))
    return jax.shard_map(shards, mesh=mesh, in_specs=in_specs, out_specs=out_specs, check_vma=False)
```

```python
import functools

import jax
import jax.numpy as jnp
from jax import lax
from jax.experimental import pallas as pl
from jax.experimental.pallas import tpu as pltpu
from jax.sharding import PartitionSpec as P

HEAD = 64
EPSILON = 1e-05
BF16 = jnp.bfloat16
F32 = jnp.float32
VMEM = pl.BlockSpec(memory_space=pltpu.VMEM)
SMEM = pl.BlockSpec(memory_space=pltpu.SMEM)
PARAMS = pltpu.CompilerParams(vmem_limit_bytes=48 * 2**20)
NT = (((1,), (1,)), ((), ()))
TN = (((0,), (0,)), ((), ()))


def dot(a, b):
    return jnp.dot(a, b, preferred_element_type=F32)


def split3(values):
    high = values.astype(BF16)
    rest = values - high.astype(F32)
    mid = rest.astype(BF16)
    low = (rest - mid.astype(F32)).astype(BF16)
    return high, mid, low


def normalize_kernel(tokens, gain, normed):
    values = tokens[...].astype(F32)
    center = values - jnp.mean(values, axis=-1, keepdims=True)
    spread = jnp.mean(center * center, axis=-1, keepdims=True)
    wide_gain = gain[...].astype(F32)[None, :]
    normed[...] = (center * lax.rsqrt(spread + EPSILON) * wide_gain).astype(BF16)


def normalize(tokens, gain):
    return pl.pallas_call(
        normalize_kernel,
        out_shape=jax.ShapeDtypeStruct(tokens.shape, BF16),
        in_specs=[VMEM, VMEM],
        out_specs=VMEM,
        compiler_params=PARAMS,
        name="normalize",
    )(tokens, gain)


def project_kernel(members, place, normed, weight, mine, theirs, turned):
    core = place[0]
    kept = mine.shape[0] * HEAD
    rows = normed[...]
    for at, member in enumerate(members):
        product = dot(rows, weight[member]).astype(BF16)
        if member == 0:
            product = product * jnp.asarray(1.0 / HEAD**0.5, BF16)
        turned[at] = product.T
        for which, out in ((1 - core, theirs), (core, mine)):
            for head in range(mine.shape[0]):
                start = pl.multiple_of(which * kept + head * HEAD, HEAD)
                out[head, at * HEAD : (at + 1) * HEAD, :] = turned[at, pl.ds(start, HEAD), :]


def project(members, place, normed, weight):
    count, length = weight.shape[2] // HEAD // 2, normed.shape[0]
    shape = jax.ShapeDtypeStruct((count, len(members) * HEAD, length), BF16)
    return pl.pallas_call(
        functools.partial(project_kernel, members),
        out_shape=(shape, shape),
        in_specs=[SMEM, VMEM, VMEM],
        out_specs=(VMEM,) * 2,
        scratch_shapes=[pltpu.VMEM((len(members), weight.shape[2], length), BF16)],
        compiler_params=PARAMS,
        name="project",
    )(place, normed, weight)


def absorb_kernel(first, *refs):
    if first:
        queries, block, out, top = refs
    else:
        queries, block, carried, carried_top, out, top = refs
    keys = block[:HEAD, :].T
    length = block.shape[1]
    values = jnp.concatenate([block[HEAD:, :], jnp.ones((16, length), BF16)], axis=0)
    width = min(512, queries.shape[1])
    depth = min(512, length)
    for at in range(0, queries.shape[1], width):
        part = queries[:, at : at + width]
        running = None if first else carried[:, at : at + width]
        best = None if first else carried_top[0:1, at : at + width]
        for below in range(0, length, depth):
            scores = dot(keys[below : below + depth], part)
            raised_top = jnp.max(scores, axis=0, keepdims=True)
            if best is not None:
                raised_top = jnp.maximum(best, raised_top)
            weights = jnp.exp(scores - raised_top).astype(BF16)
            added = dot(values[:, below : below + depth], weights)
            running = added if best is None else running * jnp.exp(best - raised_top) + added
            best = raised_top
        out[:, at : at + width] = running
        top[:, at : at + width] = jnp.broadcast_to(best, (8, width))


def absorb(queries, block, state):
    count = queries.shape[1]
    shapes = (jax.ShapeDtypeStruct((HEAD + 16, count), F32), jax.ShapeDtypeStruct((8, count), F32))
    first = state is None
    return pl.pallas_call(
        functools.partial(absorb_kernel, first),
        out_shape=shapes,
        in_specs=[VMEM] * (2 if first else 4),
        out_specs=(VMEM, VMEM),
        input_output_aliases={} if first else {2: 0, 3: 1},
        compiler_params=PARAMS,
        name="absorb",
    )(queries, block, *(() if first else state))


def finish_kernel(*refs):
    states, (folded, context, share) = refs[:-3], refs[-3:]
    for head, state in enumerate(states):
        context[head * HEAD : (head + 1) * HEAD, :] = (state[:HEAD, :] / state[HEAD : HEAD + 1, :]).astype(BF16)
    whole = context[...]
    share[...] = sum(dot(part, whole) for part in split3(folded[...]))


def finish(states, folded):
    count = states[0].shape[1]
    return pl.pallas_call(
        finish_kernel,
        out_shape=(
            jax.ShapeDtypeStruct((len(states) * HEAD, count), BF16),
            jax.ShapeDtypeStruct((folded.shape[0], count), F32),
        ),
        in_specs=[VMEM] * (len(states) + 1),
        out_specs=(VMEM, VMEM),
        compiler_params=PARAMS,
        name="finish",
    )(*states, folded)


def turned(values, step):
    return pltpu.roll(values, step % values.shape[1], 1)


def three_columns(values, cols):
    cells = values.shape[1]
    column = lax.rem(lax.broadcasted_iota(jnp.int32, (1, cells), 1), cols)
    wide = values.astype(F32)
    left = jnp.where(column == 0, 0.0, turned(wide, 1)).astype(BF16)
    right = jnp.where(column == cols - 1, 0.0, turned(wide, -1)).astype(BF16)
    return jnp.concatenate([left, values.astype(BF16), right], axis=0)


def three_rows(weights, columns, cols):
    cells = columns.shape[1] - 2 * cols
    return sum(dot(weights[a], columns[:, a * cols : a * cols + cells]) for a in range(3))


def network_kernel(
    cols, frame_rows, place, mine, theirs, forward, backward, head, context, holo, sums,
    gradient, hidden, pre_one, pre_two,
):
    core, half, row_at = place[0], place[1], place[2]
    own = context.shape[1]
    cells = hidden.shape[1]
    rim = (cells - own) // 2
    row_count = cells // cols
    above = rim // cols
    first_row = row_at - above
    piece = own // 2
    for order in range(3):
        for which, source in ((core, mine), (1 - core, theirs)):
            start = pl.multiple_of(order * own + which * piece, 128)
            hidden[:, pl.ds(start, piece)] = source[:, order * piece : (order + 1) * piece]

    def inside(start_row, rows):
        lane = lax.broadcasted_iota(jnp.int32, (1, rows * cols), 1)
        frame_lane = lane + (first_row + start_row) * cols
        return jnp.logical_and(frame_lane >= 0, frame_lane < frame_rows * cols)

    channels, outputs = forward.shape[2], head.shape[0]
    columns_zero = three_columns(hidden[:channels, :], cols)
    first = three_rows(forward[0], columns_zero, cols)
    rows_one = row_count - 2
    one = jnp.where(inside(1, rows_one), first * jax.nn.sigmoid(first), 0.0)
    columns_one = three_columns(one, cols)
    second = three_rows(forward[1], columns_one, cols)
    rows_two = row_count - 4
    sigmoid_two = jax.nn.sigmoid(second)
    two = (second * sigmoid_two).astype(BF16)
    holo[...] = dot(head[...], two[:, rim - 2 * cols : rim - 2 * cols + own])
    pieces = hidden[channels:, 2 * cols : cells - 2 * cols].astype(F32)
    cotangent = pieces[:outputs] + pieces[outputs : 2 * outputs] + pieces[2 * outputs : 3 * outputs]
    grad_two = lax.dot_general(
        head[...].astype(F32), cotangent, TN, precision=lax.Precision.HIGHEST, preferred_element_type=F32
    ).astype(BF16)
    slope = grad_two.astype(F32) * sigmoid_two * (1.0 + second * (1.0 - sigmoid_two))
    pre_grad_two = jnp.where(inside(2, rows_two), slope, 0.0)
    grad_one = three_rows(backward[1], three_columns(pre_grad_two, cols), cols).astype(BF16)
    rows_grad = row_count - 6
    middle = first[:, 2 * cols : 2 * cols + rows_grad * cols]
    sigmoid_one = jax.nn.sigmoid(middle)
    slope = grad_one.astype(F32) * sigmoid_one * (1.0 + middle * (1.0 - sigmoid_one))
    pre_grad_one = jnp.where(inside(3, rows_grad), slope, 0.0)
    grad_zero = three_rows(backward[0], three_columns(pre_grad_one, cols), cols).astype(BF16)
    pre_one[...] = pre_grad_one[:, rim - 3 * cols : rim - 3 * cols + own].astype(BF16)
    pre_two[...] = pre_grad_two[:, rim - 2 * cols : rim - 2 * cols + own].astype(BF16)

    share = sums.shape[0]
    taps = 9 * channels
    for layer, (pre, columns, offset) in enumerate(((pre_one, columns_zero, rim), (pre_two, columns_one, rim - cols))):

        @pl.when(core == layer)
        def _(pre=pre, columns=columns, offset=offset):
            stacked = jnp.concatenate(
                [columns[:, offset + (a - 1) * cols : offset + (a - 1) * cols + own] for a in range(3)], axis=0
            )
            rows = pre[pl.ds(pl.multiple_of(half * share, 16), share), :]
            sums[:, :taps] = lax.dot_general(rows, stacked, NT, preferred_element_type=F32)

    total = None
    for side in range(2):
        where = lax.rem(core + side, 2)
        seen = context[:, pl.ds(pl.multiple_of(where * piece, 128), piece)]
        term = lax.dot_general(
            grad_zero[:, side * piece : (side + 1) * piece], seen, NT, preferred_element_type=F32
        )
        total = term if total is None else total + term
    gradient[...] = total


def network(place, maps, forward, backward, head, context, cols, frame_rows, col_count):
    own = context.shape[1]
    channels = forward.shape[2]
    return pl.pallas_call(
        functools.partial(network_kernel, cols, frame_rows),
        out_shape=(
            jax.ShapeDtypeStruct((head.shape[0], own), F32),
            jax.ShapeDtypeStruct((channels // col_count, 9 * channels), F32),
            jax.ShapeDtypeStruct((channels, context.shape[0]), F32),
        ),
        in_specs=[SMEM] + [VMEM] * 6,
        out_specs=(VMEM,) * 3,
        scratch_shapes=[pltpu.VMEM((maps[0].shape[0], 3 * own), BF16)] + [pltpu.VMEM((channels, own), BF16)] * 2,
        compiler_params=PARAMS,
        name="network",
    )(place, *maps, forward, backward, head, context)


def swapped(values, axis):
    size = lax.axis_size(axis)
    return lax.ppermute(values, axis, [(i, i ^ 1) for i in range(size)])


def passed(values, step, across):
    size, cols = lax.axis_size("tok"), lax.axis_size("col")
    pairs = [
        (i * cols + j, (i + step) * cols + (j ^ 1 if across else j))
        for i in range(size)
        for j in range(cols)
        if 0 <= i + step < size
    ]
    return lax.ppermute(values, ("tok", "col"), pairs)


def round_ring(values):
    size = lax.axis_size("tok")
    chips = size // 2
    order = [at for at in range(chips) if at == 0 or at % 2 == 1] + [
        at for at in reversed(range(chips)) if at and at % 2 == 0
    ]
    following = {order[at]: order[(at + 1) % chips] for at in range(chips)}
    return lax.ppermute(values, "tok", [(i, 2 * following[i // 2] + i % 2) for i in range(size)])


def tree_sum(terms):
    while len(terms) > 1:
        terms = [sum(terms[at : at + 2][1:], terms[at]) for at in range(0, len(terms), 2)]
    return terms[0]


def other_place(at, step, count):
    return at ^ step if count & (count - 1) == 0 else (at + step) % count


def sum_chips(values):
    size = lax.axis_size("tok")
    chips = size // 2
    terms = [values.astype(F32)]
    for step in range(1, chips):
        pairs = [(i, 2 * other_place(i // 2, step, chips) + i % 2) for i in range(size)]
        terms.append(lax.ppermute(values, "tok", pairs).astype(F32))
    return tree_sum(terms)


def sum_frames(values, across):
    size, cols = lax.axis_size("dp"), lax.axis_size("col")
    terms = []
    for step in range(size):
        pairs = [
            (i * cols + j, other_place(i, step, size) * cols + (j ^ 1 if across else j))
            for i in range(size)
            for j in range(cols)
        ]
        moved = lax.ppermute(values, ("dp", "col"), pairs) if step or across else values
        terms.append(moved.astype(F32))
    return tree_sum(terms)


def in_order(core, mine, theirs, axis):
    return jnp.where(
        core == 0, jnp.concatenate([mine, theirs], axis=axis), jnp.concatenate([theirs, mine], axis=axis)
    )


def shards(
    tokens, ln_gain, qkv_weight, out_weight, readout_weight, conv_weight, head_weight, holo_cot
):
    frame_rows = tokens[0]
    cotangent = holo_cot[0]
    rows_dev, cols_dev = cotangent.shape[1:]
    tok_count, col_count, dp_count = (lax.axis_size(axis) for axis in ("tok", "col", "dp"))
    chips = tok_count // 2
    tok_at, half = lax.axis_index("tok"), lax.axis_index("col")
    core = lax.rem(tok_at, 2)
    chip_row = (tok_at - core) * rows_dev
    place = jnp.stack([core, half, chip_row]).astype(jnp.int32)
    layers, channels = conv_weight.shape[:2]
    cols = cols_dev * col_count
    length = frame_rows.shape[0]

    normed = normalize(frame_rows, ln_gain)
    own_keyed, their_keyed = project((1, 2), place, normed, qkv_weight)
    own_keyed, their_keyed, normed = lax.optimization_barrier((own_keyed, their_keyed, normed))
    got_keyed = swapped(their_keyed, "tok")
    own_queries, their_queries = project((0,), place, normed, qkv_weight)
    got_queries = swapped(their_queries, "tok")
    count = got_keyed.shape[0]
    kept = count * HEAD
    blocks = [jnp.concatenate([own_keyed[head], got_keyed[head]], axis=1) for head in range(count)]
    queries = [jnp.concatenate([own_queries[head], got_queries[head]], axis=1) for head in range(count)]
    states = [None] * count

    def prepare(conv_weight, out_weight, readout_weight, frame_rows, cotangent):
        taps = conv_weight.reshape(layers, channels, 3, 3, channels)
        forward = jnp.transpose(taps.reshape(layers, channels, 3, 3 * channels), (0, 2, 1, 3))
        backward = jnp.transpose(taps[:, :, ::-1, ::-1, :], (0, 2, 4, 3, 1)).reshape(
            layers, 3, channels, 3 * channels
        )
        own_out = lax.dynamic_slice_in_dim(out_weight, core * kept, kept, 0)
        folded = lax.dot_general(readout_weight, own_out, (((0,), (1,)), ((), ())), preferred_element_type=F32)
        direct = lax.dot_general(readout_weight, frame_rows, (((0,), (1,)), ((), ())), preferred_element_type=F32)
        wide_cot = in_order(half, cotangent, swapped(cotangent, "col"), 2)
        exact_cot = jnp.concatenate(split3(wide_cot.reshape(wide_cot.shape[0], -1)), axis=0)
        exact_cot = jnp.pad(exact_cot, ((0, -exact_cot.shape[0] % 16), (0, 0)))
        return (forward, backward, folded, direct, exact_cot)

    for turn in range(chips):
        arriving = [round_ring(block) for block in blocks] if turn < chips - 1 else blocks
        for head in range(count):
            states[head] = absorb(queries[head], blocks[head], states[head])
            if turn == 0 and head == 0:
                states[head], given = lax.optimization_barrier(
                    (states[head], (conv_weight, out_weight, readout_weight, frame_rows, cotangent))
                )
                prepared = prepare(*given)
            if turn == min(1, chips - 1) and head == count - 1:
                states[head], prepared = lax.optimization_barrier((states[head], prepared))
            arriving[head], states[head] = lax.optimization_barrier((arriving[head], states[head]))
            if head + 1 < count:
                gate = arriving[head] if turn < chips - 1 else states[head]
                blocks[head + 1], gate = lax.optimization_barrier((blocks[head + 1], gate))
                if turn < chips - 1:
                    arriving[head] = gate
                else:
                    states[head] = gate
        blocks = arriving
    forward, backward, folded, direct, exact_cot = prepared

    context, share = finish([state[0] for state in states], folded)
    partial = share[:, :length] + swapped(share[:, length:], "tok")
    partial = (partial + jnp.where(half == 0, direct, 0.0)).astype(BF16)
    with_cot = jnp.concatenate([partial, exact_cot], axis=0)
    near = (passed(with_cot, 2, False), with_cot, passed(with_cot, -2, False))
    far = (passed(partial, 2, True), swapped(partial, "col"), passed(partial, -2, True))
    maps = jnp.concatenate(
        [
            jnp.concatenate(
                [(ours[:channels].astype(F32) + others.astype(F32)).astype(BF16), ours[channels:]], axis=0
            )
            for ours, others in zip(near, far)
        ],
        axis=1,
    )
    rows_chip = 2 * rows_dev
    maps = (maps, swapped(maps, "tok"))
    holo, sums, gradient = network(
        place, maps, forward, backward, head_weight, context, cols, tok_count * rows_dev, col_count
    )
    holo = holo.reshape(-1, rows_chip, cols)
    hologram = lax.dynamic_slice(
        holo, (0, core * rows_dev, half * cols_dev), (holo.shape[0], rows_dev, cols_dev)
    )

    taps_wide = sums.shape[1]
    lanes = 128 * ((taps_wide + 127) // 128)
    rows = sums.shape[0]
    pieces = gradient.shape[0] // rows
    folded_gradient = [gradient[at * rows : (at + 1) * rows] for at in range(pieces)]
    sent = jnp.concatenate([jnp.pad(sums, ((0, 0), (0, lanes - taps_wide))), *folded_gradient], axis=1)
    summed = sum_chips(sent.astype(BF16)).astype(BF16)
    summed_taps = summed[:, :taps_wide]
    own_terms, far_terms = sum_frames(summed, False), sum_frames(summed_taps, True)
    wide = gradient.shape[1]
    own_small = jnp.concatenate(
        [own_terms[:, lanes + at * wide : lanes + (at + 1) * wide] for at in range(pieces)], axis=0
    )
    small = in_order(core, own_small, swapped(own_small, "tok"), 1)
    out_grad = lax.dot_general(
        small, readout_weight.astype(F32), (((0,), (1,)), ((), ())), precision=lax.Precision.HIGHEST
    )
    layer_grad = in_order(half, own_terms[:, :taps_wide], far_terms, 0)
    conv_grad = in_order(core, layer_grad[None], swapped(layer_grad, "tok")[None], 0)
    return (hologram[None], conv_grad, out_grad)


def solution(mesh):
    in_specs = (
        P("dp", "tok", None),
        P(),
        P(None, None, "col"),
        P("col", None),
        P(),
        P(),
        P(),
        P("dp", None, "tok", "col"),
    )
    out_specs = (P("dp", None, "tok", "col"), P(), P("col", None))
    return jax.shard_map(shards, mesh=mesh, in_specs=in_specs, out_specs=out_specs, check_vma=False)
```

```python
import functools

import jax
import jax.numpy as jnp
from jax import lax
from jax.experimental import pallas as pl
from jax.experimental.pallas import tpu as pltpu
from jax.sharding import PartitionSpec as P

HEAD = 64
EPSILON = 1e-05
BF16 = jnp.bfloat16
F32 = jnp.float32
VMEM = pl.BlockSpec(memory_space=pltpu.VMEM)
SMEM = pl.BlockSpec(memory_space=pltpu.SMEM)
PARAMS = pltpu.CompilerParams(vmem_limit_bytes=48 * 2**20)
NT = (((1,), (1,)), ((), ()))
TN = (((0,), (0,)), ((), ()))


def dot(a, b):
    return jnp.dot(a, b, preferred_element_type=F32)


def split3(values):
    high = values.astype(BF16)
    rest = values - high.astype(F32)
    mid = rest.astype(BF16)
    low = (rest - mid.astype(F32)).astype(BF16)
    return high, mid, low


def normalize_kernel(tokens, gain, normed):
    values = tokens[...].astype(F32)
    center = values - jnp.mean(values, axis=-1, keepdims=True)
    spread = jnp.mean(center * center, axis=-1, keepdims=True)
    wide_gain = gain[...].astype(F32)[None, :]
    normed[...] = (center * lax.rsqrt(spread + EPSILON) * wide_gain).astype(BF16)


def normalize(tokens, gain):
    return pl.pallas_call(
        normalize_kernel,
        out_shape=jax.ShapeDtypeStruct(tokens.shape, BF16),
        in_specs=[VMEM, VMEM],
        out_specs=VMEM,
        compiler_params=PARAMS,
        name="normalize",
    )(tokens, gain)


def project_kernel(members, place, normed, weight, mine, theirs, turned):
    core = place[0]
    kept = mine.shape[0] * HEAD
    rows = normed[...]
    for at, member in enumerate(members):
        product = dot(rows, weight[member]).astype(BF16)
        if member == 0:
            product = product * jnp.asarray(1.0 / HEAD**0.5, BF16)
        turned[at] = product.T
        for which, out in ((1 - core, theirs), (core, mine)):
            for head in range(mine.shape[0]):
                start = pl.multiple_of(which * kept + head * HEAD, HEAD)
                out[head, at * HEAD : (at + 1) * HEAD, :] = turned[at, pl.ds(start, HEAD), :]


def project(members, place, normed, weight):
    count, length = weight.shape[2] // HEAD // 2, normed.shape[0]
    shape = jax.ShapeDtypeStruct((count, len(members) * HEAD, length), BF16)
    return pl.pallas_call(
        functools.partial(project_kernel, members),
        out_shape=(shape, shape),
        in_specs=[SMEM, VMEM, VMEM],
        out_specs=(VMEM,) * 2,
        scratch_shapes=[pltpu.VMEM((len(members), weight.shape[2], length), BF16)],
        compiler_params=PARAMS,
        name="project",
    )(place, normed, weight)


def absorb_kernel(first, *refs):
    if first:
        queries, block, out, top = refs
    else:
        queries, block, carried, carried_top, out, top = refs
    keys = block[:HEAD, :].T
    length = block.shape[1]
    values = jnp.concatenate([block[HEAD:, :], jnp.ones((16, length), BF16)], axis=0)
    width = min(512, queries.shape[1])
    depth = min(512, length)
    for at in range(0, queries.shape[1], width):
        part = queries[:, at : at + width]
        running = None if first else carried[:, at : at + width]
        best = None if first else carried_top[0:1, at : at + width]
        for below in range(0, length, depth):
            scores = dot(keys[below : below + depth], part)
            raised_top = jnp.max(scores, axis=0, keepdims=True)
            if best is not None:
                raised_top = jnp.maximum(best, raised_top)
            weights = jnp.exp(scores - raised_top).astype(BF16)
            added = dot(values[:, below : below + depth], weights)
            running = added if best is None else running * jnp.exp(best - raised_top) + added
            best = raised_top
        out[:, at : at + width] = running
        top[:, at : at + width] = jnp.broadcast_to(best, (8, width))


def absorb(queries, block, state):
    count = queries.shape[1]
    shapes = (jax.ShapeDtypeStruct((HEAD + 16, count), F32), jax.ShapeDtypeStruct((8, count), F32))
    first = state is None
    return pl.pallas_call(
        functools.partial(absorb_kernel, first),
        out_shape=shapes,
        in_specs=[VMEM] * (2 if first else 4),
        out_specs=(VMEM, VMEM),
        input_output_aliases={} if first else {2: 0, 3: 1},
        compiler_params=PARAMS,
        name="absorb",
    )(queries, block, *(() if first else state))


def finish_kernel(*refs):
    states, (folded, context, share) = refs[:-3], refs[-3:]
    for head, state in enumerate(states):
        context[head * HEAD : (head + 1) * HEAD, :] = (state[:HEAD, :] / state[HEAD : HEAD + 1, :]).astype(BF16)
    whole = context[...]
    share[...] = sum(dot(part, whole) for part in split3(folded[...]))


def finish(states, folded):
    count = states[0].shape[1]
    return pl.pallas_call(
        finish_kernel,
        out_shape=(
            jax.ShapeDtypeStruct((len(states) * HEAD, count), BF16),
            jax.ShapeDtypeStruct((folded.shape[0], count), F32),
        ),
        in_specs=[VMEM] * (len(states) + 1),
        out_specs=(VMEM, VMEM),
        compiler_params=PARAMS,
        name="finish",
    )(*states, folded)


def turned(values, step):
    return pltpu.roll(values, step % values.shape[1], 1)


def three_columns(values, cols):
    cells = values.shape[1]
    column = lax.rem(lax.broadcasted_iota(jnp.int32, (1, cells), 1), cols)
    wide = values.astype(F32)
    left = jnp.where(column == 0, 0.0, turned(wide, 1)).astype(BF16)
    right = jnp.where(column == cols - 1, 0.0, turned(wide, -1)).astype(BF16)
    return jnp.concatenate([left, values.astype(BF16), right], axis=0)


def three_rows(weights, columns, cols):
    cells = columns.shape[1] - 2 * cols
    return sum(dot(weights[a], columns[:, a * cols : a * cols + cells]) for a in range(3))


def network_kernel(
    cols, frame_rows, place, own_map, other_map, rims, other_rims, forward, backward, head, context, holo, sums,
    gradient, hidden, pre_one, pre_two,
):
    core, half, row_at = place[0], place[1], place[2]
    own = context.shape[1]
    cells = hidden.shape[1]
    rim = (cells - own) // 2
    row_count = cells // cols
    above = rim // cols
    first_row = row_at - above
    piece = own // 2
    for order, (mine, theirs, at) in enumerate(
        ((rims, other_rims, 0), (own_map, other_map, 0), (rims, other_rims, piece))
    ):
        for which, source in ((core, mine), (1 - core, theirs)):
            start = pl.multiple_of(order * own + which * piece, 128)
            hidden[:, pl.ds(start, piece)] = source[:, at : at + piece]

    def inside(start_row, rows):
        lane = lax.broadcasted_iota(jnp.int32, (1, rows * cols), 1)
        frame_lane = lane + (first_row + start_row) * cols
        return jnp.logical_and(frame_lane >= 0, frame_lane < frame_rows * cols)

    channels, outputs = forward.shape[2], head.shape[0]
    columns_zero = three_columns(hidden[:channels, :], cols)
    first = three_rows(forward[0], columns_zero, cols)
    rows_one = row_count - 2
    one = jnp.where(inside(1, rows_one), first * jax.nn.sigmoid(first), 0.0)
    columns_one = three_columns(one, cols)
    second = three_rows(forward[1], columns_one, cols)
    rows_two = row_count - 4
    sigmoid_two = jax.nn.sigmoid(second)
    two = (second * sigmoid_two).astype(BF16)
    holo[...] = dot(head[...], two[:, rim - 2 * cols : rim - 2 * cols + own])
    pieces = hidden[channels:, 2 * cols : cells - 2 * cols].astype(F32)
    cotangent = pieces[:outputs] + pieces[outputs : 2 * outputs] + pieces[2 * outputs : 3 * outputs]
    grad_two = lax.dot_general(
        head[...].astype(F32), cotangent, TN, precision=lax.Precision.HIGHEST, preferred_element_type=F32
    ).astype(BF16)
    slope = grad_two.astype(F32) * sigmoid_two * (1.0 + second * (1.0 - sigmoid_two))
    pre_grad_two = jnp.where(inside(2, rows_two), slope, 0.0)
    grad_one = three_rows(backward[1], three_columns(pre_grad_two, cols), cols).astype(BF16)
    rows_grad = row_count - 6
    middle = first[:, 2 * cols : 2 * cols + rows_grad * cols]
    sigmoid_one = jax.nn.sigmoid(middle)
    slope = grad_one.astype(F32) * sigmoid_one * (1.0 + middle * (1.0 - sigmoid_one))
    pre_grad_one = jnp.where(inside(3, rows_grad), slope, 0.0)
    grad_zero = three_rows(backward[0], three_columns(pre_grad_one, cols), cols).astype(BF16)
    pre_one[...] = pre_grad_one[:, rim - 3 * cols : rim - 3 * cols + own].astype(BF16)
    pre_two[...] = pre_grad_two[:, rim - 2 * cols : rim - 2 * cols + own].astype(BF16)

    share = sums.shape[0]
    taps = 9 * channels
    for layer, (pre, columns, offset) in enumerate(((pre_one, columns_zero, rim), (pre_two, columns_one, rim - cols))):

        @pl.when(core == layer)
        def _(pre=pre, columns=columns, offset=offset):
            stacked = jnp.concatenate(
                [columns[:, offset + (a - 1) * cols : offset + (a - 1) * cols + own] for a in range(3)], axis=0
            )
            rows = pre[pl.ds(pl.multiple_of(half * share, 16), share), :]
            sums[:, :taps] = lax.dot_general(rows, stacked, NT, preferred_element_type=F32)

    total = None
    for side in range(2):
        where = lax.rem(core + side, 2)
        seen = context[:, pl.ds(pl.multiple_of(where * piece, 128), piece)]
        term = lax.dot_general(
            grad_zero[:, side * piece : (side + 1) * piece], seen, NT, preferred_element_type=F32
        )
        total = term if total is None else total + term
    gradient[...] = total


def network(place, maps, forward, backward, head, context, cols, frame_rows, col_count):
    own = context.shape[1]
    channels = forward.shape[2]
    return pl.pallas_call(
        functools.partial(network_kernel, cols, frame_rows),
        out_shape=(
            jax.ShapeDtypeStruct((head.shape[0], own), F32),
            jax.ShapeDtypeStruct((channels // col_count, 9 * channels), F32),
            jax.ShapeDtypeStruct((channels, context.shape[0]), F32),
        ),
        in_specs=[SMEM] + [VMEM] * 8,
        out_specs=(VMEM,) * 3,
        scratch_shapes=[pltpu.VMEM((maps[0].shape[0], 3 * own), BF16)] + [pltpu.VMEM((channels, own), BF16)] * 2,
        compiler_params=PARAMS,
        name="network",
    )(place, *maps, forward, backward, head, context)


def swapped(values, axis):
    size = lax.axis_size(axis)
    return lax.ppermute(values, axis, [(i, i ^ 1) for i in range(size)])


def passed(values, axis, step, wrap):
    size = lax.axis_size(axis)
    pairs = [(i, (i + step) % size) for i in range(size) if wrap or 0 <= i + step < size]
    return lax.ppermute(values, axis, pairs)


def round_ring(values):
    size = lax.axis_size("tok")
    chips = size // 2
    order = [at for at in range(chips) if at == 0 or at % 2 == 1] + [
        at for at in reversed(range(chips)) if at and at % 2 == 0
    ]
    following = {order[at]: order[(at + 1) % chips] for at in range(chips)}
    return lax.ppermute(values, "tok", [(i, 2 * following[i // 2] + i % 2) for i in range(size)])


def everyone(values, axis, stride, count):
    sent = values.astype(BF16)
    terms = [(passed(sent, axis, stride * step, True) if step else sent).astype(F32) for step in range(count)]
    while len(terms) > 1:
        apart = len(terms) // 2
        terms = [terms[at] + terms[at + apart] for at in range(apart)]
    return terms[0]


def in_order(core, mine, theirs, axis):
    return jnp.where(
        core == 0, jnp.concatenate([mine, theirs], axis=axis), jnp.concatenate([theirs, mine], axis=axis)
    )


def shards(
    tokens, ln_gain, qkv_weight, out_weight, readout_weight, conv_weight, head_weight, holo_cot
):
    frame_rows = tokens[0]
    cotangent = holo_cot[0]
    rows_dev, cols_dev = cotangent.shape[1:]
    tok_count, col_count, dp_count = (lax.axis_size(axis) for axis in ("tok", "col", "dp"))
    chips = tok_count // 2
    tok_at, half = lax.axis_index("tok"), lax.axis_index("col")
    core = lax.rem(tok_at, 2)
    chip_row = (tok_at - core) * rows_dev
    place = jnp.stack([core, half, chip_row]).astype(jnp.int32)
    layers, channels = conv_weight.shape[:2]
    cols = cols_dev * col_count
    length = frame_rows.shape[0]

    normed = normalize(frame_rows, ln_gain)
    own_keyed, their_keyed = project((1, 2), place, normed, qkv_weight)
    own_keyed, their_keyed, normed = lax.optimization_barrier((own_keyed, their_keyed, normed))
    got_keyed = swapped(their_keyed, "tok")
    own_queries, their_queries = project((0,), place, normed, qkv_weight)
    got_queries = swapped(their_queries, "tok")
    count = got_keyed.shape[0]
    kept = count * HEAD
    blocks = [jnp.concatenate([own_keyed[head], got_keyed[head]], axis=1) for head in range(count)]
    queries = [jnp.concatenate([own_queries[head], got_queries[head]], axis=1) for head in range(count)]
    states = [None] * count

    def prepare(conv_weight, out_weight, readout_weight, frame_rows, cotangent):
        taps = conv_weight.reshape(layers, channels, 3, 3, channels)
        forward = jnp.transpose(taps.reshape(layers, channels, 3, 3 * channels), (0, 2, 1, 3))
        backward = jnp.transpose(taps[:, :, ::-1, ::-1, :], (0, 2, 4, 3, 1)).reshape(
            layers, 3, channels, 3 * channels
        )
        own_out = lax.dynamic_slice_in_dim(out_weight, core * kept, kept, 0)
        folded = lax.dot_general(readout_weight, own_out, (((0,), (1,)), ((), ())), preferred_element_type=F32)
        direct = lax.dot_general(readout_weight, frame_rows, (((0,), (1,)), ((), ())), preferred_element_type=F32)
        wide_cot = in_order(half, cotangent, swapped(cotangent, "col"), 2)
        exact_cot = jnp.concatenate(split3(wide_cot.reshape(wide_cot.shape[0], -1)), axis=0)
        exact_cot = jnp.pad(exact_cot, ((0, -exact_cot.shape[0] % 16), (0, 0)))
        return (forward, backward, folded, direct, exact_cot)

    for turn in range(chips):
        arriving = [round_ring(block) for block in blocks] if turn < chips - 1 else blocks
        for head in range(count):
            states[head] = absorb(queries[head], blocks[head], states[head])
            if turn == 0 and head == 0:
                states[head], given = lax.optimization_barrier(
                    (states[head], (conv_weight, out_weight, readout_weight, frame_rows, cotangent))
                )
                prepared = prepare(*given)
            if turn == min(1, chips - 1) and head == count - 1:
                states[head], prepared = lax.optimization_barrier((states[head], prepared))
            arriving[head], states[head] = lax.optimization_barrier((arriving[head], states[head]))
            if head + 1 < count:
                gate = arriving[head] if turn < chips - 1 else states[head]
                blocks[head + 1], gate = lax.optimization_barrier((blocks[head + 1], gate))
                if turn < chips - 1:
                    arriving[head] = gate
                else:
                    states[head] = gate
        blocks = arriving
    forward, backward, folded, direct, exact_cot = prepared

    context, share = finish([state[0] for state in states], folded)
    partial = share[:, :length] + swapped(share[:, length:], "tok")
    partial = (partial + jnp.where(half == 0, direct, 0.0)).astype(BF16)
    own_map = (partial.astype(F32) + swapped(partial, "col").astype(F32)).astype(BF16)
    own_map = jnp.concatenate([own_map, exact_cot], axis=0)
    rims = jnp.concatenate([passed(own_map, "tok", 2, False), passed(own_map, "tok", -2, False)], axis=1)
    rows_chip = 2 * rows_dev
    maps = (own_map, swapped(own_map, "tok"), rims, swapped(rims, "tok"))
    holo, sums, gradient = network(
        place, maps, forward, backward, head_weight, context, cols, tok_count * rows_dev, col_count
    )
    holo = holo.reshape(-1, rows_chip, cols)
    hologram = lax.dynamic_slice(
        holo, (0, core * rows_dev, half * cols_dev), (holo.shape[0], rows_dev, cols_dev)
    )

    taps_wide = sums.shape[1]
    lanes = 128 * ((taps_wide + 127) // 128)
    rows = sums.shape[0]
    pieces = gradient.shape[0] // rows
    folded_gradient = [gradient[at * rows : (at + 1) * rows] for at in range(pieces)]
    sent = jnp.concatenate([jnp.pad(sums, ((0, 0), (0, lanes - taps_wide))), *folded_gradient], axis=1)
    summed = everyone(sent, "dp", 1, dp_count)
    total = everyone(summed, "tok", 2, chips)
    own_grad = total[:, :taps_wide]
    col_grad = swapped(own_grad, "col")
    wide = gradient.shape[1]
    own_small = jnp.concatenate(
        [total[:, lanes + at * wide : lanes + (at + 1) * wide] for at in range(pieces)], axis=0
    )
    small = in_order(core, own_small, swapped(own_small, "tok"), 1)
    out_grad = lax.dot_general(
        small, readout_weight.astype(F32), (((0,), (1,)), ((), ())), precision=lax.Precision.HIGHEST
    )
    core_grad = swapped(own_grad, "tok")
    col_grad, out_grad, core_grad = lax.optimization_barrier((col_grad, out_grad, core_grad))
    far_grad = swapped(col_grad, "tok")
    layer_grad = in_order(half, own_grad, col_grad, 0)
    other_grad = in_order(half, core_grad, far_grad, 0)
    conv_grad = in_order(core, layer_grad[None], other_grad[None], 0)
    return (hologram[None], conv_grad, out_grad)


def solution(mesh):
    in_specs = (
        P("dp", "tok", None),
        P(),
        P(None, None, "col"),
        P("col", None),
        P(),
        P(),
        P(),
        P("dp", None, "tok", "col"),
    )
    out_specs = (P("dp", None, "tok", "col"), P(), P("col", None))
    return jax.shard_map(shards, mesh=mesh, in_specs=in_specs, out_specs=out_specs, check_vma=False)
```

```python
import functools

import jax
import jax.numpy as jnp
from jax import lax
from jax.experimental import pallas as pl
from jax.experimental.pallas import tpu as pltpu
from jax.sharding import PartitionSpec as P


HEAD = 64
EPSILON = 1e-05
BF16 = jnp.bfloat16
F32 = jnp.float32
VMEM = pl.BlockSpec(memory_space=pltpu.VMEM)
SMEM = pl.BlockSpec(memory_space=pltpu.SMEM)
PARAMS = pltpu.CompilerParams(vmem_limit_bytes=48 * 2**20)
NT = (((1,), (1,)), ((), ()))
TN = (((0,), (0,)), ((), ()))


def dot(a, b):
    return jnp.dot(a, b, preferred_element_type=F32)


def split3(values):
    high = values.astype(BF16)
    rest = values - high.astype(F32)
    mid = rest.astype(BF16)
    low = (rest - mid.astype(F32)).astype(BF16)
    return high, mid, low


def normalize_kernel(tokens, gain, normed):
    values = tokens[...].astype(F32)
    center = values - jnp.mean(values, axis=-1, keepdims=True)
    spread = jnp.mean(center * center, axis=-1, keepdims=True)
    normed[...] = (center * lax.rsqrt(spread + EPSILON) * gain[...]).astype(BF16)


def normalize(tokens, gain):
    return pl.pallas_call(
        normalize_kernel,
        out_shape=jax.ShapeDtypeStruct(tokens.shape, BF16),
        in_specs=[VMEM, VMEM],
        out_specs=VMEM,
        compiler_params=PARAMS,
        name="normalize",
    )(tokens, gain)


def project_kernel(members, place, normed, weight, mine, theirs, turned):
    core = place[0]
    kept = mine.shape[0] * HEAD
    rows = normed[...]
    for at, member in enumerate(members):
        product = dot(rows, weight[member]).astype(BF16)
        if member == 0:
            product = product * jnp.asarray(1.0 / HEAD**0.5, BF16)
        turned[at] = product.T
        for which, out in ((1 - core, theirs), (core, mine)):
            for head in range(mine.shape[0]):
                start = pl.multiple_of(which * kept + head * HEAD, HEAD)
                out[head, at * HEAD : (at + 1) * HEAD, :] = turned[at, pl.ds(start, HEAD), :]


def project(members, place, normed, weight):
    count, length = weight.shape[2] // HEAD // 2, normed.shape[0]
    shape = jax.ShapeDtypeStruct((count, len(members) * HEAD, length), BF16)
    return pl.pallas_call(
        functools.partial(project_kernel, members),
        out_shape=(shape, shape),
        in_specs=[SMEM, VMEM, VMEM],
        out_specs=(VMEM,) * 2,
        scratch_shapes=[pltpu.VMEM((len(members), weight.shape[2], length), BF16)],
        compiler_params=PARAMS,
        name="project",
    )(place, normed, weight)


def absorb_kernel(first, *refs):
    if first:
        queries, block, out, top = refs
    else:
        queries, block, carried, carried_top, out, top = refs
    keys = block[:HEAD, :].T
    length = block.shape[1]
    values = jnp.concatenate([block[HEAD:, :], jnp.ones((16, length), BF16)], axis=0)
    width = min(512, queries.shape[1])
    depth = min(512, length)
    for at in range(0, queries.shape[1], width):
        part = queries[:, at : at + width]
        running = None if first else carried[:, at : at + width]
        best = None if first else carried_top[0:1, at : at + width]
        for below in range(0, length, depth):
            scores = dot(keys[below : below + depth], part)
            raised_top = jnp.max(scores, axis=0, keepdims=True)
            if best is not None:
                raised_top = jnp.maximum(best, raised_top)
            weights = jnp.exp(scores - raised_top).astype(BF16)
            added = dot(values[:, below : below + depth], weights)
            running = added if best is None else running * jnp.exp(best - raised_top) + added
            best = raised_top
        out[:, at : at + width] = running
        top[:, at : at + width] = jnp.broadcast_to(best, (8, width))


def absorb(queries, block, state):
    count = queries.shape[1]
    shapes = (jax.ShapeDtypeStruct((HEAD + 16, count), F32), jax.ShapeDtypeStruct((8, count), F32))
    first = state is None
    return pl.pallas_call(
        functools.partial(absorb_kernel, first),
        out_shape=shapes,
        in_specs=[VMEM] * (2 if first else 4),
        out_specs=(VMEM, VMEM),
        input_output_aliases={} if first else {2: 0, 3: 1},
        compiler_params=PARAMS,
        name="absorb",
    )(queries, block, *(() if first else state))


def closing_kernel(start, queries, block, *refs):
    states, (folded, context, share) = refs[:-3], refs[-3:]
    carried, carried_top = states[-2:]
    length = context.shape[1]
    where = slice(start, start + length)
    keys = block[:HEAD, :].T
    values = jnp.concatenate([block[HEAD:, :], jnp.ones((16, block.shape[1]), BF16)], axis=0)
    depth = min(512, block.shape[1])
    running, best = carried[:, where], carried_top[0:1, where]
    for below in range(0, block.shape[1], depth):
        scores = dot(keys[below : below + depth], queries[:, where])
        raised_top = jnp.maximum(best, jnp.max(scores, axis=0, keepdims=True))
        weights = jnp.exp(scores - raised_top).astype(BF16)
        running = running * jnp.exp(best - raised_top) + dot(values[:, below : below + depth], weights)
        best = raised_top
    sums = [state[:, where] for state in states[:-2]] + [running]
    for head, state in enumerate(sums):
        context[head * HEAD : (head + 1) * HEAD, :] = (state[:HEAD] / state[HEAD : HEAD + 1]).astype(BF16)
    whole = context[...]
    share[...] = sum(dot(part, whole) for part in split3(folded[...]))


def closing(start, length, queries, block, states, folded):
    sums = [state[0] for state in states[:-1]] + list(states[-1])
    return pl.pallas_call(
        functools.partial(closing_kernel, start),
        out_shape=(
            jax.ShapeDtypeStruct((len(states) * HEAD, length), BF16),
            jax.ShapeDtypeStruct((folded.shape[0], length), F32),
        ),
        in_specs=[VMEM] * (len(sums) + 3),
        out_specs=(VMEM, VMEM),
        compiler_params=PARAMS,
        name="closing",
    )(queries, block, *sums, folded)


def turned(values, step):
    return pltpu.roll(values, step % values.shape[1], 1)


def three_columns(values, cols):
    cells = values.shape[1]
    column = lax.rem(lax.broadcasted_iota(jnp.int32, (1, cells), 1), cols)
    wide = values.astype(F32)
    left = jnp.where(column == 0, 0.0, turned(wide, 1)).astype(BF16)
    right = jnp.where(column == cols - 1, 0.0, turned(wide, -1)).astype(BF16)
    return jnp.concatenate([left, values.astype(BF16), right], axis=0)


def three_rows(weights, columns, cols):
    cells = columns.shape[1] - 2 * cols
    return sum(dot(weights[a], columns[:, a * cols : a * cols + cells]) for a in range(3))


def network_kernel(
    cols, frame_rows, place, chip_map, near, far, forward, backward, head, own_context, their_context, holo, sums,
    gradient, hidden, pre_one, pre_two, grads,
):
    core, half, row_at = place[0], place[1], place[2]
    own = chip_map.shape[1]
    cells = hidden.shape[1]
    rim = (cells - own) // 2
    row_count = cells // cols
    above = rim // cols
    first_row = row_at - above
    piece = own // 2
    down = (core == place[3]).astype(jnp.int32)
    for source, base, lead in ((chip_map, own, core), (near, 2 * own * down, core), (far, 2 * own * (1 - down), 1 - core)):
        for side in range(2):
            start = pl.multiple_of(base + lax.rem(lead + side, 2) * piece, 128)
            hidden[:, pl.ds(start, piece)] = source[:, side * piece : (side + 1) * piece]

    def inside(start_row, rows):
        lane = lax.broadcasted_iota(jnp.int32, (1, rows * cols), 1)
        frame_lane = lane + (first_row + start_row) * cols
        return jnp.logical_and(frame_lane >= 0, frame_lane < frame_rows * cols)

    channels, outputs = forward.shape[2], head.shape[0]
    columns_zero = three_columns(hidden[:channels, :], cols)
    first = three_rows(forward[0], columns_zero, cols)
    rows_one = row_count - 2
    one = jnp.where(inside(1, rows_one), first * jax.nn.sigmoid(first), 0.0)
    columns_one = three_columns(one, cols)
    second = three_rows(forward[1], columns_one, cols)
    rows_two = row_count - 4
    sigmoid_two = jax.nn.sigmoid(second)
    two = (second * sigmoid_two).astype(BF16)
    holo[...] = dot(head[...], two[:, rim - 2 * cols : rim - 2 * cols + own])
    pieces = hidden[channels:, 2 * cols : cells - 2 * cols].astype(F32)
    cotangent = pieces[:outputs] + pieces[outputs : 2 * outputs] + pieces[2 * outputs : 3 * outputs]
    grad_two = lax.dot_general(
        head[...].astype(F32), cotangent, TN, precision=lax.Precision.HIGHEST, preferred_element_type=F32
    ).astype(BF16)
    slope = grad_two.astype(F32) * sigmoid_two * (1.0 + second * (1.0 - sigmoid_two))
    pre_grad_two = jnp.where(inside(2, rows_two), slope, 0.0)
    grad_one = three_rows(backward[1], three_columns(pre_grad_two, cols), cols).astype(BF16)
    rows_grad = row_count - 6
    middle = first[:, 2 * cols : 2 * cols + rows_grad * cols]
    sigmoid_one = jax.nn.sigmoid(middle)
    slope = grad_one.astype(F32) * sigmoid_one * (1.0 + middle * (1.0 - sigmoid_one))
    pre_grad_one = jnp.where(inside(3, rows_grad), slope, 0.0)
    grad_zero = three_rows(backward[0], three_columns(pre_grad_one, cols), cols).astype(BF16)
    pre_one[...] = pre_grad_one[:, rim - 3 * cols : rim - 3 * cols + own].astype(BF16)
    pre_two[...] = pre_grad_two[:, rim - 2 * cols : rim - 2 * cols + own].astype(BF16)

    share = sums.shape[0]
    taps = 9 * channels
    for layer, (pre, columns, offset) in enumerate(((pre_one, columns_zero, rim), (pre_two, columns_one, rim - cols))):

        @pl.when(core == layer)
        def _(pre=pre, columns=columns, offset=offset):
            stacked = jnp.concatenate(
                [columns[:, offset + (a - 1) * cols : offset + (a - 1) * cols + own] for a in range(3)], axis=0
            )
            rows = pre[pl.ds(pl.multiple_of(half * share, 16), share), :]
            sums[:, :taps] = lax.dot_general(rows, stacked, NT, preferred_element_type=F32)

    grads[...] = grad_zero
    gradient[...] = sum(
        lax.dot_general(
            grads[:, pl.ds(pl.multiple_of(at * piece, 128), piece)], seen[...], NT, preferred_element_type=F32
        )
        for at, seen in ((core, own_context), (1 - core, their_context))
    )


def network(place, maps, forward, backward, head, own_context, their_context, cols, frame_rows, col_count):
    own = maps[0].shape[1]
    channels = forward.shape[2]
    return pl.pallas_call(
        functools.partial(network_kernel, cols, frame_rows),
        out_shape=(
            jax.ShapeDtypeStruct((head.shape[0], own), F32),
            jax.ShapeDtypeStruct((channels // col_count, 9 * channels), F32),
            jax.ShapeDtypeStruct((channels, own_context.shape[0]), F32),
        ),
        in_specs=[SMEM] + [VMEM] * 8,
        out_specs=(VMEM,) * 3,
        scratch_shapes=[pltpu.VMEM((maps[0].shape[0], 3 * own), BF16)] + [pltpu.VMEM((channels, own), BF16)] * 3,
        compiler_params=PARAMS,
        name="network",
    )(place, *maps, forward, backward, head, own_context, their_context)


def swapped(values, axis):
    size = lax.axis_size(axis)
    return lax.ppermute(values, axis, [(i, i ^ 1) for i in range(size)])


def passed(values, axis, step, wrap):
    size = lax.axis_size(axis)
    pairs = [(i, (i + step) % size) for i in range(size) if wrap or 0 <= i + step < size]
    return lax.ppermute(values, axis, pairs)


def beside(values):
    size = lax.axis_size("tok")
    chips = size // 2
    pairs = []
    for at in range(chips):
        for core, other in ((0, at ^ 1), (1, ((at + 1) ^ 1) - 1)):
            if 0 <= other < chips:
                pairs.append((2 * at + core, 2 * other + core))
    return lax.ppermute(values, "tok", pairs)


def round_ring(values):
    size = lax.axis_size("tok")
    chips = size // 2
    order = [at for at in range(chips) if at == 0 or at % 2 == 1] + [
        at for at in reversed(range(chips)) if at and at % 2 == 0
    ]
    following = {order[at]: order[(at + 1) % chips] for at in range(chips)}
    return lax.ppermute(values, "tok", [(i, 2 * following[i // 2] + i % 2) for i in range(size)])


def everyone(values, axis, stride, count):
    sent = values.astype(BF16)
    terms = [(passed(sent, axis, stride * step, True) if step else sent).astype(F32) for step in range(count)]
    while len(terms) > 1:
        apart = len(terms) // 2
        terms = [terms[at] + terms[at + apart] for at in range(apart)]
    return terms[0]


def in_order(core, mine, theirs, axis):
    return jnp.where(
        core == 0, jnp.concatenate([mine, theirs], axis=axis), jnp.concatenate([theirs, mine], axis=axis)
    )


def step(
    tokens, ln_gain, qkv_weight, out_weight, readout_weight, conv_weight, head_weight, holo_cot
):
    frame_rows = tokens[0]
    cotangent = holo_cot[0]
    rows_dev, cols_dev = cotangent.shape[1:]
    tok_count, col_count, dp_count = (lax.axis_size(axis) for axis in ("tok", "col", "dp"))
    chips = tok_count // 2
    tok_at, half = lax.axis_index("tok"), lax.axis_index("col")
    core = lax.rem(tok_at, 2)
    chip_row = (tok_at - core) * rows_dev
    place = jnp.stack([core, half, chip_row, lax.rem(tok_at // 2, 2)]).astype(jnp.int32)
    layers, channels = conv_weight.shape[:2]
    cols = cols_dev * col_count
    length = frame_rows.shape[0]

    normed = normalize(frame_rows, ln_gain.astype(F32).reshape(1, -1))
    own_keyed, their_keyed = project((1, 2), place, normed, qkv_weight)
    got_keyed = swapped(their_keyed, "tok")
    count = got_keyed.shape[0]
    kept = count * HEAD
    blocks = [jnp.concatenate([own_keyed[head], got_keyed[head]], axis=1) for head in range(count)]
    blocks, normed = lax.optimization_barrier((blocks, normed))
    own_queries, their_queries = project((0,), place, normed, qkv_weight)
    got_queries = swapped(their_queries, "tok")
    queries = [jnp.concatenate([own_queries[head], got_queries[head]], axis=1) for head in range(count)]
    states = [None] * count

    def prepare(conv_weight, out_weight, readout_weight, frame_rows, cotangent):
        taps = conv_weight.reshape(layers, channels, 3, 3, channels)
        forward = jnp.transpose(taps.reshape(layers, channels, 3, 3 * channels), (0, 2, 1, 3))
        backward = jnp.transpose(taps[:, :, ::-1, ::-1, :], (0, 2, 4, 3, 1)).reshape(
            layers, 3, channels, 3 * channels
        )
        own_out = lax.dynamic_slice_in_dim(out_weight, core * kept, kept, 0)
        folded = lax.dot_general(readout_weight, own_out, (((0,), (1,)), ((), ())), preferred_element_type=F32)
        direct = lax.dot_general(readout_weight, frame_rows, (((0,), (1,)), ((), ())), preferred_element_type=F32)
        wide_cot = in_order(half, cotangent, swapped(cotangent, "col"), 2)
        exact_cot = jnp.concatenate(split3(wide_cot.reshape(wide_cot.shape[0], -1)), axis=0)
        exact_cot = jnp.pad(exact_cot, ((0, -exact_cot.shape[0] % 16), (0, 0)))
        return (forward, backward, folded, direct, exact_cot)

    for turn in range(chips):
        arriving = blocks
        if turn < chips - 1:
            arriving = []
            for block in blocks:
                arriving.append(round_ring(block))
        for head in range(count):
            if turn == chips - 1 and head == count - 1:
                break
            states[head] = absorb(queries[head], blocks[head], states[head])
            if turn == 0 and head == 0:
                states[head], given = lax.optimization_barrier(
                    (states[head], (conv_weight, out_weight, readout_weight, frame_rows, cotangent))
                )
                prepared = prepare(*given)
            if turn == min(1, chips - 2) and head == count - 1:
                states[head], prepared = lax.optimization_barrier((states[head], prepared))
            arriving[head], states[head] = lax.optimization_barrier((arriving[head], states[head]))
            if head + 1 < count:
                gate = arriving[head] if turn < chips - 1 else states[head]
                blocks[head + 1], gate = lax.optimization_barrier((blocks[head + 1], gate))
                if turn < chips - 1:
                    arriving[head] = gate
                else:
                    states[head] = gate
        blocks = arriving
    forward, backward, folded, direct, exact_cot = prepared

    last = (queries[-1], blocks[-1], states, folded)
    their_context, their_share = closing(length, length, *last)
    own_context, own_share = closing(0, length, *last)
    partial = own_share + swapped(their_share, "tok")
    partial = (partial + jnp.where(half == 0, direct, 0.0)).astype(BF16)
    own_map = (partial.astype(F32) + swapped(partial, "col").astype(F32)).astype(BF16)
    own_map = jnp.concatenate([own_map, exact_cot], axis=0)
    chip_map = jnp.concatenate([own_map, swapped(own_map, "tok")], axis=1)
    near = beside(chip_map)
    rows_chip = 2 * rows_dev
    maps = (chip_map, near, swapped(near, "tok"))
    holo, sums, gradient = network(
        place, maps, forward, backward, head_weight, own_context, their_context, cols, tok_count * rows_dev, col_count
    )
    holo = holo.reshape(-1, rows_chip, cols)
    hologram = lax.dynamic_slice(
        holo, (0, core * rows_dev, half * cols_dev), (holo.shape[0], rows_dev, cols_dev)
    )

    taps_wide = sums.shape[1]
    lanes = 128 * ((taps_wide + 127) // 128)
    rows = sums.shape[0]
    pieces = gradient.shape[0] // rows
    folded_gradient = [gradient[at * rows : (at + 1) * rows] for at in range(pieces)]
    sent = jnp.concatenate([jnp.pad(sums, ((0, 0), (0, lanes - taps_wide))), *folded_gradient], axis=1)
    summed = everyone(sent, "dp", 1, dp_count)
    total = everyone(summed, "tok", 2, chips)
    own_grad = total[:, :taps_wide]
    col_grad = swapped(own_grad, "col")
    wide = gradient.shape[1]
    own_small = jnp.concatenate(
        [total[:, lanes + at * wide : lanes + (at + 1) * wide] for at in range(pieces)], axis=0
    )
    small = in_order(core, own_small, swapped(own_small, "tok"), 1)
    out_grad = lax.dot_general(
        small, readout_weight.astype(F32), (((0,), (1,)), ((), ())), precision=lax.Precision.HIGHEST
    )
    core_grad = swapped(own_grad, "tok")
    col_grad, out_grad, core_grad = lax.optimization_barrier((col_grad, out_grad, core_grad))
    far_grad = swapped(col_grad, "tok")
    layer_grad = in_order(half, own_grad, col_grad, 0)
    other_grad = in_order(half, core_grad, far_grad, 0)
    conv_grad = in_order(core, layer_grad[None], other_grad[None], 0)
    return (hologram[None], conv_grad, out_grad)


def solution(mesh):
    in_specs = (
        P("dp", "tok", None),
        P(),
        P(None, None, "col"),
        P("col", None),
        P(),
        P(),
        P(),
        P("dp", None, "tok", "col"),
    )
    out_specs = (P("dp", None, "tok", "col"), P(), P("col", None))
    return jax.shard_map(step, mesh=mesh, in_specs=in_specs, out_specs=out_specs, check_vma=False)
```

```python
import functools

import jax
import jax.numpy as jnp
from jax import lax
from jax.experimental import pallas as pl
from jax.experimental.pallas import tpu as pltpu
from jax.sharding import PartitionSpec as P


HEAD = 64
EPSILON = 1e-05
BF16 = jnp.bfloat16
F32 = jnp.float32
VMEM = pl.BlockSpec(memory_space=pltpu.VMEM)
SMEM = pl.BlockSpec(memory_space=pltpu.SMEM)
PARAMS = pltpu.CompilerParams(vmem_limit_bytes=48 * 2**20)
NT = (((1,), (1,)), ((), ()))
TN = (((0,), (0,)), ((), ()))


def dot(a, b):
    return jnp.dot(a, b, preferred_element_type=F32)


def split3(values):
    high = values.astype(BF16)
    rest = values - high.astype(F32)
    mid = rest.astype(BF16)
    low = (rest - mid.astype(F32)).astype(BF16)
    return high, mid, low


def normalize_kernel(tokens, gain, normed):
    values = tokens[...].astype(F32)
    center = values - jnp.mean(values, axis=-1, keepdims=True)
    spread = jnp.mean(center * center, axis=-1, keepdims=True)
    normed[...] = (center * lax.rsqrt(spread + EPSILON) * gain[...]).astype(BF16)


def normalize(tokens, gain):
    return pl.pallas_call(
        normalize_kernel,
        out_shape=jax.ShapeDtypeStruct(tokens.shape, BF16),
        in_specs=[VMEM, VMEM],
        out_specs=VMEM,
        compiler_params=PARAMS,
        name="normalize",
    )(tokens, gain)


def project_kernel(members, place, normed, weight, mine, theirs, turned):
    core = place[0]
    kept = mine.shape[0] * HEAD
    rows = normed[...]
    for at, member in enumerate(members):
        product = dot(rows, weight[member]).astype(BF16)
        if member == 0:
            product = product * jnp.asarray(1.0 / HEAD**0.5, BF16)
        turned[at] = product.T
        for which, out in ((1 - core, theirs), (core, mine)):
            for head in range(mine.shape[0]):
                start = pl.multiple_of(which * kept + head * HEAD, HEAD)
                out[head, at * HEAD : (at + 1) * HEAD, :] = turned[at, pl.ds(start, HEAD), :]


def project(members, place, normed, weight):
    count, length = weight.shape[2] // HEAD // 2, normed.shape[0]
    shape = jax.ShapeDtypeStruct((count, len(members) * HEAD, length), BF16)
    return pl.pallas_call(
        functools.partial(project_kernel, members),
        out_shape=(shape, shape),
        in_specs=[SMEM, VMEM, VMEM],
        out_specs=(VMEM,) * 2,
        scratch_shapes=[pltpu.VMEM((len(members), weight.shape[2], length), BF16)],
        compiler_params=PARAMS,
        name="project",
    )(place, normed, weight)


def attend(queries, block, running, best):
    length = block.shape[1]
    keys = block[:HEAD].T
    values = jnp.concatenate([block[HEAD:], jnp.ones((16, length), BF16)], axis=0)
    depth = min(512, length)
    for below in range(0, length, depth):
        scores = dot(keys[below : below + depth], queries)
        raised_top = jnp.max(scores, axis=0, keepdims=True)
        if best is not None:
            raised_top = jnp.maximum(best, raised_top)
        weights = jnp.exp(scores - raised_top).astype(BF16)
        added = dot(values[:, below : below + depth], weights)
        running = added if best is None else running * jnp.exp(best - raised_top) + added
        best = raised_top
    return running, best


def absorb_kernel(first, own, got, block, *refs):
    carried, carried_top = (None, None) if first else refs[:2]
    out, top = refs[-2:]
    length = own.shape[2]
    for head in range(own.shape[0]):
        for side, queries in enumerate((own, got)):
            where = slice(side * length, (side + 1) * length)
            running = None if first else carried[head, :, where]
            best = None if first else carried_top[head, 0:1, where]
            running, best = attend(queries[head], block[head], running, best)
            out[head, :, where] = running
            top[head, :, where] = jnp.broadcast_to(best, (8, length))


def absorb(queries, block, state):
    heads, _, length = queries[0].shape
    shapes = tuple(jax.ShapeDtypeStruct((heads, rows, 2 * length), F32) for rows in (HEAD + 16, 8))
    first = state is None
    return pl.pallas_call(
        functools.partial(absorb_kernel, first),
        out_shape=shapes,
        in_specs=[VMEM] * (3 if first else 5),
        out_specs=(VMEM, VMEM),
        input_output_aliases={} if first else {3: 0, 4: 1},
        compiler_params=PARAMS,
        name="absorb",
    )(*queries, block, *(() if first else state))


def closing_kernel(side, queries, block, carried, carried_top, folded, context, share):
    length = context.shape[1]
    where = slice(side * length, (side + 1) * length)
    for head in range(queries.shape[0]):
        running, _ = attend(queries[head], block[head], carried[head, :, where], carried_top[head, 0:1, where])
        context[head * HEAD : (head + 1) * HEAD, :] = (running[:HEAD] / running[HEAD : HEAD + 1]).astype(BF16)
    whole = context[...]
    share[...] = sum(dot(part, whole) for part in split3(folded[...]))


def closing(side, queries, block, state, folded):
    heads, _, length = queries[side].shape
    return pl.pallas_call(
        functools.partial(closing_kernel, side),
        out_shape=(
            jax.ShapeDtypeStruct((heads * HEAD, length), BF16),
            jax.ShapeDtypeStruct((folded.shape[0], length), F32),
        ),
        in_specs=[VMEM] * 5,
        out_specs=(VMEM, VMEM),
        compiler_params=PARAMS,
        name="closing",
    )(queries[side], block, *state, folded)


def turned(values, step):
    return pltpu.roll(values, step % values.shape[1], 1)


def three_columns(values, cols):
    cells = values.shape[1]
    column = lax.rem(lax.broadcasted_iota(jnp.int32, (1, cells), 1), cols)
    wide = values.astype(F32)
    left = jnp.where(column == 0, 0.0, turned(wide, 1)).astype(BF16)
    right = jnp.where(column == cols - 1, 0.0, turned(wide, -1)).astype(BF16)
    return jnp.concatenate([left, values.astype(BF16), right], axis=0)


def three_rows(weights, columns, cols):
    cells = columns.shape[1] - 2 * cols
    return sum(dot(weights[a], columns[:, a * cols : a * cols + cells]) for a in range(3))


def network_kernel(
    cols, frame_rows, place, chip_map, near, far, forward, backward, head, own_context, their_context, holo, sums,
    gradient, hidden, pre_one, pre_two, grads,
):
    core, half, row_at = place[0], place[1], place[2]
    own = chip_map.shape[1]
    cells = hidden.shape[1]
    rim = (cells - own) // 2
    row_count = cells // cols
    above = rim // cols
    first_row = row_at - above
    piece = own // 2
    down = (core == place[3]).astype(jnp.int32)
    for source, base, lead in ((chip_map, own, core), (near, 2 * own * down, core), (far, 2 * own * (1 - down), 1 - core)):
        for side in range(2):
            start = pl.multiple_of(base + lax.rem(lead + side, 2) * piece, 128)
            hidden[:, pl.ds(start, piece)] = source[:, side * piece : (side + 1) * piece]

    def inside(start_row, rows):
        lane = lax.broadcasted_iota(jnp.int32, (1, rows * cols), 1)
        frame_lane = lane + (first_row + start_row) * cols
        return jnp.logical_and(frame_lane >= 0, frame_lane < frame_rows * cols)

    channels, outputs = forward.shape[2], head.shape[0]
    columns_zero = three_columns(jnp.where(inside(0, row_count), hidden[:channels, :].astype(F32), 0.0), cols)
    first = three_rows(forward[0], columns_zero, cols)
    rows_one = row_count - 2
    one = jnp.where(inside(1, rows_one), first * jax.nn.sigmoid(first), 0.0)
    columns_one = three_columns(one, cols)
    second = three_rows(forward[1], columns_one, cols)
    rows_two = row_count - 4
    sigmoid_two = jax.nn.sigmoid(second)
    two = (second * sigmoid_two).astype(BF16)
    holo[...] = dot(head[...], two[:, rim - 2 * cols : rim - 2 * cols + own])
    pieces = hidden[channels:, 2 * cols : cells - 2 * cols].astype(F32)
    cotangent = pieces[:outputs] + pieces[outputs : 2 * outputs] + pieces[2 * outputs : 3 * outputs]
    grad_two = lax.dot_general(
        head[...].astype(F32), cotangent, TN, precision=lax.Precision.HIGHEST, preferred_element_type=F32
    ).astype(BF16)
    slope = grad_two.astype(F32) * sigmoid_two * (1.0 + second * (1.0 - sigmoid_two))
    pre_grad_two = jnp.where(inside(2, rows_two), slope, 0.0)
    grad_one = three_rows(backward[1], three_columns(pre_grad_two, cols), cols).astype(BF16)
    rows_grad = row_count - 6
    middle = first[:, 2 * cols : 2 * cols + rows_grad * cols]
    sigmoid_one = jax.nn.sigmoid(middle)
    slope = grad_one.astype(F32) * sigmoid_one * (1.0 + middle * (1.0 - sigmoid_one))
    pre_grad_one = jnp.where(inside(3, rows_grad), slope, 0.0)
    grad_zero = three_rows(backward[0], three_columns(pre_grad_one, cols), cols).astype(BF16)
    pre_one[...] = pre_grad_one[:, rim - 3 * cols : rim - 3 * cols + own].astype(BF16)
    pre_two[...] = pre_grad_two[:, rim - 2 * cols : rim - 2 * cols + own].astype(BF16)

    share = sums.shape[0]
    taps = 9 * channels
    for layer, (pre, columns, offset) in enumerate(((pre_one, columns_zero, rim), (pre_two, columns_one, rim - cols))):

        @pl.when(core == layer)
        def _(pre=pre, columns=columns, offset=offset):
            stacked = jnp.concatenate(
                [columns[:, offset + (a - 1) * cols : offset + (a - 1) * cols + own] for a in range(3)], axis=0
            )
            rows = pre[pl.ds(pl.multiple_of(half * share, 16), share), :]
            sums[:, :taps] = lax.dot_general(rows, stacked, NT, preferred_element_type=F32)

    grads[...] = grad_zero
    gradient[...] = sum(
        lax.dot_general(
            grads[:, pl.ds(pl.multiple_of(at * piece, 128), piece)], seen[...], NT, preferred_element_type=F32
        )
        for at, seen in ((core, own_context), (1 - core, their_context))
    )


def network(place, maps, forward, backward, head, own_context, their_context, cols, frame_rows, col_count):
    own = maps[0].shape[1]
    channels = forward.shape[2]
    return pl.pallas_call(
        functools.partial(network_kernel, cols, frame_rows),
        out_shape=(
            jax.ShapeDtypeStruct((head.shape[0], own), F32),
            jax.ShapeDtypeStruct((channels // col_count, 9 * channels), F32),
            jax.ShapeDtypeStruct((channels, own_context.shape[0]), F32),
        ),
        in_specs=[SMEM] + [VMEM] * 8,
        out_specs=(VMEM,) * 3,
        scratch_shapes=[pltpu.VMEM((maps[0].shape[0], 3 * own), BF16)] + [pltpu.VMEM((channels, own), BF16)] * 3,
        compiler_params=PARAMS,
        name="network",
    )(place, *maps, forward, backward, head, own_context, their_context)


def swapped(values, axis):
    size = lax.axis_size(axis)
    return lax.ppermute(values, axis, [(i, i ^ 1) for i in range(size)])


def passed(values, axis, step, wrap):
    size = lax.axis_size(axis)
    pairs = [(i, (i + step) % size) for i in range(size) if wrap or 0 <= i + step < size]
    return lax.ppermute(values, axis, pairs)


def beside(values):
    size, cols = lax.axis_size("tok"), lax.axis_size("col")
    pairs = []
    for at in range(size // 2):
        for core, other in ((0, at ^ 1), (1, ((at + 1) ^ 1) - 1)):
            inside = 0 <= other < size // 2
            for col in range(cols):
                target = (other if inside else at, col if inside or cols == 1 else col ^ 1)
                pairs.append(((2 * at + core) * cols + col, (2 * target[0] + core) * cols + target[1]))
    return lax.ppermute(values, ("tok", "col"), pairs)


def round_ring(values):
    size = lax.axis_size("tok")
    chips = size // 2
    order = [at for at in range(chips) if at == 0 or at % 2 == 1] + [
        at for at in reversed(range(chips)) if at and at % 2 == 0
    ]
    following = {order[at]: order[(at + 1) % chips] for at in range(chips)}
    return lax.ppermute(values, "tok", [(i, 2 * following[i // 2] + i % 2) for i in range(size)])


def everyone(values, axis, stride, count):
    sent = values.astype(BF16)
    terms = [(passed(sent, axis, stride * step, True) if step else sent).astype(F32) for step in range(count)]
    while len(terms) > 1:
        apart = len(terms) // 2
        terms = [terms[at] + terms[at + apart] for at in range(apart)]
    return terms[0]


def in_order(core, mine, theirs, axis):
    return jnp.where(
        core == 0, jnp.concatenate([mine, theirs], axis=axis), jnp.concatenate([theirs, mine], axis=axis)
    )


def step(
    tokens, ln_gain, qkv_weight, out_weight, readout_weight, conv_weight, head_weight, holo_cot
):
    frame_rows = tokens[0]
    cotangent = holo_cot[0]
    rows_dev, cols_dev = cotangent.shape[1:]
    tok_count, col_count, dp_count = (lax.axis_size(axis) for axis in ("tok", "col", "dp"))
    chips = tok_count // 2
    tok_at, half = lax.axis_index("tok"), lax.axis_index("col")
    core = lax.rem(tok_at, 2)
    chip_row = (tok_at - core) * rows_dev
    place = jnp.stack([core, half, chip_row, lax.rem(tok_at // 2, 2)]).astype(jnp.int32)
    layers, channels = conv_weight.shape[:2]
    cols = cols_dev * col_count

    normed = normalize(frame_rows, ln_gain.astype(F32).reshape(1, -1))
    own_keyed, their_keyed = project((1, 2), place, normed, qkv_weight)
    own_keyed, their_keyed, normed = lax.optimization_barrier((own_keyed, their_keyed, normed))
    got_keyed = swapped(their_keyed, "tok")
    own_queries, their_queries = project((0,), place, normed, qkv_weight)
    queries = (own_queries, swapped(their_queries, "tok"))
    kept = own_keyed.shape[0] * HEAD

    def prepare(conv_weight, out_weight, readout_weight, frame_rows, cotangent):
        taps = conv_weight.reshape(layers, channels, 3, 3, channels)
        forward = jnp.transpose(taps.reshape(layers, channels, 3, 3 * channels), (0, 2, 1, 3))
        backward = jnp.transpose(taps[:, :, ::-1, ::-1, :], (0, 2, 4, 3, 1)).reshape(
            layers, 3, channels, 3 * channels
        )
        own_out = lax.dynamic_slice_in_dim(out_weight, core * kept, kept, 0)
        folded = lax.dot_general(readout_weight, own_out, (((0,), (1,)), ((), ())), preferred_element_type=F32)
        direct = lax.dot_general(readout_weight, frame_rows, (((0,), (1,)), ((), ())), preferred_element_type=F32)
        wide_cot = in_order(half, cotangent, swapped(cotangent, "col"), 2)
        exact_cot = jnp.concatenate(split3(wide_cot.reshape(wide_cot.shape[0], -1)), axis=0)
        exact_cot = jnp.pad(exact_cot, ((0, -exact_cot.shape[0] % 16), (0, 0)))
        return (forward, backward, folded, direct, exact_cot)

    state, blocks = None, [own_keyed, got_keyed]
    for turn in range(chips):
        arriving = []
        if turn < chips - 1:
            for block in blocks:
                arriving.append(round_ring(block))
        for at, block in enumerate(blocks):
            if turn == chips - 1 and at == 1:
                break
            state = absorb(queries, block, state)
            if at == 0 and turn == min(1, chips - 2):
                state, given = lax.optimization_barrier(
                    (state, (conv_weight, out_weight, readout_weight, frame_rows, cotangent))
                )
                prepared = prepare(*given)
            if at == 0 and turn == chips - 2:
                state, prepared = lax.optimization_barrier((state, prepared))
            if turn < chips - 2:
                arriving[at], state = lax.optimization_barrier((arriving[at], state))
        blocks = arriving if turn < chips - 1 else blocks
    forward, backward, folded, direct, exact_cot = prepared

    their_context, their_share = closing(1, queries, blocks[1], state, folded)
    own_context, own_share = closing(0, queries, blocks[1], state, folded)
    partial = own_share + swapped(their_share, "tok")
    partial = (partial + jnp.where(half == 0, direct, 0.0)).astype(BF16)
    own_map = (partial.astype(F32) + swapped(partial, "col").astype(F32)).astype(BF16)
    own_map = jnp.concatenate([own_map, exact_cot], axis=0)
    chip_map = jnp.concatenate([own_map, swapped(own_map, "tok")], axis=1)
    near = beside(chip_map)
    rows_chip = 2 * rows_dev
    maps = (chip_map, near, swapped(near, "tok"))
    holo, sums, gradient = network(
        place, maps, forward, backward, head_weight, own_context, their_context, cols, tok_count * rows_dev, col_count
    )
    holo = holo.reshape(-1, rows_chip, cols)
    hologram = lax.dynamic_slice(
        holo, (0, core * rows_dev, half * cols_dev), (holo.shape[0], rows_dev, cols_dev)
    )

    taps_wide = sums.shape[1]
    lanes = 128 * ((taps_wide + 127) // 128)
    rows = sums.shape[0]
    pieces = gradient.shape[0] // rows
    folded_gradient = [gradient[at * rows : (at + 1) * rows] for at in range(pieces)]
    sent = jnp.concatenate([jnp.pad(sums, ((0, 0), (0, lanes - taps_wide))), *folded_gradient], axis=1)
    summed = everyone(sent, "dp", 1, dp_count)
    total = everyone(summed, "tok", 2, chips)
    own_grad = total[:, :taps_wide]
    col_grad = swapped(own_grad, "col")
    wide = gradient.shape[1]
    own_small = jnp.concatenate(
        [total[:, lanes + at * wide : lanes + (at + 1) * wide] for at in range(pieces)], axis=0
    )
    small = in_order(core, own_small, swapped(own_small, "tok"), 1)
    out_grad = lax.dot_general(
        small, readout_weight.astype(F32), (((0,), (1,)), ((), ())), precision=lax.Precision.HIGHEST
    )
    core_grad = swapped(own_grad, "tok")
    col_grad, out_grad, core_grad = lax.optimization_barrier((col_grad, out_grad, core_grad))
    far_grad = swapped(col_grad, "tok")
    layer_grad = in_order(half, own_grad, col_grad, 0)
    other_grad = in_order(half, core_grad, far_grad, 0)
    conv_grad = in_order(core, layer_grad[None], other_grad[None], 0)
    return (hologram[None], conv_grad, out_grad)


def solution(mesh):
    in_specs = (
        P("dp", "tok", None),
        P(),
        P(None, None, "col"),
        P("col", None),
        P(),
        P(),
        P(),
        P("dp", None, "tok", "col"),
    )
    out_specs = (P("dp", None, "tok", "col"), P(), P("col", None))
    return jax.shard_map(step, mesh=mesh, in_specs=in_specs, out_specs=out_specs, check_vma=False)
```

```python
import functools

import jax
import jax.numpy as jnp
from jax import lax
from jax.experimental import pallas as pl
from jax.experimental.pallas import tpu as pltpu
from jax.sharding import PartitionSpec as P


HEAD = 64
EPSILON = 1e-05
BF16 = jnp.bfloat16
F32 = jnp.float32
VMEM = pl.BlockSpec(memory_space=pltpu.VMEM)
SMEM = pl.BlockSpec(memory_space=pltpu.SMEM)
PARAMS = pltpu.CompilerParams(vmem_limit_bytes=16 * 2**20)
NT = (((1,), (1,)), ((), ()))
TN = (((0,), (0,)), ((), ()))


def dot(a, b):
    return jnp.dot(a, b, preferred_element_type=F32)


def split3(values):
    high = values.astype(BF16)
    rest = values - high.astype(F32)
    mid = rest.astype(BF16)
    low = (rest - mid.astype(F32)).astype(BF16)
    return high, mid, low


def normalize_kernel(tokens, gain, normed):
    values = tokens[...].astype(F32)
    center = values - jnp.mean(values, axis=-1, keepdims=True)
    spread = jnp.mean(center * center, axis=-1, keepdims=True)
    normed[...] = (center * lax.rsqrt(spread + EPSILON) * gain[...]).astype(BF16)


def normalize(tokens, gain):
    return pl.pallas_call(
        normalize_kernel,
        out_shape=jax.ShapeDtypeStruct(tokens.shape, BF16),
        in_specs=[VMEM, VMEM],
        out_specs=VMEM,
        compiler_params=PARAMS,
        name="normalize",
    )(tokens, gain)


def project_kernel(members, place, normed, weight, mine, theirs, turned):
    core = place[0]
    kept = mine.shape[0] * HEAD
    rows = normed[...]
    for at, member in enumerate(members):
        product = dot(rows, weight[member]).astype(BF16)
        if member == 0:
            product = product * jnp.asarray(1.0 / HEAD**0.5, BF16)
        turned[at] = product.T
        for which, out in ((1 - core, theirs), (core, mine)):
            for head in range(mine.shape[0]):
                start = pl.multiple_of(which * kept + head * HEAD, HEAD)
                out[head, at * HEAD : (at + 1) * HEAD, :] = turned[at, pl.ds(start, HEAD), :]


def project(members, place, normed, weight):
    count, length = weight.shape[2] // HEAD // 2, normed.shape[0]
    shape = jax.ShapeDtypeStruct((count, len(members) * HEAD, length), BF16)
    return pl.pallas_call(
        functools.partial(project_kernel, members),
        out_shape=(shape, shape),
        in_specs=[SMEM, VMEM, VMEM],
        out_specs=(VMEM,) * 2,
        scratch_shapes=[pltpu.VMEM((len(members), weight.shape[2], length), BF16)],
        compiler_params=PARAMS,
        name="project",
    )(place, normed, weight)


def attend(queries, block, running, best):
    length = block.shape[1]
    keys = block[:HEAD].T
    values = jnp.concatenate([block[HEAD:], jnp.ones((16, length), BF16)], axis=0)
    depth = min(512, length)
    for below in range(0, length, depth):
        scores = dot(keys[below : below + depth], queries)
        raised_top = jnp.max(scores, axis=0, keepdims=True)
        if best is not None:
            raised_top = jnp.maximum(best, raised_top)
        weights = jnp.exp(scores - raised_top).astype(BF16)
        added = dot(values[:, below : below + depth], weights)
        running = added if best is None else running * jnp.exp(best - raised_top) + added
        best = raised_top
    return running, best


def absorb_kernel(first, own, got, block, *refs):
    carried, carried_top = (None, None) if first else refs[:2]
    out, top = refs[-2:]
    length = own.shape[2]
    for head in range(own.shape[0]):
        for side, queries in enumerate((own, got)):
            where = slice(side * length, (side + 1) * length)
            running = None if first else carried[head, :, where]
            best = None if first else carried_top[head, 0:1, where]
            running, best = attend(queries[head], block[head], running, best)
            out[head, :, where] = running
            top[head, :, where] = jnp.broadcast_to(best, (8, length))


def absorb(queries, block, state):
    heads, _, length = queries[0].shape
    shapes = tuple(jax.ShapeDtypeStruct((heads, rows, 2 * length), F32) for rows in (HEAD + 16, 8))
    first = state is None
    return pl.pallas_call(
        functools.partial(absorb_kernel, first),
        out_shape=shapes,
        in_specs=[VMEM] * (3 if first else 5),
        out_specs=(VMEM, VMEM),
        input_output_aliases={} if first else {3: 0, 4: 1},
        compiler_params=PARAMS,
        name="absorb",
    )(*queries, block, *(() if first else state))


def closing_kernel(side, queries, block, carried, carried_top, folded, context, share):
    length = context.shape[1]
    where = slice(side * length, (side + 1) * length)
    for head in range(queries.shape[0]):
        running, _ = attend(queries[head], block[head], carried[head, :, where], carried_top[head, 0:1, where])
        context[head * HEAD : (head + 1) * HEAD, :] = (running[:HEAD] / running[HEAD : HEAD + 1]).astype(BF16)
    whole = context[...]
    share[...] = sum(dot(part, whole) for part in split3(folded[...]))


def closing(side, queries, block, state, folded):
    heads, _, length = queries[side].shape
    return pl.pallas_call(
        functools.partial(closing_kernel, side),
        out_shape=(
            jax.ShapeDtypeStruct((heads * HEAD, length), BF16),
            jax.ShapeDtypeStruct((folded.shape[0], length), F32),
        ),
        in_specs=[VMEM] * 5,
        out_specs=(VMEM, VMEM),
        compiler_params=PARAMS,
        name="closing",
    )(queries[side], block, *state, folded)


def arrange_kernel(weight, forward, backward):
    channels = weight.shape[1]
    for layer in range(weight.shape[0]):
        taps = weight[layer]
        turned_taps = taps.astype(F32).T
        for row in range(3):
            forward[layer, row] = taps[:, row * 3 * channels : (row + 1) * 3 * channels]
            at = [((2 - row) * 3 + 2 - column) * channels for column in range(3)]
            backward[layer, row] = jnp.concatenate(
                [turned_taps[start : start + channels, :] for start in at], axis=1
            ).astype(BF16)


def arrange(weight):
    layers, channels, wide = weight.shape
    shape = jax.ShapeDtypeStruct((layers, 3, channels, wide // 3), BF16)
    return pl.pallas_call(
        arrange_kernel,
        out_shape=(shape, shape),
        in_specs=[VMEM],
        out_specs=(VMEM, VMEM),
        compiler_params=PARAMS,
        name="arrange",
    )(weight)


def turned(values, step):
    return pltpu.roll(values, step % values.shape[1], 1)


def three_columns(values, cols):
    cells = values.shape[1]
    column = lax.rem(lax.broadcasted_iota(jnp.int32, (1, cells), 1), cols)
    wide = values.astype(F32)
    left = jnp.where(column == 0, 0.0, turned(wide, 1)).astype(BF16)
    right = jnp.where(column == cols - 1, 0.0, turned(wide, -1)).astype(BF16)
    return jnp.concatenate([left, values.astype(BF16), right], axis=0)


def three_rows(weights, columns, cols):
    cells = columns.shape[1] - 2 * cols
    return sum(dot(weights[a], columns[:, a * cols : a * cols + cells]) for a in range(3))


def network_kernel(
    cols, frame_rows, place, chip_map, near, far, forward, backward, head, own_context, their_context, holo, sums,
    gradient, hidden, pre_one, pre_two, grads,
):
    core, half, row_at = place[0], place[1], place[2]
    own = chip_map.shape[1]
    cells = hidden.shape[1]
    rim = (cells - own) // 2
    row_count = cells // cols
    above = rim // cols
    first_row = row_at - above
    piece = own // 2
    down = (core == place[3]).astype(jnp.int32)
    for source, base, lead in ((chip_map, own, core), (near, 2 * own * down, core), (far, 2 * own * (1 - down), 1 - core)):
        for side in range(2):
            start = pl.multiple_of(base + lax.rem(lead + side, 2) * piece, 128)
            hidden[:, pl.ds(start, piece)] = source[:, side * piece : (side + 1) * piece]

    def inside(start_row, rows):
        lane = lax.broadcasted_iota(jnp.int32, (1, rows * cols), 1)
        frame_lane = lane + (first_row + start_row) * cols
        return jnp.logical_and(frame_lane >= 0, frame_lane < frame_rows * cols)

    channels, outputs = forward.shape[2], head.shape[0]
    columns_zero = three_columns(jnp.where(inside(0, row_count), hidden[:channels, :].astype(F32), 0.0), cols)
    first = three_rows(forward[0], columns_zero, cols)
    rows_one = row_count - 2
    one = jnp.where(inside(1, rows_one), first * jax.nn.sigmoid(first), 0.0)
    columns_one = three_columns(one, cols)
    second = three_rows(forward[1], columns_one, cols)
    rows_two = row_count - 4
    sigmoid_two = jax.nn.sigmoid(second)
    two = (second * sigmoid_two).astype(BF16)
    holo[...] = dot(head[...], two[:, rim - 2 * cols : rim - 2 * cols + own])
    pieces = hidden[channels:, 2 * cols : cells - 2 * cols].astype(F32)
    cotangent = pieces[:outputs] + pieces[outputs : 2 * outputs] + pieces[2 * outputs : 3 * outputs]
    grad_two = lax.dot_general(
        head[...].astype(F32), cotangent, TN, precision=lax.Precision.HIGHEST, preferred_element_type=F32
    ).astype(BF16)
    slope = grad_two.astype(F32) * sigmoid_two * (1.0 + second * (1.0 - sigmoid_two))
    pre_grad_two = jnp.where(inside(2, rows_two), slope, 0.0)
    grad_one = three_rows(backward[1], three_columns(pre_grad_two, cols), cols).astype(BF16)
    rows_grad = row_count - 6
    middle = first[:, 2 * cols : 2 * cols + rows_grad * cols]
    sigmoid_one = jax.nn.sigmoid(middle)
    slope = grad_one.astype(F32) * sigmoid_one * (1.0 + middle * (1.0 - sigmoid_one))
    pre_grad_one = jnp.where(inside(3, rows_grad), slope, 0.0)
    grad_zero = three_rows(backward[0], three_columns(pre_grad_one, cols), cols).astype(BF16)
    pre_one[...] = pre_grad_one[:, rim - 3 * cols : rim - 3 * cols + own].astype(BF16)
    pre_two[...] = pre_grad_two[:, rim - 2 * cols : rim - 2 * cols + own].astype(BF16)

    share = sums.shape[0]
    taps = 9 * channels
    for layer, (pre, columns, offset) in enumerate(((pre_one, columns_zero, rim), (pre_two, columns_one, rim - cols))):

        @pl.when(core == layer)
        def _(pre=pre, columns=columns, offset=offset):
            stacked = jnp.concatenate(
                [columns[:, offset + (a - 1) * cols : offset + (a - 1) * cols + own] for a in range(3)], axis=0
            )
            rows = pre[pl.ds(pl.multiple_of(half * share, 16), share), :]
            sums[:, :taps] = lax.dot_general(rows, stacked, NT, preferred_element_type=F32)

    grads[...] = grad_zero
    gradient[...] = sum(
        lax.dot_general(
            grads[:, pl.ds(pl.multiple_of(at * piece, 128), piece)], seen[...], NT, preferred_element_type=F32
        )
        for at, seen in ((core, own_context), (1 - core, their_context))
    )


def network(place, maps, forward, backward, head, own_context, their_context, cols, frame_rows, col_count):
    own = maps[0].shape[1]
    channels = forward.shape[2]
    return pl.pallas_call(
        functools.partial(network_kernel, cols, frame_rows),
        out_shape=(
            jax.ShapeDtypeStruct((head.shape[0], own), F32),
            jax.ShapeDtypeStruct((channels // col_count, 9 * channels), F32),
            jax.ShapeDtypeStruct((channels, own_context.shape[0]), F32),
        ),
        in_specs=[SMEM] + [VMEM] * 8,
        out_specs=(VMEM,) * 3,
        scratch_shapes=[pltpu.VMEM((maps[0].shape[0], 3 * own), BF16)] + [pltpu.VMEM((channels, own), BF16)] * 3,
        compiler_params=PARAMS,
        name="network",
    )(place, *maps, forward, backward, head, own_context, their_context)


def swapped(values, axis):
    size = lax.axis_size(axis)
    return lax.ppermute(values, axis, [(i, i ^ 1) for i in range(size)])


def passed(values, axis, step, wrap):
    size = lax.axis_size(axis)
    pairs = [(i, (i + step) % size) for i in range(size) if wrap or 0 <= i + step < size]
    return lax.ppermute(values, axis, pairs)


def beside(values):
    size, cols = lax.axis_size("tok"), lax.axis_size("col")
    pairs = []
    for at in range(size // 2):
        for core, other in ((0, at ^ 1), (1, ((at + 1) ^ 1) - 1)):
            inside = 0 <= other < size // 2
            for col in range(cols):
                target = (other if inside else at, col if inside or cols == 1 else col ^ 1)
                pairs.append(((2 * at + core) * cols + col, (2 * target[0] + core) * cols + target[1]))
    return lax.ppermute(values, ("tok", "col"), pairs)


def round_ring(values):
    size = lax.axis_size("tok")
    chips = size // 2
    order = [at for at in range(chips) if at == 0 or at % 2 == 1] + [
        at for at in reversed(range(chips)) if at and at % 2 == 0
    ]
    following = {order[at]: order[(at + 1) % chips] for at in range(chips)}
    return lax.ppermute(values, "tok", [(i, 2 * following[i // 2] + i % 2) for i in range(size)])


def everyone(values, axis, stride, count):
    sent = values.astype(BF16)
    terms = [(passed(sent, axis, stride * step, True) if step else sent).astype(F32) for step in range(count)]
    while len(terms) > 1:
        apart = len(terms) // 2
        terms = [terms[at] + terms[at + apart] for at in range(apart)]
    return terms[0]


def in_order(core, mine, theirs, axis):
    return jnp.where(
        core == 0, jnp.concatenate([mine, theirs], axis=axis), jnp.concatenate([theirs, mine], axis=axis)
    )


def step(
    tokens, ln_gain, qkv_weight, out_weight, readout_weight, conv_weight, head_weight, holo_cot
):
    frame_rows = tokens[0]
    cotangent = holo_cot[0]
    rows_dev, cols_dev = cotangent.shape[1:]
    tok_count, col_count, dp_count = (lax.axis_size(axis) for axis in ("tok", "col", "dp"))
    chips = tok_count // 2
    tok_at, half = lax.axis_index("tok"), lax.axis_index("col")
    core = lax.rem(tok_at, 2)
    chip_row = (tok_at - core) * rows_dev
    place = jnp.stack([core, half, chip_row, lax.rem(tok_at // 2, 2)]).astype(jnp.int32)
    cols = cols_dev * col_count

    gain, qkv_weight, out_weight = lax.optimization_barrier(
        (ln_gain.astype(F32).reshape(1, -1), qkv_weight, out_weight)
    )
    normed = normalize(frame_rows, gain)
    own_keyed, their_keyed = project((1, 2), place, normed, qkv_weight)
    own_keyed, their_keyed, normed = lax.optimization_barrier((own_keyed, their_keyed, normed))
    got_keyed = swapped(their_keyed, "tok")
    own_queries, their_queries = project((0,), place, normed, qkv_weight)
    queries = (own_queries, swapped(their_queries, "tok"))
    kept = own_keyed.shape[0] * HEAD

    def prepare(conv_weight, out_weight, readout_weight, frame_rows, cotangent):
        forward, backward = arrange(conv_weight)
        own_out = lax.dynamic_slice_in_dim(out_weight, core * kept, kept, 0)
        folded = lax.dot_general(readout_weight, own_out, (((0,), (1,)), ((), ())), preferred_element_type=F32)
        direct = lax.dot_general(readout_weight, frame_rows, (((0,), (1,)), ((), ())), preferred_element_type=F32)
        wide_cot = in_order(half, cotangent, swapped(cotangent, "col"), 2)
        exact_cot = jnp.concatenate(split3(wide_cot.reshape(wide_cot.shape[0], -1)), axis=0)
        exact_cot = jnp.pad(exact_cot, ((0, -exact_cot.shape[0] % 16), (0, 0)))
        return (forward, backward, folded, direct, exact_cot)

    state, blocks = None, [own_keyed, got_keyed]
    for turn in range(chips):
        arriving = []
        if turn < chips - 1:
            for block in blocks:
                arriving.append(round_ring(block))
        for at, block in enumerate(blocks):
            if turn == chips - 1 and at == 1:
                break
            state = absorb(queries, block, state)
            if at == 1 and turn == min(1, chips - 2):
                state, given = lax.optimization_barrier(
                    (state, (conv_weight, out_weight, readout_weight, frame_rows, cotangent))
                )
                prepared = prepare(*given)
            if at == 0 and turn == chips - 1:
                state, prepared = lax.optimization_barrier((state, prepared))
            if turn < chips - 2:
                arriving[at], state = lax.optimization_barrier((arriving[at], state))
        blocks = arriving if turn < chips - 1 else blocks
    forward, backward, folded, direct, exact_cot = prepared

    their_context, their_share = closing(1, queries, blocks[1], state, folded)
    own_context, own_share = closing(0, queries, blocks[1], state, folded)
    partial = own_share + swapped(their_share, "tok")
    partial = (partial + jnp.where(half == 0, direct, 0.0)).astype(BF16)
    own_map = (partial.astype(F32) + swapped(partial, "col").astype(F32)).astype(BF16)
    own_map = jnp.concatenate([own_map, exact_cot], axis=0)
    chip_map = jnp.concatenate([own_map, swapped(own_map, "tok")], axis=1)
    near = beside(chip_map)
    rows_chip = 2 * rows_dev
    maps = (chip_map, near, swapped(near, "tok"))
    holo, sums, gradient = network(
        place, maps, forward, backward, head_weight, own_context, their_context, cols, tok_count * rows_dev, col_count
    )
    holo = holo.reshape(-1, rows_chip, cols)
    hologram = lax.dynamic_slice(
        holo, (0, core * rows_dev, half * cols_dev), (holo.shape[0], rows_dev, cols_dev)
    )

    taps_wide = sums.shape[1]
    lanes = 128 * ((taps_wide + 127) // 128)
    rows = sums.shape[0]
    pieces = gradient.shape[0] // rows
    folded_gradient = [gradient[at * rows : (at + 1) * rows] for at in range(pieces)]
    sent = jnp.concatenate([jnp.pad(sums, ((0, 0), (0, lanes - taps_wide))), *folded_gradient], axis=1)
    summed = everyone(sent, "dp", 1, dp_count)
    total = everyone(summed, "tok", 2, chips)
    own_grad = total[:, :taps_wide]
    col_grad = swapped(own_grad, "col")
    wide = gradient.shape[1]
    own_small = jnp.concatenate(
        [total[:, lanes + at * wide : lanes + (at + 1) * wide] for at in range(pieces)], axis=0
    )
    small = in_order(core, own_small, swapped(own_small, "tok"), 1)
    out_grad = lax.dot_general(
        small, readout_weight.astype(F32), (((0,), (1,)), ((), ())), precision=lax.Precision.HIGHEST
    )
    core_grad = swapped(own_grad, "tok")
    col_grad, out_grad, core_grad = lax.optimization_barrier((col_grad, out_grad, core_grad))
    far_grad = swapped(col_grad, "tok")
    layer_grad = in_order(half, own_grad, col_grad, 0)
    other_grad = in_order(half, core_grad, far_grad, 0)
    conv_grad = in_order(core, layer_grad[None], other_grad[None], 0)
    return (hologram[None], conv_grad, out_grad)


def solution(mesh):
    in_specs = (
        P("dp", "tok", None),
        P(),
        P(None, None, "col"),
        P("col", None),
        P(),
        P(),
        P(),
        P("dp", None, "tok", "col"),
    )
    out_specs = (P("dp", None, "tok", "col"), P(), P("col", None))
    return jax.shard_map(step, mesh=mesh, in_specs=in_specs, out_specs=out_specs, check_vma=False)
```

```python
import functools

import jax
import jax.numpy as jnp
from jax import lax
from jax.experimental import pallas as pl
from jax.experimental.pallas import tpu as pltpu
from jax.sharding import PartitionSpec as P


HEAD = 64
EPSILON = 1e-05
BF16 = jnp.bfloat16
F32 = jnp.float32
VMEM = pl.BlockSpec(memory_space=pltpu.VMEM)
SMEM = pl.BlockSpec(memory_space=pltpu.SMEM)
PARAMS = pltpu.CompilerParams(vmem_limit_bytes=16 * 2**20)
NT = (((1,), (1,)), ((), ()))


def dot(a, b):
    return jnp.dot(a, b, preferred_element_type=F32)


def split3(values):
    high = values.astype(BF16)
    rest = values - high.astype(F32)
    mid = rest.astype(BF16)
    low = (rest - mid.astype(F32)).astype(BF16)
    return high, mid, low


def normalize_kernel(tokens, gain, normed):
    values = tokens[...].astype(F32)
    center = values - jnp.mean(values, axis=-1, keepdims=True)
    spread = jnp.mean(center * center, axis=-1, keepdims=True)
    normed[...] = (center * lax.rsqrt(spread + EPSILON) * gain[...]).astype(BF16)


def normalize(tokens, gain):
    return pl.pallas_call(
        normalize_kernel,
        out_shape=jax.ShapeDtypeStruct(tokens.shape, BF16),
        in_specs=[VMEM, VMEM],
        out_specs=VMEM,
        compiler_params=PARAMS,
        name="normalize",
    )(tokens, gain)


def project_kernel(members, place, normed, weight, mine, theirs, turned):
    core = place[0]
    kept = mine.shape[0] * HEAD
    rows = normed[...]
    for at, member in enumerate(members):
        product = dot(rows, weight[member]).astype(BF16)
        if member == 0:
            product = product * jnp.asarray(1.0 / HEAD**0.5, BF16)
        turned[at] = product.T
        for which, out in ((1 - core, theirs), (core, mine)):
            for head in range(mine.shape[0]):
                start = pl.multiple_of(which * kept + head * HEAD, HEAD)
                out[head, at * HEAD : (at + 1) * HEAD, :] = turned[at, pl.ds(start, HEAD), :]


def project(members, place, normed, weight):
    count, length = weight.shape[2] // HEAD // 2, normed.shape[0]
    shape = jax.ShapeDtypeStruct((count, len(members) * HEAD, length), BF16)
    return pl.pallas_call(
        functools.partial(project_kernel, members),
        out_shape=(shape, shape),
        in_specs=[SMEM, VMEM, VMEM],
        out_specs=(VMEM,) * 2,
        scratch_shapes=[pltpu.VMEM((len(members), weight.shape[2], length), BF16)],
        compiler_params=PARAMS,
        name="project",
    )(place, normed, weight)


def attend(queries, block, running, best):
    length = block.shape[1]
    keys = block[:HEAD].T
    values = jnp.concatenate([block[HEAD:], jnp.ones((16, length), BF16)], axis=0)
    depth = min(512, length)
    for below in range(0, length, depth):
        scores = dot(keys[below : below + depth], queries)
        raised_top = jnp.max(scores, axis=0, keepdims=True)
        if best is not None:
            raised_top = jnp.maximum(best, raised_top)
        weights = jnp.exp(scores - raised_top).astype(BF16)
        added = dot(values[:, below : below + depth], weights)
        running = added if best is None else running * jnp.exp(best - raised_top) + added
        best = raised_top
    return running, best


def absorb_kernel(first, own, got, block, *refs):
    carried, carried_top = (None, None) if first else refs[:2]
    out, top = refs[-2:]
    length = own.shape[2]
    for head in range(own.shape[0]):
        for side, queries in enumerate((own, got)):
            where = slice(side * length, (side + 1) * length)
            running = None if first else carried[head, :, where]
            best = None if first else carried_top[head, 0:1, where]
            running, best = attend(queries[head], block[head], running, best)
            out[head, :, where] = running
            top[head, :, where] = jnp.broadcast_to(best, (8, length))


def absorb(queries, block, state):
    heads, _, length = queries[0].shape
    shapes = tuple(jax.ShapeDtypeStruct((heads, rows, 2 * length), F32) for rows in (HEAD + 16, 8))
    first = state is None
    return pl.pallas_call(
        functools.partial(absorb_kernel, first),
        out_shape=shapes,
        in_specs=[VMEM] * (3 if first else 5),
        out_specs=(VMEM, VMEM),
        input_output_aliases={} if first else {3: 0, 4: 1},
        compiler_params=PARAMS,
        name="absorb",
    )(*queries, block, *(() if first else state))


def closing_kernel(side, queries, block, carried, carried_top, folded, context, share):
    length = context.shape[1]
    where = slice(side * length, (side + 1) * length)
    for head in range(queries.shape[0]):
        running, _ = attend(queries[head], block[head], carried[head, :, where], carried_top[head, 0:1, where])
        context[head * HEAD : (head + 1) * HEAD, :] = (running[:HEAD] / running[HEAD : HEAD + 1]).astype(BF16)
    whole = context[...]
    share[...] = sum(dot(part, whole) for part in split3(folded[...]))


def closing(side, queries, block, state, folded):
    heads, _, length = queries[side].shape
    return pl.pallas_call(
        functools.partial(closing_kernel, side),
        out_shape=(
            jax.ShapeDtypeStruct((heads * HEAD, length), BF16),
            jax.ShapeDtypeStruct((folded.shape[0], length), F32),
        ),
        in_specs=[VMEM] * 5,
        out_specs=(VMEM, VMEM),
        compiler_params=PARAMS,
        name="closing",
    )(queries[side], block, *state, folded)


def arrange_kernel(weight, forward, backward):
    channels = weight.shape[1]
    for layer in range(weight.shape[0]):
        taps = weight[layer]
        turned_taps = taps.astype(F32).T
        for row in range(3):
            forward[layer, row] = taps[:, row * 3 * channels : (row + 1) * 3 * channels]
            at = [((2 - row) * 3 + 2 - column) * channels for column in range(3)]
            backward[layer, row] = jnp.concatenate(
                [turned_taps[start : start + channels, :] for start in at], axis=1
            ).astype(BF16)


def arrange(weight):
    layers, channels, wide = weight.shape
    shape = jax.ShapeDtypeStruct((layers, 3, channels, wide // 3), BF16)
    return pl.pallas_call(
        arrange_kernel,
        out_shape=(shape, shape),
        in_specs=[VMEM],
        out_specs=(VMEM, VMEM),
        compiler_params=PARAMS,
        name="arrange",
    )(weight)


def turned(values, step):
    return pltpu.roll(values, step % values.shape[1], 1)


def three_columns(values, cols):
    cells = values.shape[1]
    column = lax.rem(lax.broadcasted_iota(jnp.int32, (1, cells), 1), cols)
    wide = values.astype(F32)
    left = jnp.where(column == 0, 0.0, turned(wide, 1)).astype(BF16)
    right = jnp.where(column == cols - 1, 0.0, turned(wide, -1)).astype(BF16)
    return jnp.concatenate([left, values.astype(BF16), right], axis=0)


def three_rows(weights, columns, cols):
    cells = columns.shape[1] - 2 * cols
    return sum(dot(weights[a], columns[:, a * cols : a * cols + cells]) for a in range(3))


def network_kernel(
    cols, frame_rows, place, chip_map, near, far, forward, backward, head, own_context, their_context, holo, sums,
    gradient, hidden, pre_one, pre_two, grads,
):
    core, half, row_at = place[0], place[1], place[2]
    own = chip_map.shape[1]
    cells = hidden.shape[1]
    rim = (cells - own) // 2
    row_count = cells // cols
    above = rim // cols
    first_row = row_at - above
    piece = own // 2
    down = (core == place[3]).astype(jnp.int32)
    for source, base, lead in ((chip_map, own, core), (near, 2 * own * down, core), (far, 2 * own * (1 - down), 1 - core)):
        for side in range(2):
            start = pl.multiple_of(base + lax.rem(lead + side, 2) * piece, 128)
            hidden[:, pl.ds(start, piece)] = source[:, side * piece : (side + 1) * piece]

    def inside(start_row, rows):
        lane = lax.broadcasted_iota(jnp.int32, (1, rows * cols), 1)
        frame_lane = lane + (first_row + start_row) * cols
        return jnp.logical_and(frame_lane >= 0, frame_lane < frame_rows * cols)

    channels, outputs = forward.shape[2], head.shape[0]
    columns_zero = three_columns(jnp.where(inside(0, row_count), hidden[:channels, :].astype(F32), 0.0), cols)
    first = three_rows(forward[0], columns_zero, cols)
    rows_one = row_count - 2
    sigmoid_first = jax.nn.sigmoid(first)
    one = jnp.where(inside(1, rows_one), first * sigmoid_first, 0.0)
    columns_one = three_columns(one, cols)
    second = three_rows(forward[1], columns_one, cols)
    rows_two = row_count - 4
    sigmoid_two = jax.nn.sigmoid(second)
    two = (second * sigmoid_two).astype(BF16)
    holo[...] = dot(head[...], two[:, rim - 2 * cols : rim - 2 * cols + own])
    pieces = hidden[channels:, 2 * cols : cells - 2 * cols].astype(F32)
    cotangent = pieces[:outputs] + pieces[outputs : 2 * outputs] + pieces[2 * outputs : 3 * outputs]
    wide_head = head[...].astype(F32).T
    grad_two = sum(wide_head[:, at : at + 1] * cotangent[at : at + 1, :] for at in range(outputs)).astype(BF16)
    slope = grad_two.astype(F32) * sigmoid_two * (1.0 + second * (1.0 - sigmoid_two))
    pre_grad_two = jnp.where(inside(2, rows_two), slope, 0.0)
    grad_one = three_rows(backward[1], three_columns(pre_grad_two, cols), cols).astype(BF16)
    rows_grad = row_count - 6
    middle = first[:, 2 * cols : 2 * cols + rows_grad * cols]
    sigmoid_one = sigmoid_first[:, 2 * cols : 2 * cols + rows_grad * cols]
    slope = grad_one.astype(F32) * sigmoid_one * (1.0 + middle * (1.0 - sigmoid_one))
    pre_grad_one = jnp.where(inside(3, rows_grad), slope, 0.0)
    grad_zero = three_rows(backward[0], three_columns(pre_grad_one, cols), cols).astype(BF16)
    pre_one[...] = pre_grad_one[:, rim - 3 * cols : rim - 3 * cols + own].astype(BF16)
    pre_two[...] = pre_grad_two[:, rim - 2 * cols : rim - 2 * cols + own].astype(BF16)

    share = sums.shape[0]
    taps = 9 * channels
    for layer, (pre, columns, offset) in enumerate(((pre_one, columns_zero, rim), (pre_two, columns_one, rim - cols))):

        @pl.when(core == layer)
        def _(pre=pre, columns=columns, offset=offset):
            stacked = jnp.concatenate(
                [columns[:, offset + (a - 1) * cols : offset + (a - 1) * cols + own] for a in range(3)], axis=0
            )
            rows = pre[pl.ds(pl.multiple_of(half * share, 16), share), :]
            sums[:, :taps] = lax.dot_general(rows, stacked, NT, preferred_element_type=F32)

    grads[...] = grad_zero
    gradient[...] = sum(
        lax.dot_general(
            grads[:, pl.ds(pl.multiple_of(at * piece, 128), piece)], seen[...], NT, preferred_element_type=F32
        )
        for at, seen in ((core, own_context), (1 - core, their_context))
    )


def network(place, maps, forward, backward, head, own_context, their_context, cols, frame_rows, col_count):
    own = maps[0].shape[1]
    channels = forward.shape[2]
    return pl.pallas_call(
        functools.partial(network_kernel, cols, frame_rows),
        out_shape=(
            jax.ShapeDtypeStruct((head.shape[0], own), F32),
            jax.ShapeDtypeStruct((channels // col_count, 9 * channels), F32),
            jax.ShapeDtypeStruct((channels, own_context.shape[0]), F32),
        ),
        in_specs=[SMEM] + [VMEM] * 8,
        out_specs=(VMEM,) * 3,
        scratch_shapes=[pltpu.VMEM((maps[0].shape[0], 3 * own), BF16)] + [pltpu.VMEM((channels, own), BF16)] * 3,
        compiler_params=PARAMS,
        name="network",
    )(place, *maps, forward, backward, head, own_context, their_context)


def swapped(values, axis):
    size = lax.axis_size(axis)
    return lax.ppermute(values, axis, [(i, i ^ 1) for i in range(size)])


def passed(values, axis, step, wrap):
    size = lax.axis_size(axis)
    pairs = [(i, (i + step) % size) for i in range(size) if wrap or 0 <= i + step < size]
    return lax.ppermute(values, axis, pairs)


def beside(values):
    size, cols = lax.axis_size("tok"), lax.axis_size("col")
    pairs = []
    for at in range(size // 2):
        for core, other in ((0, at ^ 1), (1, ((at + 1) ^ 1) - 1)):
            inside = 0 <= other < size // 2
            for col in range(cols):
                target = (other if inside else at, col if inside or cols == 1 else col ^ 1)
                pairs.append(((2 * at + core) * cols + col, (2 * target[0] + core) * cols + target[1]))
    return lax.ppermute(values, ("tok", "col"), pairs)


def round_ring(values):
    size = lax.axis_size("tok")
    chips = size // 2
    order = [at for at in range(chips) if at == 0 or at % 2 == 1] + [
        at for at in reversed(range(chips)) if at and at % 2 == 0
    ]
    following = {order[at]: order[(at + 1) % chips] for at in range(chips)}
    return lax.ppermute(values, "tok", [(i, 2 * following[i // 2] + i % 2) for i in range(size)])


def everyone(values, axis, stride, count):
    sent = values.astype(BF16)
    terms = [(passed(sent, axis, stride * step, True) if step else sent).astype(F32) for step in range(count)]
    while len(terms) > 1:
        apart = len(terms) // 2
        terms = [terms[at] + terms[at + apart] for at in range(apart)]
    return terms[0]


def in_order(core, mine, theirs, axis):
    return jnp.where(
        core == 0, jnp.concatenate([mine, theirs], axis=axis), jnp.concatenate([theirs, mine], axis=axis)
    )


def step(
    tokens, ln_gain, qkv_weight, out_weight, readout_weight, conv_weight, head_weight, holo_cot
):
    frame_rows = tokens[0]
    cotangent = holo_cot[0]
    rows_dev, cols_dev = cotangent.shape[1:]
    tok_count, col_count, dp_count = (lax.axis_size(axis) for axis in ("tok", "col", "dp"))
    chips = tok_count // 2
    tok_at, half = lax.axis_index("tok"), lax.axis_index("col")
    core = lax.rem(tok_at, 2)
    chip_row = (tok_at - core) * rows_dev
    place = jnp.stack([core, half, chip_row, lax.rem(tok_at // 2, 2)]).astype(jnp.int32)
    cols = cols_dev * col_count

    gain, qkv_weight, out_weight = lax.optimization_barrier(
        (ln_gain.astype(F32).reshape(1, -1), qkv_weight, out_weight)
    )
    normed = normalize(frame_rows, gain)
    own_keyed, their_keyed = project((1, 2), place, normed, qkv_weight)
    own_keyed, their_keyed, normed = lax.optimization_barrier((own_keyed, their_keyed, normed))
    got_keyed = swapped(their_keyed, "tok")
    own_queries, their_queries = project((0,), place, normed, qkv_weight)
    queries = (own_queries, swapped(their_queries, "tok"))
    kept = own_keyed.shape[0] * HEAD

    def prepare(conv_weight, out_weight, readout_weight, frame_rows):
        forward, backward = arrange(conv_weight)
        own_out = lax.dynamic_slice_in_dim(out_weight, core * kept, kept, 0)
        folded = lax.dot_general(readout_weight, own_out, (((0,), (1,)), ((), ())), preferred_element_type=F32)
        direct = lax.dot_general(readout_weight, frame_rows, (((0,), (1,)), ((), ())), preferred_element_type=F32)
        return (forward, backward, folded, direct)

    def exact_rows(other_cot):
        wide_cot = in_order(half, cotangent, other_cot, 2)
        exact_cot = jnp.concatenate(split3(wide_cot.reshape(wide_cot.shape[0], -1)), axis=0)
        return jnp.pad(exact_cot, ((0, -exact_cot.shape[0] % 16), (0, 0)))

    state, blocks = None, [own_keyed, got_keyed]
    for turn in range(chips):
        arriving = []
        if turn < chips - 1:
            for block in blocks:
                arriving.append(round_ring(block))
        for at, block in enumerate(blocks):
            if turn == chips - 1 and at == 1:
                break
            state = absorb(queries, block, state)
            if at == 0 and turn == chips - 2:
                state, given, own_cot = lax.optimization_barrier(
                    (state, (conv_weight, out_weight, readout_weight, frame_rows), cotangent)
                )
                prepared, other_cot = prepare(*given), swapped(own_cot, "col")
            if at == 1 and turn == chips - 2:
                state, other_cot = lax.optimization_barrier((state, other_cot))
                exact_cot = exact_rows(other_cot)
            if at == 0 and turn == chips - 1:
                state, prepared, exact_cot = lax.optimization_barrier((state, prepared, exact_cot))
            if turn < chips - 2:
                arriving[at], state = lax.optimization_barrier((arriving[at], state))
        blocks = arriving if turn < chips - 1 else blocks
    forward, backward, folded, direct = prepared

    their_context, their_share = closing(1, queries, blocks[1], state, folded)
    own_context, own_share = closing(0, queries, blocks[1], state, folded)
    partial = own_share + swapped(their_share, "tok")
    partial = (partial + jnp.where(half == 0, direct, 0.0)).astype(BF16)
    own_map = (partial.astype(F32) + swapped(partial, "col").astype(F32)).astype(BF16)
    own_map = jnp.concatenate([own_map, exact_cot], axis=0)
    chip_map = jnp.concatenate([own_map, swapped(own_map, "tok")], axis=1)
    near = beside(chip_map)
    rows_chip = 2 * rows_dev
    maps = (chip_map, near, swapped(near, "tok"))
    holo, sums, gradient = network(
        place, maps, forward, backward, head_weight, own_context, their_context, cols, tok_count * rows_dev, col_count
    )
    holo = holo.reshape(-1, rows_chip, cols)
    hologram = lax.dynamic_slice(
        holo, (0, core * rows_dev, half * cols_dev), (holo.shape[0], rows_dev, cols_dev)
    )

    taps_wide = sums.shape[1]
    lanes = 128 * ((taps_wide + 127) // 128)
    rows = sums.shape[0]
    pieces = gradient.shape[0] // rows
    folded_gradient = [gradient[at * rows : (at + 1) * rows] for at in range(pieces)]
    sent = jnp.concatenate([jnp.pad(sums, ((0, 0), (0, lanes - taps_wide))), *folded_gradient], axis=1)
    summed = everyone(sent, "dp", 1, dp_count)
    total = everyone(summed, "tok", 2, chips)
    own_grad = total[:, :taps_wide]
    col_grad = swapped(own_grad, "col")
    wide = gradient.shape[1]
    own_small = jnp.concatenate(
        [total[:, lanes + at * wide : lanes + (at + 1) * wide] for at in range(pieces)], axis=0
    )
    small = in_order(core, own_small, swapped(own_small, "tok"), 1)
    out_grad = lax.dot_general(
        small, readout_weight.astype(F32), (((0,), (1,)), ((), ())), precision=lax.Precision.HIGHEST
    )
    core_grad = swapped(own_grad, "tok")
    col_grad, out_grad, core_grad = lax.optimization_barrier((col_grad, out_grad, core_grad))
    far_grad = swapped(col_grad, "tok")
    layer_grad = in_order(half, own_grad, col_grad, 0)
    other_grad = in_order(half, core_grad, far_grad, 0)
    conv_grad = in_order(core, layer_grad[None], other_grad[None], 0)
    return (hologram[None], conv_grad, out_grad)


def solution(mesh):
    in_specs = (
        P("dp", "tok", None),
        P(),
        P(None, None, "col"),
        P("col", None),
        P(),
        P(),
        P(),
        P("dp", None, "tok", "col"),
    )
    out_specs = (P("dp", None, "tok", "col"), P(), P("col", None))
    return jax.shard_map(step, mesh=mesh, in_specs=in_specs, out_specs=out_specs, check_vma=False)
```

```python
import functools

import jax
import jax.numpy as jnp
from jax import lax
from jax.experimental import pallas as pl
from jax.experimental.pallas import tpu as pltpu
from jax.sharding import PartitionSpec as P


HEAD = 64
EPSILON = 1e-05
BF16 = jnp.bfloat16
F32 = jnp.float32
VMEM = pl.BlockSpec(memory_space=pltpu.VMEM)
SMEM = pl.BlockSpec(memory_space=pltpu.SMEM)
PARAMS = pltpu.CompilerParams(vmem_limit_bytes=16 * 2**20)
NT = (((1,), (1,)), ((), ()))


def dot(a, b):
    return jnp.dot(a, b, preferred_element_type=F32)


def split3(values):
    high = values.astype(BF16)
    rest = values - high.astype(F32)
    mid = rest.astype(BF16)
    low = (rest - mid.astype(F32)).astype(BF16)
    return high, mid, low


def project_kernel(members, raw, place, rows, *refs):
    if raw:
        gain, weight, normed, mine, theirs, parts, turned, sems, taken, wide_gain, row_sems = refs
        pieces = row_sems.shape[0] - 1
        size = taken.shape[0] // pieces
        row_copies = [pltpu.make_async_copy(gain, wide_gain, row_sems.at[pieces])] + [
            pltpu.make_async_copy(
                rows.at[pl.ds(at * size, size)], taken.at[pl.ds(at * size, size)], row_sems.at[at]
            )
            for at in range(pieces)
        ]
        for copy in row_copies:
            copy.start()
    else:
        weight, mine, theirs, parts, turned, sems = refs
    copies = [
        pltpu.make_async_copy(weight.at[member], parts.at[at], sems.at[at]) for at, member in enumerate(members)
    ]
    for copy in copies:
        copy.start()
    if raw:
        row_copies[0].wait()
        for at in range(pieces):
            row_copies[at + 1].wait()
            values = taken[at * size : (at + 1) * size, :].astype(F32)
            center = values - jnp.mean(values, axis=-1, keepdims=True)
            spread = jnp.mean(center * center, axis=-1, keepdims=True)
            scaled = center * lax.rsqrt(spread + EPSILON) * wide_gain[...].astype(F32)[None, :]
            normed[at * size : (at + 1) * size, :] = scaled.astype(BF16)
        rows = normed
    core = place[0]
    kept = mine.shape[0] * HEAD
    for at, member in enumerate(members):
        copies[at].wait()
        product = dot(rows[...], parts[at]).astype(BF16)
        if member == 0:
            product = product * jnp.asarray(1.0 / HEAD**0.5, BF16)
        turned[at] = product.T
        for which, out in ((1 - core, theirs), (core, mine)):
            for head in range(mine.shape[0]):
                start = pl.multiple_of(which * kept + head * HEAD, HEAD)
                out[head, at * HEAD : (at + 1) * HEAD, :] = turned[at, pl.ds(start, HEAD), :]


def project(members, place, rows, weight, gain=None):
    length, width = rows.shape[0], weight.shape[2]
    shape = jax.ShapeDtypeStruct((width // HEAD // 2, len(members) * HEAD, length), BF16)
    raw = gain is not None
    far = pl.BlockSpec(memory_space=pltpu.HBM)
    pieces = 4 if length % 64 == 0 else 1
    return pl.pallas_call(
        functools.partial(project_kernel, members, raw),
        out_shape=((jax.ShapeDtypeStruct(rows.shape, BF16),) if raw else ()) + (shape, shape),
        in_specs=[SMEM] + ([far, far] if raw else [VMEM]) + [far],
        out_specs=(VMEM,) * (2 + raw),
        scratch_shapes=[
            pltpu.VMEM((len(members),) + weight.shape[1:], BF16),
            pltpu.VMEM((len(members), width, length), BF16),
            pltpu.SemaphoreType.DMA((len(members),)),
        ]
        + (
            [pltpu.VMEM(rows.shape, BF16), pltpu.VMEM(gain.shape, BF16), pltpu.SemaphoreType.DMA((pieces + 1,))]
            if raw
            else []
        ),
        compiler_params=PARAMS,
        name="project",
    )(place, rows, *((gain,) if raw else ()), weight)


def attend(queries, block, running, best):
    length = block.shape[1]
    keys = block[:HEAD].T
    values = jnp.concatenate([block[HEAD:], jnp.ones((16, length), BF16)], axis=0)
    depth = min(512, length)
    for below in range(0, length, depth):
        scores = dot(keys[below : below + depth], queries)
        raised_top = jnp.max(scores, axis=0, keepdims=True)
        if best is not None:
            raised_top = jnp.maximum(best, raised_top)
        weights = jnp.exp(scores - raised_top).astype(BF16)
        added = dot(values[:, below : below + depth], weights)
        running = added if best is None else running * jnp.exp(best - raised_top) + added
        best = raised_top
    return running, best


def absorb_kernel(first, own, got, block, *refs):
    carried, carried_top = (None, None) if first else refs[:2]
    out, top = refs[-2:]
    length = own.shape[2]
    for head in range(own.shape[0]):
        for side, queries in enumerate((own, got)):
            where = slice(side * length, (side + 1) * length)
            running = None if first else carried[head, :, where]
            best = None if first else carried_top[head, 0:1, where]
            running, best = attend(queries[head], block[head], running, best)
            out[head, :, where] = running
            top[head, :, where] = jnp.broadcast_to(best, (8, length))


def absorb(queries, block, state):
    heads, _, length = queries[0].shape
    shapes = tuple(jax.ShapeDtypeStruct((heads, rows, 2 * length), F32) for rows in (HEAD + 16, 8))
    first = state is None
    return pl.pallas_call(
        functools.partial(absorb_kernel, first),
        out_shape=shapes,
        in_specs=[VMEM] * (3 if first else 5),
        out_specs=(VMEM, VMEM),
        input_output_aliases={} if first else {3: 0, 4: 1},
        compiler_params=PARAMS,
        name="absorb",
    )(*queries, block, *(() if first else state))


def closing_kernel(side, queries, block, carried, carried_top, folded, context, share):
    length = context.shape[1]
    where = slice(side * length, (side + 1) * length)
    for head in range(queries.shape[0]):
        running, _ = attend(queries[head], block[head], carried[head, :, where], carried_top[head, 0:1, where])
        context[head * HEAD : (head + 1) * HEAD, :] = (running[:HEAD] / running[HEAD : HEAD + 1]).astype(BF16)
    whole = context[...]
    share[...] = sum(dot(part, whole) for part in split3(folded[...]))


def closing(side, queries, block, state, folded):
    heads, _, length = queries[side].shape
    return pl.pallas_call(
        functools.partial(closing_kernel, side),
        out_shape=(
            jax.ShapeDtypeStruct((heads * HEAD, length), BF16),
            jax.ShapeDtypeStruct((folded.shape[0], length), F32),
        ),
        in_specs=[VMEM] * 5,
        out_specs=(VMEM, VMEM),
        compiler_params=PARAMS,
        name="closing",
    )(queries[side], block, *state, folded)


def arrange_kernel(weight, forward, backward):
    channels = weight.shape[1]
    for layer in range(weight.shape[0]):
        taps = weight[layer]
        turned_taps = taps.astype(F32).T
        for row in range(3):
            forward[layer, row] = taps[:, row * 3 * channels : (row + 1) * 3 * channels]
            at = [((2 - row) * 3 + 2 - column) * channels for column in range(3)]
            backward[layer, row] = jnp.concatenate(
                [turned_taps[start : start + channels, :] for start in at], axis=1
            ).astype(BF16)


def arrange(weight):
    layers, channels, wide = weight.shape
    shape = jax.ShapeDtypeStruct((layers, 3, channels, wide // 3), BF16)
    return pl.pallas_call(
        arrange_kernel,
        out_shape=(shape, shape),
        in_specs=[VMEM],
        out_specs=(VMEM, VMEM),
        compiler_params=PARAMS,
        name="arrange",
    )(weight)


def turned(values, step):
    return pltpu.roll(values, step % values.shape[1], 1)


def three_columns(values, cols):
    cells = values.shape[1]
    column = lax.rem(lax.broadcasted_iota(jnp.int32, (1, cells), 1), cols)
    wide = values.astype(F32)
    left = jnp.where(column == 0, 0.0, turned(wide, 1)).astype(BF16)
    right = jnp.where(column == cols - 1, 0.0, turned(wide, -1)).astype(BF16)
    return jnp.concatenate([left, values.astype(BF16), right], axis=0)


def three_rows(weights, columns, cols):
    cells = columns.shape[1] - 2 * cols
    return sum(dot(weights[a], columns[:, a * cols : a * cols + cells]) for a in range(3))


def network_kernel(
    cols, frame_rows, place, chip_map, near, far, forward, backward, head, own_context, their_context, holo, sums,
    gradient, hidden, pre_one, pre_two, grads,
):
    core, half, row_at = place[0], place[1], place[2]
    own = chip_map.shape[1]
    cells = hidden.shape[1]
    rim = (cells - own) // 2
    row_count = cells // cols
    above = rim // cols
    first_row = row_at - above
    piece = own // 2
    down = (core == place[3]).astype(jnp.int32)
    for source, base, lead in ((chip_map, own, core), (near, 2 * own * down, core), (far, 2 * own * (1 - down), 1 - core)):
        for side in range(2):
            start = pl.multiple_of(base + lax.rem(lead + side, 2) * piece, 128)
            hidden[:, pl.ds(start, piece)] = source[:, side * piece : (side + 1) * piece]

    def inside(start_row, rows):
        lane = lax.broadcasted_iota(jnp.int32, (1, rows * cols), 1)
        frame_lane = lane + (first_row + start_row) * cols
        return jnp.logical_and(frame_lane >= 0, frame_lane < frame_rows * cols)

    channels, outputs = forward.shape[2], head.shape[0]
    columns_zero = three_columns(jnp.where(inside(0, row_count), hidden[:channels, :].astype(F32), 0.0), cols)
    first = three_rows(forward[0], columns_zero, cols)
    rows_one = row_count - 2
    sigmoid_first = jax.nn.sigmoid(first)
    one = jnp.where(inside(1, rows_one), first * sigmoid_first, 0.0)
    columns_one = three_columns(one, cols)
    second = three_rows(forward[1], columns_one, cols)
    rows_two = row_count - 4
    sigmoid_two = jax.nn.sigmoid(second)
    two = (second * sigmoid_two).astype(BF16)
    holo[...] = dot(head[...], two[:, rim - 2 * cols : rim - 2 * cols + own])
    pieces = hidden[channels:, 2 * cols : cells - 2 * cols].astype(F32)
    cotangent = pieces[:outputs] + pieces[outputs : 2 * outputs] + pieces[2 * outputs : 3 * outputs]
    wide_head = head[...].astype(F32).T
    grad_two = sum(wide_head[:, at : at + 1] * cotangent[at : at + 1, :] for at in range(outputs)).astype(BF16)
    slope = grad_two.astype(F32) * sigmoid_two * (1.0 + second * (1.0 - sigmoid_two))
    pre_grad_two = jnp.where(inside(2, rows_two), slope, 0.0)
    grad_one = three_rows(backward[1], three_columns(pre_grad_two, cols), cols).astype(BF16)
    rows_grad = row_count - 6
    middle = first[:, 2 * cols : 2 * cols + rows_grad * cols]
    sigmoid_one = sigmoid_first[:, 2 * cols : 2 * cols + rows_grad * cols]
    slope = grad_one.astype(F32) * sigmoid_one * (1.0 + middle * (1.0 - sigmoid_one))
    pre_grad_one = jnp.where(inside(3, rows_grad), slope, 0.0)
    grad_zero = three_rows(backward[0], three_columns(pre_grad_one, cols), cols).astype(BF16)
    pre_one[...] = pre_grad_one[:, rim - 3 * cols : rim - 3 * cols + own].astype(BF16)
    pre_two[...] = pre_grad_two[:, rim - 2 * cols : rim - 2 * cols + own].astype(BF16)

    share = sums.shape[0]
    taps = 9 * channels
    for layer, (pre, columns, offset) in enumerate(((pre_one, columns_zero, rim), (pre_two, columns_one, rim - cols))):

        @pl.when(core == layer)
        def _(pre=pre, columns=columns, offset=offset):
            stacked = jnp.concatenate(
                [columns[:, offset + (a - 1) * cols : offset + (a - 1) * cols + own] for a in range(3)], axis=0
            )
            rows = pre[pl.ds(pl.multiple_of(half * share, 16), share), :]
            sums[:, :taps] = lax.dot_general(rows, stacked, NT, preferred_element_type=F32)

    grads[...] = grad_zero
    gradient[...] = sum(
        lax.dot_general(
            grads[:, pl.ds(pl.multiple_of(at * piece, 128), piece)], seen[...], NT, preferred_element_type=F32
        )
        for at, seen in ((core, own_context), (1 - core, their_context))
    )


def network(place, maps, forward, backward, head, own_context, their_context, cols, frame_rows, col_count):
    own = maps[0].shape[1]
    channels = forward.shape[2]
    return pl.pallas_call(
        functools.partial(network_kernel, cols, frame_rows),
        out_shape=(
            jax.ShapeDtypeStruct((head.shape[0], own), F32),
            jax.ShapeDtypeStruct((channels // col_count, 9 * channels), F32),
            jax.ShapeDtypeStruct((channels, own_context.shape[0]), F32),
        ),
        in_specs=[SMEM] + [VMEM] * 8,
        out_specs=(VMEM,) * 3,
        scratch_shapes=[pltpu.VMEM((maps[0].shape[0], 3 * own), BF16)] + [pltpu.VMEM((channels, own), BF16)] * 3,
        compiler_params=PARAMS,
        name="network",
    )(place, *maps, forward, backward, head, own_context, their_context)


def swapped(values, axis):
    size = lax.axis_size(axis)
    return lax.ppermute(values, axis, [(i, i ^ 1) for i in range(size)])


def passed(values, axis, step, wrap):
    size = lax.axis_size(axis)
    pairs = [(i, (i + step) % size) for i in range(size) if wrap or 0 <= i + step < size]
    return lax.ppermute(values, axis, pairs)


def beside(values):
    size, cols = lax.axis_size("tok"), lax.axis_size("col")
    pairs = []
    for at in range(size // 2):
        for core, other in ((0, at ^ 1), (1, ((at + 1) ^ 1) - 1)):
            inside = 0 <= other < size // 2
            for col in range(cols):
                target = (other if inside else at, col if inside or cols == 1 else col ^ 1)
                pairs.append(((2 * at + core) * cols + col, (2 * target[0] + core) * cols + target[1]))
    return lax.ppermute(values, ("tok", "col"), pairs)


def round_ring(values):
    size = lax.axis_size("tok")
    chips = size // 2
    order = [at for at in range(chips) if at == 0 or at % 2 == 1] + [
        at for at in reversed(range(chips)) if at and at % 2 == 0
    ]
    following = {order[at]: order[(at + 1) % chips] for at in range(chips)}
    return lax.ppermute(values, "tok", [(i, 2 * following[i // 2] + i % 2) for i in range(size)])


def everyone(values, axis, stride, count):
    sent = values.astype(BF16)
    terms = [(passed(sent, axis, stride * step, True) if step else sent).astype(F32) for step in range(count)]
    while len(terms) > 1:
        apart = len(terms) // 2
        terms = [terms[at] + terms[at + apart] for at in range(apart)]
    return terms[0]


def in_order(core, mine, theirs, axis):
    return jnp.where(
        core == 0, jnp.concatenate([mine, theirs], axis=axis), jnp.concatenate([theirs, mine], axis=axis)
    )


def step(
    tokens, ln_gain, qkv_weight, out_weight, readout_weight, conv_weight, head_weight, holo_cot
):
    frame_rows = tokens[0]
    cotangent = holo_cot[0]
    rows_dev, cols_dev = cotangent.shape[1:]
    tok_count, col_count, dp_count = (lax.axis_size(axis) for axis in ("tok", "col", "dp"))
    chips = tok_count // 2
    tok_at, half = lax.axis_index("tok"), lax.axis_index("col")
    core = lax.rem(tok_at, 2)
    chip_row = (tok_at - core) * rows_dev
    place = jnp.stack([core, half, chip_row, lax.rem(tok_at // 2, 2)]).astype(jnp.int32)
    cols = cols_dev * col_count

    qkv_weight, far_rows, far_gain = (
        pltpu.with_memory_space_constraint(array, pltpu.HBM) for array in (qkv_weight, frame_rows, ln_gain)
    )
    normed, own_keyed, their_keyed = project((1, 2), place, far_rows, qkv_weight, far_gain)
    got_keyed = swapped(their_keyed, "tok")
    own_queries, their_queries = project((0,), place, normed, qkv_weight)
    queries = (own_queries, swapped(their_queries, "tok"))
    kept = own_keyed.shape[0] * HEAD

    def prepare(conv_weight, out_weight, readout_weight, frame_rows):
        forward, backward = arrange(conv_weight)
        own_out = lax.dynamic_slice_in_dim(out_weight, core * kept, kept, 0)
        folded = lax.dot_general(readout_weight, own_out, (((0,), (1,)), ((), ())), preferred_element_type=F32)
        direct = lax.dot_general(readout_weight, frame_rows, (((0,), (1,)), ((), ())), preferred_element_type=F32)
        return (forward, backward, folded, direct)

    def exact_rows(other_cot):
        wide_cot = in_order(half, cotangent, other_cot, 2)
        exact_cot = jnp.concatenate(split3(wide_cot.reshape(wide_cot.shape[0], -1)), axis=0)
        return jnp.pad(exact_cot, ((0, -exact_cot.shape[0] % 16), (0, 0)))

    state, blocks = None, [own_keyed, got_keyed]
    for turn in range(chips):
        arriving = []
        if turn < chips - 1:
            for block in blocks:
                arriving.append(round_ring(block))
        for at, block in enumerate(blocks):
            if turn == chips - 1 and at == 1:
                break
            state = absorb(queries, block, state)
            if at == 0 and turn == chips - 2:
                state, given, own_cot = lax.optimization_barrier(
                    (state, (conv_weight, out_weight, readout_weight, frame_rows), cotangent)
                )
                prepared, other_cot = prepare(*given), swapped(own_cot, "col")
            if at == 1 and turn == chips - 2:
                state, other_cot = lax.optimization_barrier((state, other_cot))
                exact_cot = exact_rows(other_cot)
            if at == 0 and turn == chips - 1:
                state, prepared, exact_cot = lax.optimization_barrier((state, prepared, exact_cot))
            if turn < chips - 2:
                arriving[at], state = lax.optimization_barrier((arriving[at], state))
        blocks = arriving if turn < chips - 1 else blocks
    forward, backward, folded, direct = prepared

    their_context, their_share = closing(1, queries, blocks[1], state, folded)
    own_context, own_share = closing(0, queries, blocks[1], state, folded)
    partial = own_share + swapped(their_share, "tok")
    partial = (partial + jnp.where(half == 0, direct, 0.0)).astype(BF16)
    own_map = (partial.astype(F32) + swapped(partial, "col").astype(F32)).astype(BF16)
    own_map = jnp.concatenate([own_map, exact_cot], axis=0)
    chip_map = jnp.concatenate([own_map, swapped(own_map, "tok")], axis=1)
    near = beside(chip_map)
    rows_chip = 2 * rows_dev
    maps = (chip_map, near, swapped(near, "tok"))
    holo, sums, gradient = network(
        place, maps, forward, backward, head_weight, own_context, their_context, cols, tok_count * rows_dev, col_count
    )
    holo = holo.reshape(-1, rows_chip, cols)
    hologram = lax.dynamic_slice(
        holo, (0, core * rows_dev, half * cols_dev), (holo.shape[0], rows_dev, cols_dev)
    )

    taps_wide = sums.shape[1]
    lanes = 128 * ((taps_wide + 127) // 128)
    rows = sums.shape[0]
    pieces = gradient.shape[0] // rows
    folded_gradient = [gradient[at * rows : (at + 1) * rows] for at in range(pieces)]
    sent = jnp.concatenate([jnp.pad(sums, ((0, 0), (0, lanes - taps_wide))), *folded_gradient], axis=1)
    summed = everyone(sent, "dp", 1, dp_count)
    total = everyone(summed, "tok", 2, chips)
    own_grad = total[:, :taps_wide]
    col_grad = swapped(own_grad, "col")
    wide = gradient.shape[1]
    own_small = jnp.concatenate(
        [total[:, lanes + at * wide : lanes + (at + 1) * wide] for at in range(pieces)], axis=0
    )
    small = in_order(core, own_small, swapped(own_small, "tok"), 1)
    out_grad = lax.dot_general(
        small, readout_weight.astype(F32), (((0,), (1,)), ((), ())), precision=lax.Precision.HIGHEST
    )
    core_grad = swapped(own_grad, "tok")
    col_grad, out_grad, core_grad = lax.optimization_barrier((col_grad, out_grad, core_grad))
    far_grad = swapped(col_grad, "tok")
    layer_grad = in_order(half, own_grad, col_grad, 0)
    other_grad = in_order(half, core_grad, far_grad, 0)
    conv_grad = in_order(core, layer_grad[None], other_grad[None], 0)
    return (hologram[None], conv_grad, out_grad)


def solution(mesh):
    in_specs = (
        P("dp", "tok", None),
        P(),
        P(None, None, "col"),
        P("col", None),
        P(),
        P(),
        P(),
        P("dp", None, "tok", "col"),
    )
    out_specs = (P("dp", None, "tok", "col"), P(), P("col", None))
    return jax.shard_map(step, mesh=mesh, in_specs=in_specs, out_specs=out_specs, check_vma=False)
```

```python
import functools

import jax
import jax.numpy as jnp
from jax import lax
from jax.experimental import pallas as pl
from jax.experimental.pallas import tpu as pltpu
from jax.sharding import PartitionSpec as P


HEAD = 64
EPSILON = 1e-05
BF16 = jnp.bfloat16
F32 = jnp.float32
VMEM = pl.BlockSpec(memory_space=pltpu.VMEM)
SMEM = pl.BlockSpec(memory_space=pltpu.SMEM)
PARAMS = pltpu.CompilerParams(vmem_limit_bytes=16 * 2**20)
NT = (((1,), (1,)), ((), ()))


def dot(a, b):
    return jnp.dot(a, b, preferred_element_type=F32)


def split3(values):
    high = values.astype(BF16)
    rest = values - high.astype(F32)
    mid = rest.astype(BF16)
    low = (rest - mid.astype(F32)).astype(BF16)
    return high, mid, low


def normalize_kernel(tokens, gain, normed):
    values = tokens[...].astype(F32)
    center = values - jnp.mean(values, axis=-1, keepdims=True)
    spread = jnp.mean(center * center, axis=-1, keepdims=True)
    normed[...] = (center * lax.rsqrt(spread + EPSILON) * gain[...]).astype(BF16)


def normalize(tokens, gain):
    return pl.pallas_call(
        normalize_kernel,
        out_shape=jax.ShapeDtypeStruct(tokens.shape, BF16),
        in_specs=[VMEM, VMEM],
        out_specs=VMEM,
        compiler_params=PARAMS,
        name="normalize",
    )(tokens, gain)


def project_kernel(members, place, normed, weight, mine, theirs, turned):
    core = place[0]
    kept = mine.shape[0] * HEAD
    rows = normed[...]
    for at, member in enumerate(members):
        product = dot(rows, weight[member]).astype(BF16)
        if member == 0:
            product = product * jnp.asarray(1.0 / HEAD**0.5, BF16)
        turned[at] = product.T
        for which, out in ((1 - core, theirs), (core, mine)):
            for head in range(mine.shape[0]):
                start = pl.multiple_of(which * kept + head * HEAD, HEAD)
                out[head, at * HEAD : (at + 1) * HEAD, :] = turned[at, pl.ds(start, HEAD), :]


def project(members, place, normed, weight):
    count, length = weight.shape[2] // HEAD // 2, normed.shape[0]
    shape = jax.ShapeDtypeStruct((count, len(members) * HEAD, length), BF16)
    return pl.pallas_call(
        functools.partial(project_kernel, members),
        out_shape=(shape, shape),
        in_specs=[SMEM, VMEM, VMEM],
        out_specs=(VMEM,) * 2,
        scratch_shapes=[pltpu.VMEM((len(members), weight.shape[2], length), BF16)],
        compiler_params=PARAMS,
        name="project",
    )(place, normed, weight)


def attend(queries, block, running, best):
    length = block.shape[1]
    keys = block[:HEAD].T
    values = jnp.concatenate([block[HEAD:], jnp.ones((16, length), BF16)], axis=0)
    depth = min(512, length)
    for below in range(0, length, depth):
        scores = dot(keys[below : below + depth], queries)
        raised_top = jnp.max(scores, axis=0, keepdims=True)
        if best is not None:
            raised_top = jnp.maximum(best, raised_top)
        weights = jnp.exp(scores - raised_top).astype(BF16)
        added = dot(values[:, below : below + depth], weights)
        running = added if best is None else running * jnp.exp(best - raised_top) + added
        best = raised_top
    return running, best


def absorb_kernel(first, own, got, block, *refs):
    carried, carried_top = (None, None) if first else refs[:2]
    out, top = refs[-2:]
    length = own.shape[2]
    for head in range(own.shape[0]):
        for side, queries in enumerate((own, got)):
            where = slice(side * length, (side + 1) * length)
            running = None if first else carried[head, :, where]
            best = None if first else carried_top[head, 0:1, where]
            running, best = attend(queries[head], block[head], running, best)
            out[head, :, where] = running
            top[head, :, where] = jnp.broadcast_to(best, (8, length))


def absorb(queries, block, state):
    heads, _, length = queries[0].shape
    shapes = tuple(jax.ShapeDtypeStruct((heads, rows, 2 * length), F32) for rows in (HEAD + 16, 8))
    first = state is None
    return pl.pallas_call(
        functools.partial(absorb_kernel, first),
        out_shape=shapes,
        in_specs=[VMEM] * (3 if first else 5),
        out_specs=(VMEM, VMEM),
        input_output_aliases={} if first else {3: 0, 4: 1},
        compiler_params=PARAMS,
        name="absorb",
    )(*queries, block, *(() if first else state))


def closing_kernel(side, queries, block, carried, carried_top, folded, context, share):
    length = context.shape[1]
    where = slice(side * length, (side + 1) * length)
    for head in range(queries.shape[0]):
        running, _ = attend(queries[head], block[head], carried[head, :, where], carried_top[head, 0:1, where])
        context[head * HEAD : (head + 1) * HEAD, :] = (running[:HEAD] / running[HEAD : HEAD + 1]).astype(BF16)
    whole = context[...]
    share[...] = sum(dot(part, whole) for part in split3(folded[...]))


def closing(side, queries, block, state, folded):
    heads, _, length = queries[side].shape
    return pl.pallas_call(
        functools.partial(closing_kernel, side),
        out_shape=(
            jax.ShapeDtypeStruct((heads * HEAD, length), BF16),
            jax.ShapeDtypeStruct((folded.shape[0], length), F32),
        ),
        in_specs=[VMEM] * 5,
        out_specs=(VMEM, VMEM),
        compiler_params=PARAMS,
        name="closing",
    )(queries[side], block, *state, folded)


def arrange_kernel(weight, forward, backward):
    channels = weight.shape[1]
    for layer in range(weight.shape[0]):
        taps = weight[layer]
        turned_taps = taps.astype(F32).T
        for row in range(3):
            forward[layer, row] = taps[:, row * 3 * channels : (row + 1) * 3 * channels]
            at = [((2 - row) * 3 + 2 - column) * channels for column in range(3)]
            backward[layer, row] = jnp.concatenate(
                [turned_taps[start : start + channels, :] for start in at], axis=1
            ).astype(BF16)


def arrange(weight):
    layers, channels, wide = weight.shape
    shape = jax.ShapeDtypeStruct((layers, 3, channels, wide // 3), BF16)
    return pl.pallas_call(
        arrange_kernel,
        out_shape=(shape, shape),
        in_specs=[VMEM],
        out_specs=(VMEM, VMEM),
        compiler_params=PARAMS,
        name="arrange",
    )(weight)


def turned(values, step):
    return pltpu.roll(values, step % values.shape[1], 1)


def three_columns(values, cols):
    cells = values.shape[1]
    column = lax.rem(lax.broadcasted_iota(jnp.int32, (1, cells), 1), cols)
    wide = values.astype(F32)
    left = jnp.where(column == 0, 0.0, turned(wide, 1)).astype(BF16)
    right = jnp.where(column == cols - 1, 0.0, turned(wide, -1)).astype(BF16)
    return jnp.concatenate([left, values.astype(BF16), right], axis=0)


def three_rows(weights, columns, cols):
    cells = columns.shape[1] - 2 * cols
    return sum(dot(weights[a], columns[:, a * cols : a * cols + cells]) for a in range(3))


def network_kernel(
    cols, frame_rows, place, chip_map, near, far, forward, backward, head, own_context, their_context, holo, sums,
    gradient, hidden, pre_one, pre_two, grads,
):
    core, half, row_at = place[0], place[1], place[2]
    own = chip_map.shape[1]
    cells = hidden.shape[1]
    rim = (cells - own) // 2
    row_count = cells // cols
    above = rim // cols
    first_row = row_at - above
    piece = own // 2
    down = (core == place[3]).astype(jnp.int32)
    for source, base, lead in ((chip_map, own, core), (near, 2 * own * down, core), (far, 2 * own * (1 - down), 1 - core)):
        for side in range(2):
            start = pl.multiple_of(base + lax.rem(lead + side, 2) * piece, 128)
            hidden[:, pl.ds(start, piece)] = source[:, side * piece : (side + 1) * piece]

    def inside(start_row, rows):
        lane = lax.broadcasted_iota(jnp.int32, (1, rows * cols), 1)
        frame_lane = lane + (first_row + start_row) * cols
        return jnp.logical_and(frame_lane >= 0, frame_lane < frame_rows * cols)

    channels, outputs = forward.shape[2], head.shape[0]
    columns_zero = three_columns(jnp.where(inside(0, row_count), hidden[:channels, :].astype(F32), 0.0), cols)
    first = three_rows(forward[0], columns_zero, cols)
    rows_one = row_count - 2
    sigmoid_first = jax.nn.sigmoid(first)
    one = jnp.where(inside(1, rows_one), first * sigmoid_first, 0.0)
    columns_one = three_columns(one, cols)
    second = three_rows(forward[1], columns_one, cols)
    rows_two = row_count - 4
    sigmoid_two = jax.nn.sigmoid(second)
    two = (second * sigmoid_two).astype(BF16)
    holo[...] = dot(head[...], two[:, rim - 2 * cols : rim - 2 * cols + own])
    pieces = hidden[channels:, 2 * cols : cells - 2 * cols].astype(F32)
    cotangent = pieces[:outputs] + pieces[outputs : 2 * outputs] + pieces[2 * outputs : 3 * outputs]
    wide_head = head[...].astype(F32).T
    grad_two = sum(wide_head[:, at : at + 1] * cotangent[at : at + 1, :] for at in range(outputs)).astype(BF16)
    slope = grad_two.astype(F32) * sigmoid_two * (1.0 + second * (1.0 - sigmoid_two))
    pre_grad_two = jnp.where(inside(2, rows_two), slope, 0.0)
    grad_one = three_rows(backward[1], three_columns(pre_grad_two, cols), cols).astype(BF16)
    rows_grad = row_count - 6
    middle = first[:, 2 * cols : 2 * cols + rows_grad * cols]
    sigmoid_one = sigmoid_first[:, 2 * cols : 2 * cols + rows_grad * cols]
    slope = grad_one.astype(F32) * sigmoid_one * (1.0 + middle * (1.0 - sigmoid_one))
    pre_grad_one = jnp.where(inside(3, rows_grad), slope, 0.0)
    grad_zero = three_rows(backward[0], three_columns(pre_grad_one, cols), cols).astype(BF16)
    pre_one[...] = pre_grad_one[:, rim - 3 * cols : rim - 3 * cols + own].astype(BF16)
    pre_two[...] = pre_grad_two[:, rim - 2 * cols : rim - 2 * cols + own].astype(BF16)

    share = sums.shape[0]
    taps = 9 * channels
    for layer, (pre, columns, offset) in enumerate(((pre_one, columns_zero, rim), (pre_two, columns_one, rim - cols))):

        @pl.when(core == layer)
        def _(pre=pre, columns=columns, offset=offset):
            stacked = jnp.concatenate(
                [columns[:, offset + (a - 1) * cols : offset + (a - 1) * cols + own] for a in range(3)], axis=0
            )
            rows = pre[pl.ds(pl.multiple_of(half * share, 16), share), :]
            sums[:, :taps] = lax.dot_general(rows, stacked, NT, preferred_element_type=F32)

    grads[...] = grad_zero
    gradient[...] = sum(
        lax.dot_general(
            grads[:, pl.ds(pl.multiple_of(at * piece, 128), piece)], seen[...], NT, preferred_element_type=F32
        )
        for at, seen in ((core, own_context), (1 - core, their_context))
    )


def network(place, maps, forward, backward, head, own_context, their_context, cols, frame_rows, col_count):
    own = maps[0].shape[1]
    channels = forward.shape[2]
    return pl.pallas_call(
        functools.partial(network_kernel, cols, frame_rows),
        out_shape=(
            jax.ShapeDtypeStruct((head.shape[0], own), F32),
            jax.ShapeDtypeStruct((channels // col_count, 9 * channels), F32),
            jax.ShapeDtypeStruct((channels, own_context.shape[0]), F32),
        ),
        in_specs=[SMEM] + [VMEM] * 8,
        out_specs=(VMEM,) * 3,
        scratch_shapes=[pltpu.VMEM((maps[0].shape[0], 3 * own), BF16)] + [pltpu.VMEM((channels, own), BF16)] * 3,
        compiler_params=PARAMS,
        name="network",
    )(place, *maps, forward, backward, head, own_context, their_context)


def swapped(values, axis):
    size = lax.axis_size(axis)
    return lax.ppermute(values, axis, [(i, i ^ 1) for i in range(size)])


def passed(values, axis, step, wrap):
    size = lax.axis_size(axis)
    pairs = [(i, (i + step) % size) for i in range(size) if wrap or 0 <= i + step < size]
    return lax.ppermute(values, axis, pairs)


def beside(values):
    size, cols = lax.axis_size("tok"), lax.axis_size("col")
    pairs = []
    for at in range(size // 2):
        for core, other in ((0, at ^ 1), (1, ((at + 1) ^ 1) - 1)):
            inside = 0 <= other < size // 2
            for col in range(cols):
                target = (other if inside else at, col if inside or cols == 1 else col ^ 1)
                pairs.append(((2 * at + core) * cols + col, (2 * target[0] + core) * cols + target[1]))
    return lax.ppermute(values, ("tok", "col"), pairs)


def round_ring(values):
    size = lax.axis_size("tok")
    chips = size // 2
    order = [at for at in range(chips) if at == 0 or at % 2 == 1] + [
        at for at in reversed(range(chips)) if at and at % 2 == 0
    ]
    following = {order[at]: order[(at + 1) % chips] for at in range(chips)}
    return lax.ppermute(values, "tok", [(i, 2 * following[i // 2] + i % 2) for i in range(size)])


def everyone(values, axis, stride, count):
    sent = values.astype(BF16)
    terms = [(passed(sent, axis, stride * step, True) if step else sent).astype(F32) for step in range(count)]
    while len(terms) > 1:
        apart = len(terms) // 2
        terms = [terms[at] + terms[at + apart] for at in range(apart)]
    return terms[0]


def sum_frames(values, across):
    size, cols = lax.axis_size("dp"), lax.axis_size("col")
    sent = values.astype(BF16)
    terms = []
    for step in range(size):
        pairs = []
        for i in range(size):
            other = i ^ step if size & (size - 1) == 0 else (i + step) % size
            pairs += [(i * cols + j, other * cols + (j ^ 1 if across else j)) for j in range(cols)]
        moved = lax.ppermute(sent, ("dp", "col"), pairs) if step or across else sent
        terms.append(moved.astype(F32))
    while len(terms) > 1:
        terms = [sum(terms[at : at + 2][1:], terms[at]) for at in range(0, len(terms), 2)]
    return terms[0]


def in_order(core, mine, theirs, axis):
    return jnp.where(
        core == 0, jnp.concatenate([mine, theirs], axis=axis), jnp.concatenate([theirs, mine], axis=axis)
    )


def step(
    tokens, ln_gain, qkv_weight, out_weight, readout_weight, conv_weight, head_weight, holo_cot
):
    frame_rows = tokens[0]
    cotangent = holo_cot[0]
    rows_dev, cols_dev = cotangent.shape[1:]
    tok_count, col_count = lax.axis_size("tok"), lax.axis_size("col")
    chips = tok_count // 2
    tok_at, half = lax.axis_index("tok"), lax.axis_index("col")
    core = lax.rem(tok_at, 2)
    chip_row = (tok_at - core) * rows_dev
    place = jnp.stack([core, half, chip_row, lax.rem(tok_at // 2, 2)]).astype(jnp.int32)
    cols = cols_dev * col_count

    gain, qkv_weight, out_weight = lax.optimization_barrier(
        (ln_gain.astype(F32).reshape(1, -1), qkv_weight, out_weight)
    )
    normed = normalize(frame_rows, gain)
    own_keyed, their_keyed = project((1, 2), place, normed, qkv_weight)
    own_keyed, their_keyed, normed = lax.optimization_barrier((own_keyed, their_keyed, normed))
    got_keyed = swapped(their_keyed, "tok")
    own_queries, their_queries = project((0,), place, normed, qkv_weight)
    queries = (own_queries, swapped(their_queries, "tok"))
    kept = own_keyed.shape[0] * HEAD

    def prepare(conv_weight, out_weight, readout_weight, frame_rows):
        forward, backward = arrange(conv_weight)
        own_out = lax.dynamic_slice_in_dim(out_weight, core * kept, kept, 0)
        folded = lax.dot_general(readout_weight, own_out, (((0,), (1,)), ((), ())), preferred_element_type=F32)
        direct = lax.dot_general(readout_weight, frame_rows, (((0,), (1,)), ((), ())), preferred_element_type=F32)
        return (forward, backward, folded, direct)

    def exact_rows(other_cot):
        wide_cot = in_order(half, cotangent, other_cot, 2)
        exact_cot = jnp.concatenate(split3(wide_cot.reshape(wide_cot.shape[0], -1)), axis=0)
        return jnp.pad(exact_cot, ((0, -exact_cot.shape[0] % 16), (0, 0)))

    state, blocks = None, [own_keyed, got_keyed]
    for turn in range(chips):
        arriving = []
        if turn < chips - 1:
            for block in blocks:
                arriving.append(round_ring(block))
        for at, block in enumerate(blocks):
            if turn == chips - 1 and at == 1:
                break
            state = absorb(queries, block, state)
            if at == 0 and turn == chips - 2:
                state, given, own_cot = lax.optimization_barrier(
                    (state, (conv_weight, out_weight, readout_weight, frame_rows), cotangent)
                )
                prepared, other_cot = prepare(*given), swapped(own_cot, "col")
            if at == 1 and turn == chips - 2:
                state, other_cot = lax.optimization_barrier((state, other_cot))
                exact_cot = exact_rows(other_cot)
            if at == 0 and turn == chips - 1:
                state, prepared, exact_cot = lax.optimization_barrier((state, prepared, exact_cot))
            if turn < chips - 2:
                arriving[at], state = lax.optimization_barrier((arriving[at], state))
        blocks = arriving if turn < chips - 1 else blocks
    forward, backward, folded, direct = prepared

    their_context, their_share = closing(1, queries, blocks[1], state, folded)
    own_context, own_share = closing(0, queries, blocks[1], state, folded)
    partial = own_share + swapped(their_share, "tok")
    partial = (partial + jnp.where(half == 0, direct, 0.0)).astype(BF16)
    own_map = (partial.astype(F32) + swapped(partial, "col").astype(F32)).astype(BF16)
    own_map = jnp.concatenate([own_map, exact_cot], axis=0)
    chip_map = jnp.concatenate([own_map, swapped(own_map, "tok")], axis=1)
    near = beside(chip_map)
    rows_chip = 2 * rows_dev
    maps = (chip_map, near, swapped(near, "tok"))
    holo, sums, gradient = network(
        place, maps, forward, backward, head_weight, own_context, their_context, cols, tok_count * rows_dev, col_count
    )
    holo = holo.reshape(-1, rows_chip, cols)
    hologram = lax.dynamic_slice(
        holo, (0, core * rows_dev, half * cols_dev), (holo.shape[0], rows_dev, cols_dev)
    )

    taps_wide = sums.shape[1]
    lanes = 128 * ((taps_wide + 127) // 128)
    rows = sums.shape[0]
    pieces = gradient.shape[0] // rows
    folded_gradient = [gradient[at * rows : (at + 1) * rows] for at in range(pieces)]
    sent = jnp.concatenate([jnp.pad(sums, ((0, 0), (0, lanes - taps_wide))), *folded_gradient], axis=1)
    summed, hologram = lax.optimization_barrier((everyone(sent, "tok", 2, chips), hologram))
    own_terms = sum_frames(summed, False)
    far_terms = sum_frames(summed[:, :taps_wide], True)
    wide = gradient.shape[1]
    own_small = jnp.concatenate(
        [own_terms[:, lanes + at * wide : lanes + (at + 1) * wide] for at in range(pieces)], axis=0
    )
    other_small = swapped(own_small, "tok")
    small = in_order(core, own_small, other_small, 1)
    out_grad = lax.dot_general(
        small, readout_weight.astype(F32), (((0,), (1,)), ((), ())), precision=lax.Precision.HIGHEST
    )
    layer_grad = in_order(half, own_terms[:, :taps_wide], far_terms, 0)
    other_grad = swapped(layer_grad, "tok")
    conv_grad = in_order(core, layer_grad[None], other_grad[None], 0)
    return (hologram[None], conv_grad, out_grad)


def solution(mesh):
    in_specs = (
        P("dp", "tok", None),
        P(),
        P(None, None, "col"),
        P("col", None),
        P(),
        P(),
        P(),
        P("dp", None, "tok", "col"),
    )
    out_specs = (P("dp", None, "tok", "col"), P(), P("col", None))
    return jax.shard_map(step, mesh=mesh, in_specs=in_specs, out_specs=out_specs, check_vma=False)
```

```python
import functools

import jax
import jax.numpy as jnp
from jax import lax
from jax.experimental import pallas as pl
from jax.experimental.pallas import tpu as pltpu
from jax.sharding import PartitionSpec as P


HEAD = 64
EPSILON = 1e-05
BF16 = jnp.bfloat16
F32 = jnp.float32
VMEM = pl.BlockSpec(memory_space=pltpu.VMEM)
SMEM = pl.BlockSpec(memory_space=pltpu.SMEM)
PARAMS = pltpu.CompilerParams(vmem_limit_bytes=16 * 2**20)
NT = (((1,), (1,)), ((), ()))


def dot(a, b):
    return jnp.dot(a, b, preferred_element_type=F32)


def split3(values):
    high = values.astype(BF16)
    rest = values - high.astype(F32)
    mid = rest.astype(BF16)
    low = (rest - mid.astype(F32)).astype(BF16)
    return high, mid, low


def normalize_kernel(tokens, gain, normed):
    values = tokens[...].astype(F32)
    center = values - jnp.mean(values, axis=-1, keepdims=True)
    spread = jnp.mean(center * center, axis=-1, keepdims=True)
    normed[...] = (center * lax.rsqrt(spread + EPSILON) * gain[...]).astype(BF16)


def normalize(tokens, gain):
    return pl.pallas_call(
        normalize_kernel,
        out_shape=jax.ShapeDtypeStruct(tokens.shape, BF16),
        in_specs=[VMEM, VMEM],
        out_specs=VMEM,
        compiler_params=PARAMS,
        name="normalize",
    )(tokens, gain)


def project_kernel(members, place, normed, weight, mine, theirs, turned):
    core = place[0]
    kept = mine.shape[0] * HEAD
    rows = normed[...]
    for at, member in enumerate(members):
        product = dot(rows, weight[member]).astype(BF16)
        if member == 0:
            product = product * jnp.asarray(1.0 / HEAD**0.5, BF16)
        turned[at] = product.T
        for which, out in ((1 - core, theirs), (core, mine)):
            for head in range(mine.shape[0]):
                start = pl.multiple_of(which * kept + head * HEAD, HEAD)
                out[head, at * HEAD : (at + 1) * HEAD, :] = turned[at, pl.ds(start, HEAD), :]


def project(members, place, normed, weight):
    count, length = weight.shape[2] // HEAD // 2, normed.shape[0]
    shape = jax.ShapeDtypeStruct((count, len(members) * HEAD, length), BF16)
    return pl.pallas_call(
        functools.partial(project_kernel, members),
        out_shape=(shape, shape),
        in_specs=[SMEM, VMEM, VMEM],
        out_specs=(VMEM,) * 2,
        scratch_shapes=[pltpu.VMEM((len(members), weight.shape[2], length), BF16)],
        compiler_params=PARAMS,
        name="project",
    )(place, normed, weight)


def attend(queries, block, running, best):
    length = block.shape[1]
    keys = block[:HEAD].T
    values = jnp.concatenate([block[HEAD:], jnp.ones((16, length), BF16)], axis=0)
    depth = min(512, length)
    for below in range(0, length, depth):
        scores = dot(keys[below : below + depth], queries)
        raised_top = jnp.max(scores, axis=0, keepdims=True)
        if best is not None:
            raised_top = jnp.maximum(best, raised_top)
        weights = jnp.exp(scores - raised_top).astype(BF16)
        added = dot(values[:, below : below + depth], weights)
        running = added if best is None else running * jnp.exp(best - raised_top) + added
        best = raised_top
    return running, best


def absorb_kernel(first, own, got, block, *refs):
    carried, carried_top = (None, None) if first else refs[:2]
    out, top = refs[-2:]
    length = own.shape[2]
    for head in range(own.shape[0]):
        for side, queries in enumerate((own, got)):
            where = slice(side * length, (side + 1) * length)
            running = None if first else carried[head, :, where]
            best = None if first else carried_top[head, 0:1, where]
            running, best = attend(queries[head], block[head], running, best)
            out[head, :, where] = running
            top[head, :, where] = jnp.broadcast_to(best, (8, length))


def absorb(queries, block, state):
    heads, _, length = queries[0].shape
    shapes = tuple(jax.ShapeDtypeStruct((heads, rows, 2 * length), F32) for rows in (HEAD + 16, 8))
    first = state is None
    return pl.pallas_call(
        functools.partial(absorb_kernel, first),
        out_shape=shapes,
        in_specs=[VMEM] * (3 if first else 5),
        out_specs=(VMEM, VMEM),
        input_output_aliases={} if first else {3: 0, 4: 1},
        compiler_params=PARAMS,
        name="absorb",
    )(*queries, block, *(() if first else state))


def closing_kernel(side, queries, block, carried, carried_top, folded, context, share):
    length = context.shape[1]
    where = slice(side * length, (side + 1) * length)
    for head in range(queries.shape[0]):
        running, _ = attend(queries[head], block[head], carried[head, :, where], carried_top[head, 0:1, where])
        context[head * HEAD : (head + 1) * HEAD, :] = (running[:HEAD] / running[HEAD : HEAD + 1]).astype(BF16)
    whole = context[...]
    share[...] = sum(dot(part, whole) for part in split3(folded[...]))


def closing(side, queries, block, state, folded):
    heads, _, length = queries[side].shape
    return pl.pallas_call(
        functools.partial(closing_kernel, side),
        out_shape=(
            jax.ShapeDtypeStruct((heads * HEAD, length), BF16),
            jax.ShapeDtypeStruct((folded.shape[0], length), F32),
        ),
        in_specs=[VMEM] * 5,
        out_specs=(VMEM, VMEM),
        compiler_params=PARAMS,
        name="closing",
    )(queries[side], block, *state, folded)


def arrange_kernel(weight, forward, backward):
    channels = weight.shape[1]
    for layer in range(weight.shape[0]):
        taps = weight[layer]
        turned_taps = taps.astype(F32).T
        for row in range(3):
            forward[layer, row] = taps[:, row * 3 * channels : (row + 1) * 3 * channels]
            at = [((2 - row) * 3 + 2 - column) * channels for column in range(3)]
            backward[layer, row] = jnp.concatenate(
                [turned_taps[start : start + channels, :] for start in at], axis=1
            ).astype(BF16)


def arrange(weight):
    layers, channels, wide = weight.shape
    shape = jax.ShapeDtypeStruct((layers, 3, channels, wide // 3), BF16)
    return pl.pallas_call(
        arrange_kernel,
        out_shape=(shape, shape),
        in_specs=[VMEM],
        out_specs=(VMEM, VMEM),
        compiler_params=PARAMS,
        name="arrange",
    )(weight)


def turned(values, step):
    return pltpu.roll(values, step % values.shape[1], 1)


def three_columns(values, cols):
    cells = values.shape[1]
    column = lax.rem(lax.broadcasted_iota(jnp.int32, (1, cells), 1), cols)
    wide = values.astype(F32)
    left = jnp.where(column == 0, 0.0, turned(wide, 1)).astype(BF16)
    right = jnp.where(column == cols - 1, 0.0, turned(wide, -1)).astype(BF16)
    return jnp.concatenate([left, values.astype(BF16), right], axis=0)


def three_rows(weights, columns, cols):
    cells = columns.shape[1] - 2 * cols
    return sum(dot(weights[a], columns[:, a * cols : a * cols + cells]) for a in range(3))


def network_kernel(
    cols, frame_rows, place, chip_map, near, far, forward, backward, head, own_context, their_context, holo, sums,
    gradient, hidden, pre_one, pre_two, grads,
):
    core, half, row_at = place[0], place[1], place[2]
    own = chip_map.shape[1]
    cells = hidden.shape[1]
    rim = (cells - own) // 2
    row_count = cells // cols
    above = rim // cols
    first_row = row_at - above
    piece = own // 2
    down = (core == place[3]).astype(jnp.int32)
    for source, base, lead in ((chip_map, own, core), (near, 2 * own * down, core), (far, 2 * own * (1 - down), 1 - core)):
        for side in range(2):
            start = pl.multiple_of(base + lax.rem(lead + side, 2) * piece, 128)
            hidden[:, pl.ds(start, piece)] = source[:, side * piece : (side + 1) * piece]

    def inside(start_row, rows):
        lane = lax.broadcasted_iota(jnp.int32, (1, rows * cols), 1)
        frame_lane = lane + (first_row + start_row) * cols
        return jnp.logical_and(frame_lane >= 0, frame_lane < frame_rows * cols)

    channels, outputs = forward.shape[2], head.shape[0]
    columns_zero = three_columns(jnp.where(inside(0, row_count), hidden[:channels, :].astype(F32), 0.0), cols)
    first = three_rows(forward[0], columns_zero, cols)
    rows_one = row_count - 2
    sigmoid_first = jax.nn.sigmoid(first)
    one = jnp.where(inside(1, rows_one), first * sigmoid_first, 0.0)
    columns_one = three_columns(one, cols)
    second = three_rows(forward[1], columns_one, cols)
    rows_two = row_count - 4
    sigmoid_two = jax.nn.sigmoid(second)
    two = (second * sigmoid_two).astype(BF16)
    holo[...] = dot(head[...], two[:, rim - 2 * cols : rim - 2 * cols + own])
    pieces = hidden[channels:, 2 * cols : cells - 2 * cols].astype(F32)
    cotangent = pieces[:outputs] + pieces[outputs : 2 * outputs] + pieces[2 * outputs : 3 * outputs]
    wide_head = head[...].astype(F32).T
    grad_two = sum(wide_head[:, at : at + 1] * cotangent[at : at + 1, :] for at in range(outputs)).astype(BF16)
    slope = grad_two.astype(F32) * sigmoid_two * (1.0 + second * (1.0 - sigmoid_two))
    pre_grad_two = jnp.where(inside(2, rows_two), slope, 0.0)
    grad_one = three_rows(backward[1], three_columns(pre_grad_two, cols), cols).astype(BF16)
    rows_grad = row_count - 6
    middle = first[:, 2 * cols : 2 * cols + rows_grad * cols]
    sigmoid_one = sigmoid_first[:, 2 * cols : 2 * cols + rows_grad * cols]
    slope = grad_one.astype(F32) * sigmoid_one * (1.0 + middle * (1.0 - sigmoid_one))
    pre_grad_one = jnp.where(inside(3, rows_grad), slope, 0.0)
    grad_zero = three_rows(backward[0], three_columns(pre_grad_one, cols), cols).astype(BF16)
    pre_one[...] = pre_grad_one[:, rim - 3 * cols : rim - 3 * cols + own].astype(BF16)
    pre_two[...] = pre_grad_two[:, rim - 2 * cols : rim - 2 * cols + own].astype(BF16)

    share = sums.shape[0]
    taps = 9 * channels
    for layer, (pre, columns, offset) in enumerate(((pre_one, columns_zero, rim), (pre_two, columns_one, rim - cols))):

        @pl.when(core == layer)
        def _(pre=pre, columns=columns, offset=offset):
            stacked = jnp.concatenate(
                [columns[:, offset + (a - 1) * cols : offset + (a - 1) * cols + own] for a in range(3)], axis=0
            )
            rows = pre[pl.ds(pl.multiple_of(half * share, 16), share), :]
            sums[:, :taps] = lax.dot_general(rows, stacked, NT, preferred_element_type=F32)

    grads[...] = grad_zero
    gradient[...] = sum(
        lax.dot_general(
            grads[:, pl.ds(pl.multiple_of(at * piece, 128), piece)], seen[...], NT, preferred_element_type=F32
        )
        for at, seen in ((core, own_context), (1 - core, their_context))
    )


def network(place, maps, forward, backward, head, own_context, their_context, cols, frame_rows, col_count):
    own = maps[0].shape[1]
    channels = forward.shape[2]
    return pl.pallas_call(
        functools.partial(network_kernel, cols, frame_rows),
        out_shape=(
            jax.ShapeDtypeStruct((head.shape[0], own), F32),
            jax.ShapeDtypeStruct((channels // col_count, 9 * channels), F32),
            jax.ShapeDtypeStruct((channels, own_context.shape[0]), F32),
        ),
        in_specs=[SMEM] + [VMEM] * 8,
        out_specs=(VMEM,) * 3,
        scratch_shapes=[pltpu.VMEM((maps[0].shape[0], 3 * own), BF16)] + [pltpu.VMEM((channels, own), BF16)] * 3,
        compiler_params=PARAMS,
        name="network",
    )(place, *maps, forward, backward, head, own_context, their_context)


def swapped(values, axis):
    size = lax.axis_size(axis)
    return lax.ppermute(values, axis, [(i, i ^ 1) for i in range(size)])


def passed(values, axis, step, wrap):
    size = lax.axis_size(axis)
    pairs = [(i, (i + step) % size) for i in range(size) if wrap or 0 <= i + step < size]
    return lax.ppermute(values, axis, pairs)


def beside(values):
    size, cols = lax.axis_size("tok"), lax.axis_size("col")
    pairs = []
    for at in range(size // 2):
        for core, other in ((0, at ^ 1), (1, ((at + 1) ^ 1) - 1)):
            inside = 0 <= other < size // 2
            for col in range(cols):
                target = (other if inside else at, col if inside or cols == 1 else col ^ 1)
                pairs.append(((2 * at + core) * cols + col, (2 * target[0] + core) * cols + target[1]))
    return lax.ppermute(values, ("tok", "col"), pairs)


def round_ring(values):
    size = lax.axis_size("tok")
    chips = size // 2
    order = [at for at in range(chips) if at == 0 or at % 2 == 1] + [
        at for at in reversed(range(chips)) if at and at % 2 == 0
    ]
    following = {order[at]: order[(at + 1) % chips] for at in range(chips)}
    return lax.ppermute(values, "tok", [(i, 2 * following[i // 2] + i % 2) for i in range(size)])


def everyone(values, axis, stride, count):
    sent = values.astype(BF16)
    terms = [(passed(sent, axis, stride * step, True) if step else sent).astype(F32) for step in range(count)]
    while len(terms) > 1:
        apart = len(terms) // 2
        terms = [terms[at] + terms[at + apart] for at in range(apart)]
    return terms[0]


def sum_frames(values, across):
    size, cols = lax.axis_size("dp"), lax.axis_size("col")
    sent = values.astype(BF16)
    terms = []
    for step in range(size):
        pairs = []
        for i in range(size):
            other = i ^ step if size & (size - 1) == 0 else (i + step) % size
            pairs += [(i * cols + j, other * cols + (j ^ 1 if across else j)) for j in range(cols)]
        moved = lax.ppermute(sent, ("dp", "col"), pairs) if step or across else sent
        terms.append(moved.astype(F32))
    while len(terms) > 1:
        terms = [sum(terms[at : at + 2][1:], terms[at]) for at in range(0, len(terms), 2)]
    return terms[0]


def in_order(core, mine, theirs, axis):
    return jnp.where(
        core == 0, jnp.concatenate([mine, theirs], axis=axis), jnp.concatenate([theirs, mine], axis=axis)
    )


def step(
    tokens, ln_gain, qkv_weight, out_weight, readout_weight, conv_weight, head_weight, holo_cot
):
    frame_rows = tokens[0]
    cotangent = holo_cot[0]
    rows_dev, cols_dev = cotangent.shape[1:]
    tok_count, col_count = lax.axis_size("tok"), lax.axis_size("col")
    chips = tok_count // 2
    tok_at, half = lax.axis_index("tok"), lax.axis_index("col")
    core = lax.rem(tok_at, 2)
    chip_row = (tok_at - core) * rows_dev
    place = jnp.stack([core, half, chip_row, lax.rem(tok_at // 2, 2)]).astype(jnp.int32)
    cols = cols_dev * col_count

    gain, qkv_weight, out_weight = lax.optimization_barrier(
        (ln_gain.astype(F32).reshape(1, -1), qkv_weight, out_weight)
    )
    normed = normalize(frame_rows, gain)
    own_keyed, their_keyed = project((1, 2), place, normed, qkv_weight)
    own_keyed, their_keyed, normed = lax.optimization_barrier((own_keyed, their_keyed, normed))
    got_keyed = swapped(their_keyed, "tok")
    own_queries, their_queries = project((0,), place, normed, qkv_weight)
    queries = (own_queries, swapped(their_queries, "tok"))
    kept = own_keyed.shape[0] * HEAD

    def prepare(conv_weight, out_weight, readout_weight, frame_rows):
        forward, backward = arrange(conv_weight)
        own_out = lax.dynamic_slice_in_dim(out_weight, core * kept, kept, 0)
        folded = lax.dot_general(readout_weight, own_out, (((0,), (1,)), ((), ())), preferred_element_type=F32)
        direct = lax.dot_general(readout_weight, frame_rows, (((0,), (1,)), ((), ())), preferred_element_type=F32)
        return (forward, backward, folded, direct)

    def exact_rows(other_cot):
        wide_cot = in_order(half, cotangent, other_cot, 2)
        exact_cot = jnp.concatenate(split3(wide_cot.reshape(wide_cot.shape[0], -1)), axis=0)
        return jnp.pad(exact_cot, ((0, -exact_cot.shape[0] % 16), (0, 0)))

    state, blocks = None, [own_keyed, got_keyed]
    for turn in range(chips):
        arriving = []
        if turn < chips - 1:
            leaving = blocks
            if turn == chips - 2:
                leaving = blocks[:-1] + jnp.split(blocks[-1], 2, axis=2)
            for block in leaving:
                arriving.append(round_ring(block))
        for at, block in enumerate(blocks):
            if turn == chips - 1 and at == len(blocks) - 1:
                break
            state = absorb(queries, block, state)
            if at == 0 and turn == chips - 2:
                state, given, own_cot = lax.optimization_barrier(
                    (state, (conv_weight, out_weight, readout_weight, frame_rows), cotangent)
                )
                prepared, other_cot = prepare(*given), swapped(own_cot, "col")
            if at == 1 and turn == chips - 2:
                state, other_cot = lax.optimization_barrier((state, other_cot))
                exact_cot = exact_rows(other_cot)
            if at == 0 and turn == chips - 1:
                state, prepared, exact_cot = lax.optimization_barrier((state, prepared, exact_cot))
            if turn < chips - 2:
                arriving[at], state = lax.optimization_barrier((arriving[at], state))
        blocks = arriving if turn < chips - 1 else blocks
    forward, backward, folded, direct = prepared

    their_context, their_share = closing(1, queries, blocks[-1], state, folded)
    own_context, own_share = closing(0, queries, blocks[-1], state, folded)
    partial = own_share + swapped(their_share, "tok")
    partial = (partial + jnp.where(half == 0, direct, 0.0)).astype(BF16)
    own_map = (partial.astype(F32) + swapped(partial, "col").astype(F32)).astype(BF16)
    own_map = jnp.concatenate([own_map, exact_cot], axis=0)
    chip_map = jnp.concatenate([own_map, swapped(own_map, "tok")], axis=1)
    near = beside(chip_map)
    rows_chip = 2 * rows_dev
    maps = (chip_map, near, swapped(near, "tok"))
    holo, sums, gradient = network(
        place, maps, forward, backward, head_weight, own_context, their_context, cols, tok_count * rows_dev, col_count
    )
    holo = holo.reshape(-1, rows_chip, cols)
    hologram = lax.dynamic_slice(
        holo, (0, core * rows_dev, half * cols_dev), (holo.shape[0], rows_dev, cols_dev)
    )

    taps_wide = sums.shape[1]
    lanes = 128 * ((taps_wide + 127) // 128)
    rows = sums.shape[0]
    pieces = gradient.shape[0] // rows
    folded_gradient = [gradient[at * rows : (at + 1) * rows] for at in range(pieces)]
    sent = jnp.concatenate([jnp.pad(sums, ((0, 0), (0, lanes - taps_wide))), *folded_gradient], axis=1)
    summed = everyone(sent, "tok", 2, chips)
    own_terms = sum_frames(summed, False)
    far_terms = sum_frames(summed[:, :taps_wide], True)
    wide = gradient.shape[1]
    own_small = jnp.concatenate(
        [own_terms[:, lanes + at * wide : lanes + (at + 1) * wide] for at in range(pieces)], axis=0
    )
    small = in_order(core, own_small, swapped(own_small, "tok"), 1)
    out_grad = lax.dot_general(
        small, readout_weight.astype(F32), (((0,), (1,)), ((), ())), precision=lax.Precision.HIGHEST
    )
    layer_grad = in_order(half, own_terms[:, :taps_wide], far_terms, 0)
    conv_grad = in_order(core, layer_grad[None], swapped(layer_grad, "tok")[None], 0)
    return (hologram[None], conv_grad, out_grad)


def solution(mesh):
    in_specs = (
        P("dp", "tok", None),
        P(),
        P(None, None, "col"),
        P("col", None),
        P(),
        P(),
        P(),
        P("dp", None, "tok", "col"),
    )
    out_specs = (P("dp", None, "tok", "col"), P(), P("col", None))
    return jax.shard_map(step, mesh=mesh, in_specs=in_specs, out_specs=out_specs, check_vma=False)
```

```python
import functools

import jax
import jax.numpy as jnp
from jax import lax
from jax.experimental import pallas as pl
from jax.experimental.pallas import tpu as pltpu
from jax.sharding import PartitionSpec as P


HEAD = 64
EPSILON = 1e-05
BF16 = jnp.bfloat16
F32 = jnp.float32
VMEM = pl.BlockSpec(memory_space=pltpu.VMEM)
SMEM = pl.BlockSpec(memory_space=pltpu.SMEM)
PARAMS = pltpu.CompilerParams(vmem_limit_bytes=16 * 2**20)
NT = (((1,), (1,)), ((), ()))


def dot(a, b):
    return jnp.dot(a, b, preferred_element_type=F32)


def split3(values):
    high = values.astype(BF16)
    rest = values - high.astype(F32)
    mid = rest.astype(BF16)
    low = (rest - mid.astype(F32)).astype(BF16)
    return high, mid, low


def project_kernel(members, raw, place, rows, *refs):
    if raw:
        gain, weight, normed, mine, theirs, parts, turned, sems = refs
    else:
        weight, mine, theirs, parts, turned, sems = refs
    copies = [
        pltpu.make_async_copy(weight.at[member], parts.at[at], sems.at[at]) for at, member in enumerate(members)
    ]
    for copy in copies:
        copy.start()
    if raw:
        values = rows[...].astype(F32)
        center = values - jnp.mean(values, axis=-1, keepdims=True)
        spread = jnp.mean(center * center, axis=-1, keepdims=True)
        normed[...] = (center * lax.rsqrt(spread + EPSILON) * gain[...]).astype(BF16)
        rows = normed
    core = place[0]
    kept = mine.shape[0] * HEAD
    for at, member in enumerate(members):
        copies[at].wait()
        product = dot(rows[...], parts[at]).astype(BF16)
        if member == 0:
            product = product * jnp.asarray(1.0 / HEAD**0.5, BF16)
        turned[at] = product.T
        for which, out in ((1 - core, theirs), (core, mine)):
            for head in range(mine.shape[0]):
                start = pl.multiple_of(which * kept + head * HEAD, HEAD)
                out[head, at * HEAD : (at + 1) * HEAD, :] = turned[at, pl.ds(start, HEAD), :]


def project(members, place, rows, weight, gain=None):
    length, width = rows.shape[0], weight.shape[2]
    shape = jax.ShapeDtypeStruct((width // HEAD // 2, len(members) * HEAD, length), BF16)
    raw = gain is not None
    return pl.pallas_call(
        functools.partial(project_kernel, members, raw),
        out_shape=((jax.ShapeDtypeStruct(rows.shape, BF16),) if raw else ()) + (shape, shape),
        in_specs=[SMEM, VMEM] + [VMEM] * raw + [pl.BlockSpec(memory_space=pltpu.HBM)],
        out_specs=(VMEM,) * (2 + raw),
        scratch_shapes=[
            pltpu.VMEM((len(members),) + weight.shape[1:], BF16),
            pltpu.VMEM((len(members), width, length), BF16),
            pltpu.SemaphoreType.DMA((len(members),)),
        ],
        compiler_params=PARAMS,
        name="project",
    )(place, rows, *((gain,) if raw else ()), weight)


def attend(queries, block, running, best):
    length = block.shape[1]
    keys = block[:HEAD].T
    values = jnp.concatenate([block[HEAD:], jnp.ones((16, length), BF16)], axis=0)
    depth = min(512, length)
    for below in range(0, length, depth):
        scores = dot(keys[below : below + depth], queries)
        raised_top = jnp.max(scores, axis=0, keepdims=True)
        if best is not None:
            raised_top = jnp.maximum(best, raised_top)
        weights = jnp.exp(scores - raised_top).astype(BF16)
        added = dot(values[:, below : below + depth], weights)
        running = added if best is None else running * jnp.exp(best - raised_top) + added
        best = raised_top
    return running, best


def absorb_kernel(first, own, got, block, *refs):
    carried, carried_top = (None, None) if first else refs[:2]
    out, top = refs[-2:]
    length = own.shape[2]
    for head in range(own.shape[0]):
        for side, queries in enumerate((own, got)):
            where = slice(side * length, (side + 1) * length)
            running = None if first else carried[head, :, where]
            best = None if first else carried_top[head, 0:1, where]
            running, best = attend(queries[head], block[head], running, best)
            out[head, :, where] = running
            top[head, :, where] = jnp.broadcast_to(best, (8, length))


def absorb(queries, block, state):
    heads, _, length = queries[0].shape
    shapes = tuple(jax.ShapeDtypeStruct((heads, rows, 2 * length), F32) for rows in (HEAD + 16, 8))
    first = state is None
    return pl.pallas_call(
        functools.partial(absorb_kernel, first),
        out_shape=shapes,
        in_specs=[VMEM] * (3 if first else 5),
        out_specs=(VMEM, VMEM),
        input_output_aliases={} if first else {3: 0, 4: 1},
        compiler_params=PARAMS,
        name="absorb",
    )(*queries, block, *(() if first else state))


def closing_kernel(side, queries, block, carried, carried_top, folded, context, share):
    length = context.shape[1]
    where = slice(side * length, (side + 1) * length)
    for head in range(queries.shape[0]):
        running, _ = attend(queries[head], block[head], carried[head, :, where], carried_top[head, 0:1, where])
        context[head * HEAD : (head + 1) * HEAD, :] = (running[:HEAD] / running[HEAD : HEAD + 1]).astype(BF16)
    whole = context[...]
    share[...] = sum(dot(part, whole) for part in split3(folded[...]))


def closing(side, queries, block, state, folded):
    heads, _, length = queries[side].shape
    return pl.pallas_call(
        functools.partial(closing_kernel, side),
        out_shape=(
            jax.ShapeDtypeStruct((heads * HEAD, length), BF16),
            jax.ShapeDtypeStruct((folded.shape[0], length), F32),
        ),
        in_specs=[VMEM] * 5,
        out_specs=(VMEM, VMEM),
        compiler_params=PARAMS,
        name="closing",
    )(queries[side], block, *state, folded)


def arrange_kernel(weight, forward, backward):
    channels = weight.shape[1]
    for layer in range(weight.shape[0]):
        taps = weight[layer]
        turned_taps = taps.astype(F32).T
        for row in range(3):
            forward[layer, row] = taps[:, row * 3 * channels : (row + 1) * 3 * channels]
            at = [((2 - row) * 3 + 2 - column) * channels for column in range(3)]
            backward[layer, row] = jnp.concatenate(
                [turned_taps[start : start + channels, :] for start in at], axis=1
            ).astype(BF16)


def arrange(weight):
    layers, channels, wide = weight.shape
    shape = jax.ShapeDtypeStruct((layers, 3, channels, wide // 3), BF16)
    return pl.pallas_call(
        arrange_kernel,
        out_shape=(shape, shape),
        in_specs=[VMEM],
        out_specs=(VMEM, VMEM),
        compiler_params=PARAMS,
        name="arrange",
    )(weight)


def fold_kernel(place, out_weight, readout_weight, folded, rows, sem):
    kept = rows.shape[0]
    start = pl.multiple_of(place[0] * kept, kept)
    copy = pltpu.make_async_copy(out_weight.at[pl.ds(start, kept)], rows, sem.at[0])
    copy.start()
    copy.wait()
    folded[...] = dot(rows[...], readout_weight[...]).T


def fold(place, out_weight, readout_weight, kept):
    return pl.pallas_call(
        fold_kernel,
        out_shape=jax.ShapeDtypeStruct((readout_weight.shape[1], kept), F32),
        in_specs=[SMEM, pl.BlockSpec(memory_space=pltpu.HBM), VMEM],
        out_specs=VMEM,
        scratch_shapes=[pltpu.VMEM((kept, out_weight.shape[1]), BF16), pltpu.SemaphoreType.DMA((1,))],
        compiler_params=PARAMS,
        name="fold",
    )(place, pltpu.with_memory_space_constraint(out_weight, pltpu.HBM), readout_weight)


def turned(values, step):
    return pltpu.roll(values, step % values.shape[1], 1)


def three_columns(values, cols):
    cells = values.shape[1]
    column = lax.rem(lax.broadcasted_iota(jnp.int32, (1, cells), 1), cols)
    wide = values.astype(F32)
    left = jnp.where(column == 0, 0.0, turned(wide, 1)).astype(BF16)
    right = jnp.where(column == cols - 1, 0.0, turned(wide, -1)).astype(BF16)
    return jnp.concatenate([left, values.astype(BF16), right], axis=0)


def three_rows(weights, columns, cols):
    cells = columns.shape[1] - 2 * cols
    return sum(dot(weights[a], columns[:, a * cols : a * cols + cells]) for a in range(3))


def network_kernel(
    cols, frame_rows, place, chip_map, near, far, forward, backward, head, own_context, their_context, holo, sums,
    gradient, hidden, pre_one, pre_two, grads,
):
    core, half, row_at = place[0], place[1], place[2]
    own = chip_map.shape[1]
    cells = hidden.shape[1]
    rim = (cells - own) // 2
    row_count = cells // cols
    above = rim // cols
    first_row = row_at - above
    piece = own // 2
    down = (core == place[3]).astype(jnp.int32)
    for source, base, lead in ((chip_map, own, core), (near, 2 * own * down, core), (far, 2 * own * (1 - down), 1 - core)):
        for side in range(2):
            start = pl.multiple_of(base + lax.rem(lead + side, 2) * piece, 128)
            hidden[:, pl.ds(start, piece)] = source[:, side * piece : (side + 1) * piece]

    def inside(start_row, rows):
        lane = lax.broadcasted_iota(jnp.int32, (1, rows * cols), 1)
        frame_lane = lane + (first_row + start_row) * cols
        return jnp.logical_and(frame_lane >= 0, frame_lane < frame_rows * cols)

    channels, outputs = forward.shape[2], head.shape[0]
    columns_zero = three_columns(jnp.where(inside(0, row_count), hidden[:channels, :].astype(F32), 0.0), cols)
    first = three_rows(forward[0], columns_zero, cols)
    rows_one = row_count - 2
    sigmoid_first = jax.nn.sigmoid(first)
    one = jnp.where(inside(1, rows_one), first * sigmoid_first, 0.0)
    columns_one = three_columns(one, cols)
    second = three_rows(forward[1], columns_one, cols)
    rows_two = row_count - 4
    sigmoid_two = jax.nn.sigmoid(second)
    two = (second * sigmoid_two).astype(BF16)
    holo[...] = dot(head[...], two[:, rim - 2 * cols : rim - 2 * cols + own])
    pieces = hidden[channels:, 2 * cols : cells - 2 * cols].astype(F32)
    cotangent = pieces[:outputs] + pieces[outputs : 2 * outputs] + pieces[2 * outputs : 3 * outputs]
    wide_head = head[...].astype(F32).T
    grad_two = sum(wide_head[:, at : at + 1] * cotangent[at : at + 1, :] for at in range(outputs)).astype(BF16)
    slope = grad_two.astype(F32) * sigmoid_two * (1.0 + second * (1.0 - sigmoid_two))
    pre_grad_two = jnp.where(inside(2, rows_two), slope, 0.0)
    grad_one = three_rows(backward[1], three_columns(pre_grad_two, cols), cols).astype(BF16)
    rows_grad = row_count - 6
    middle = first[:, 2 * cols : 2 * cols + rows_grad * cols]
    sigmoid_one = sigmoid_first[:, 2 * cols : 2 * cols + rows_grad * cols]
    slope = grad_one.astype(F32) * sigmoid_one * (1.0 + middle * (1.0 - sigmoid_one))
    pre_grad_one = jnp.where(inside(3, rows_grad), slope, 0.0)
    grad_zero = three_rows(backward[0], three_columns(pre_grad_one, cols), cols).astype(BF16)
    pre_one[...] = pre_grad_one[:, rim - 3 * cols : rim - 3 * cols + own].astype(BF16)
    pre_two[...] = pre_grad_two[:, rim - 2 * cols : rim - 2 * cols + own].astype(BF16)

    share = sums.shape[0]
    taps = 9 * channels
    for layer, (pre, columns, offset) in enumerate(((pre_one, columns_zero, rim), (pre_two, columns_one, rim - cols))):

        @pl.when(core == layer)
        def _(pre=pre, columns=columns, offset=offset):
            stacked = jnp.concatenate(
                [columns[:, offset + (a - 1) * cols : offset + (a - 1) * cols + own] for a in range(3)], axis=0
            )
            rows = pre[pl.ds(pl.multiple_of(half * share, 16), share), :]
            sums[:, :taps] = lax.dot_general(rows, stacked, NT, preferred_element_type=F32)

    grads[...] = grad_zero
    gradient[...] = sum(
        lax.dot_general(
            grads[:, pl.ds(pl.multiple_of(at * piece, 128), piece)], seen[...], NT, preferred_element_type=F32
        )
        for at, seen in ((core, own_context), (1 - core, their_context))
    )


def network(place, maps, forward, backward, head, own_context, their_context, cols, frame_rows, col_count):
    own = maps[0].shape[1]
    channels = forward.shape[2]
    return pl.pallas_call(
        functools.partial(network_kernel, cols, frame_rows),
        out_shape=(
            jax.ShapeDtypeStruct((head.shape[0], own), F32),
            jax.ShapeDtypeStruct((channels // col_count, 9 * channels), F32),
            jax.ShapeDtypeStruct((channels, own_context.shape[0]), F32),
        ),
        in_specs=[SMEM] + [VMEM] * 8,
        out_specs=(VMEM,) * 3,
        scratch_shapes=[pltpu.VMEM((maps[0].shape[0], 3 * own), BF16)] + [pltpu.VMEM((channels, own), BF16)] * 3,
        compiler_params=PARAMS,
        name="network",
    )(place, *maps, forward, backward, head, own_context, their_context)


def swapped(values, axis):
    size = lax.axis_size(axis)
    return lax.ppermute(values, axis, [(i, i ^ 1) for i in range(size)])


def passed(values, axis, step, wrap):
    size = lax.axis_size(axis)
    pairs = [(i, (i + step) % size) for i in range(size) if wrap or 0 <= i + step < size]
    return lax.ppermute(values, axis, pairs)


def beside(values):
    size, cols = lax.axis_size("tok"), lax.axis_size("col")
    pairs = []
    for at in range(size // 2):
        for core, other in ((0, at ^ 1), (1, ((at + 1) ^ 1) - 1)):
            inside = 0 <= other < size // 2
            for col in range(cols):
                target = (other if inside else at, col if inside or cols == 1 else col ^ 1)
                pairs.append(((2 * at + core) * cols + col, (2 * target[0] + core) * cols + target[1]))
    return lax.ppermute(values, ("tok", "col"), pairs)


def round_ring(values):
    size = lax.axis_size("tok")
    chips = size // 2
    order = [at for at in range(chips) if at == 0 or at % 2 == 1] + [
        at for at in reversed(range(chips)) if at and at % 2 == 0
    ]
    following = {order[at]: order[(at + 1) % chips] for at in range(chips)}
    return lax.ppermute(values, "tok", [(i, 2 * following[i // 2] + i % 2) for i in range(size)])


def everyone(values, axis, stride, count):
    sent = values.astype(BF16)
    terms = [(passed(sent, axis, stride * step, True) if step else sent).astype(F32) for step in range(count)]
    while len(terms) > 1:
        apart = len(terms) // 2
        terms = [terms[at] + terms[at + apart] for at in range(apart)]
    return terms[0]


def sum_frames(values, across):
    size, cols = lax.axis_size("dp"), lax.axis_size("col")
    sent = values.astype(BF16)
    terms = []
    for step in range(size):
        pairs = []
        for i in range(size):
            other = i ^ step if size & (size - 1) == 0 else (i + step) % size
            pairs += [(i * cols + j, other * cols + (j ^ 1 if across else j)) for j in range(cols)]
        moved = lax.ppermute(sent, ("dp", "col"), pairs) if step or across else sent
        terms.append(moved.astype(F32))
    while len(terms) > 1:
        terms = [sum(terms[at : at + 2][1:], terms[at]) for at in range(0, len(terms), 2)]
    return terms[0]


def in_order(core, mine, theirs, axis):
    return jnp.where(
        core == 0, jnp.concatenate([mine, theirs], axis=axis), jnp.concatenate([theirs, mine], axis=axis)
    )


def step(
    tokens, ln_gain, qkv_weight, out_weight, readout_weight, conv_weight, head_weight, holo_cot
):
    frame_rows = tokens[0]
    cotangent = holo_cot[0]
    rows_dev, cols_dev = cotangent.shape[1:]
    tok_count, col_count = lax.axis_size("tok"), lax.axis_size("col")
    chips = tok_count // 2
    tok_at, half = lax.axis_index("tok"), lax.axis_index("col")
    core = lax.rem(tok_at, 2)
    chip_row = (tok_at - core) * rows_dev
    place = jnp.stack([core, half, chip_row, lax.rem(tok_at // 2, 2)]).astype(jnp.int32)
    cols = cols_dev * col_count

    qkv_weight = pltpu.with_memory_space_constraint(qkv_weight, pltpu.HBM)
    gain = ln_gain.astype(F32).reshape(1, -1)
    normed, own_keyed, their_keyed = project((1, 2), place, frame_rows, qkv_weight, gain)
    own_keyed, their_keyed, normed = lax.optimization_barrier((own_keyed, their_keyed, normed))
    got_keyed = swapped(their_keyed, "tok")
    own_queries, their_queries = project((0,), place, normed, qkv_weight)
    queries = (own_queries, swapped(their_queries, "tok"))
    kept = own_keyed.shape[0] * HEAD

    def prepare(conv_weight, out_weight, readout_weight, frame_rows):
        forward, backward = arrange(conv_weight)
        folded = fold(place, out_weight, readout_weight, kept)
        direct = lax.dot_general(readout_weight, frame_rows, (((0,), (1,)), ((), ())), preferred_element_type=F32)
        return (forward, backward, folded, direct)

    def exact_rows(other_cot):
        wide_cot = in_order(half, cotangent, other_cot, 2)
        exact_cot = jnp.concatenate(split3(wide_cot.reshape(wide_cot.shape[0], -1)), axis=0)
        return jnp.pad(exact_cot, ((0, -exact_cot.shape[0] % 16), (0, 0)))

    state, blocks = None, [own_keyed, got_keyed]
    for turn in range(chips):
        arriving = []
        if turn < chips - 1:
            for block in blocks:
                arriving.append(round_ring(block))
        for at, block in enumerate(blocks):
            if turn == chips - 1 and at == 1:
                break
            state = absorb(queries, block, state)
            if at == 0 and turn == chips - 2:
                state, given, own_cot = lax.optimization_barrier(
                    (state, (conv_weight, out_weight, readout_weight, frame_rows), cotangent)
                )
                prepared, other_cot = prepare(*given), swapped(own_cot, "col")
            if at == 1 and turn == chips - 2:
                state, other_cot = lax.optimization_barrier((state, other_cot))
                exact_cot = exact_rows(other_cot)
            if at == 0 and turn == chips - 1:
                state, prepared, exact_cot = lax.optimization_barrier((state, prepared, exact_cot))
            if turn < chips - 2:
                arriving[at], state = lax.optimization_barrier((arriving[at], state))
        blocks = arriving if turn < chips - 1 else blocks
    forward, backward, folded, direct = prepared

    their_context, their_share = closing(1, queries, blocks[1], state, folded)
    own_context, own_share = closing(0, queries, blocks[1], state, folded)
    partial = own_share + swapped(their_share, "tok")
    partial = (partial + jnp.where(half == 0, direct, 0.0)).astype(BF16)
    own_map = (partial.astype(F32) + swapped(partial, "col").astype(F32)).astype(BF16)
    own_map = jnp.concatenate([own_map, exact_cot], axis=0)
    chip_map = jnp.concatenate([own_map, swapped(own_map, "tok")], axis=1)
    near = beside(chip_map)
    rows_chip = 2 * rows_dev
    maps = (chip_map, near, swapped(near, "tok"))
    holo, sums, gradient = network(
        place, maps, forward, backward, head_weight, own_context, their_context, cols, tok_count * rows_dev, col_count
    )
    holo = holo.reshape(-1, rows_chip, cols)
    hologram = lax.dynamic_slice(
        holo, (0, core * rows_dev, half * cols_dev), (holo.shape[0], rows_dev, cols_dev)
    )

    taps_wide = sums.shape[1]
    lanes = 128 * ((taps_wide + 127) // 128)
    rows = sums.shape[0]
    pieces = gradient.shape[0] // rows
    folded_gradient = [gradient[at * rows : (at + 1) * rows] for at in range(pieces)]
    sent = jnp.concatenate([jnp.pad(sums, ((0, 0), (0, lanes - taps_wide))), *folded_gradient], axis=1)
    summed = everyone(sent, "tok", 2, chips)
    own_terms = sum_frames(summed, False)
    far_terms = sum_frames(summed[:, :taps_wide], True)
    wide = gradient.shape[1]
    own_small = jnp.concatenate(
        [own_terms[:, lanes + at * wide : lanes + (at + 1) * wide] for at in range(pieces)], axis=0
    )
    small = in_order(core, own_small, swapped(own_small, "tok"), 1)
    out_grad = lax.dot_general(
        small, readout_weight.astype(F32), (((0,), (1,)), ((), ())), precision=lax.Precision.HIGHEST
    )
    layer_grad = in_order(half, own_terms[:, :taps_wide], far_terms, 0)
    conv_grad = in_order(core, layer_grad[None], swapped(layer_grad, "tok")[None], 0)
    return (hologram[None], conv_grad, out_grad)


def solution(mesh):
    in_specs = (
        P("dp", "tok", None),
        P(),
        P(None, None, "col"),
        P("col", None),
        P(),
        P(),
        P(),
        P("dp", None, "tok", "col"),
    )
    out_specs = (P("dp", None, "tok", "col"), P(), P("col", None))
    return jax.shard_map(step, mesh=mesh, in_specs=in_specs, out_specs=out_specs, check_vma=False)
```

```python
import functools

import jax
import jax.numpy as jnp
from jax import lax
from jax.experimental import pallas as pl
from jax.experimental.pallas import tpu as pltpu
from jax.sharding import PartitionSpec as P


HEAD = 64
EPSILON = 1e-05
BF16 = jnp.bfloat16
F32 = jnp.float32
VMEM = pl.BlockSpec(memory_space=pltpu.VMEM)
SMEM = pl.BlockSpec(memory_space=pltpu.SMEM)
PARAMS = pltpu.CompilerParams(vmem_limit_bytes=16 * 2**20)
NT = (((1,), (1,)), ((), ()))


def dot(a, b):
    return jnp.dot(a, b, preferred_element_type=F32)


def split3(values):
    high = values.astype(BF16)
    rest = values - high.astype(F32)
    mid = rest.astype(BF16)
    low = (rest - mid.astype(F32)).astype(BF16)
    return high, mid, low


def normalize_kernel(tokens, gain, normed):
    values = tokens[...].astype(F32)
    center = values - jnp.mean(values, axis=-1, keepdims=True)
    spread = jnp.mean(center * center, axis=-1, keepdims=True)
    normed[...] = (center * lax.rsqrt(spread + EPSILON) * gain[...]).astype(BF16)


def normalize(tokens, gain):
    return pl.pallas_call(
        normalize_kernel,
        out_shape=jax.ShapeDtypeStruct(tokens.shape, BF16),
        in_specs=[VMEM, VMEM],
        out_specs=VMEM,
        compiler_params=PARAMS,
        name="normalize",
    )(tokens, gain)


def project_kernel(members, place, normed, weight, mine, theirs, turned):
    core = place[0]
    kept = mine.shape[0] * HEAD
    rows = normed[...]
    for at, member in enumerate(members):
        product = dot(rows, weight[member]).astype(BF16)
        if member == 0:
            product = product * jnp.asarray(1.0 / HEAD**0.5, BF16)
        turned[at] = product.T
        for which, out in ((1 - core, theirs), (core, mine)):
            for head in range(mine.shape[0]):
                start = pl.multiple_of(which * kept + head * HEAD, HEAD)
                out[head, at * HEAD : (at + 1) * HEAD, :] = turned[at, pl.ds(start, HEAD), :]


def project_side_kernel(members, their, place, normed, weight, out):
    kept = out.shape[0] * HEAD
    which = 1 - place[0] if their else place[0]
    for at, member in enumerate(members):
        part = weight[member, :, pl.ds(pl.multiple_of(which * kept, 128), kept)]
        columns = dot(normed[...], part).astype(BF16).T
        for head in range(out.shape[0]):
            out[head, at * HEAD : (at + 1) * HEAD, :] = columns[head * HEAD : (head + 1) * HEAD, :]


def project_side(members, their, place, normed, weight):
    shape = (weight.shape[2] // HEAD // 2, len(members) * HEAD, normed.shape[0])
    return pl.pallas_call(
        functools.partial(project_side_kernel, members, their),
        out_shape=jax.ShapeDtypeStruct(shape, BF16),
        in_specs=[SMEM, VMEM, VMEM],
        out_specs=VMEM,
        compiler_params=PARAMS,
        name="project_side",
    )(place, normed, weight)


def project(members, place, normed, weight):
    count, length = weight.shape[2] // HEAD // 2, normed.shape[0]
    shape = jax.ShapeDtypeStruct((count, len(members) * HEAD, length), BF16)
    return pl.pallas_call(
        functools.partial(project_kernel, members),
        out_shape=(shape, shape),
        in_specs=[SMEM, VMEM, VMEM],
        out_specs=(VMEM,) * 2,
        scratch_shapes=[pltpu.VMEM((len(members), weight.shape[2], length), BF16)],
        compiler_params=PARAMS,
        name="project",
    )(place, normed, weight)


def attend(queries, block, running, best):
    length = block.shape[1]
    keys = block[:HEAD].T
    values = jnp.concatenate([block[HEAD:], jnp.ones((16, length), BF16)], axis=0)
    depth = min(512, length)
    for below in range(0, length, depth):
        scores = dot(keys[below : below + depth], queries)
        raised_top = jnp.max(scores, axis=0, keepdims=True)
        if best is not None:
            raised_top = jnp.maximum(best, raised_top)
        weights = jnp.exp(scores - raised_top).astype(BF16)
        added = dot(values[:, below : below + depth], weights)
        running = added if best is None else running * jnp.exp(best - raised_top) + added
        best = raised_top
    return running, best


def absorb_kernel(first, own, got, block, *refs):
    carried, carried_top = (None, None) if first else refs[:2]
    out, top = refs[-2:]
    length = own.shape[2]
    for head in range(own.shape[0]):
        for side, queries in enumerate((own, got)):
            where = slice(side * length, (side + 1) * length)
            running = None if first else carried[head, :, where]
            best = None if first else carried_top[head, 0:1, where]
            running, best = attend(queries[head], block[head], running, best)
            out[head, :, where] = running
            top[head, :, where] = jnp.broadcast_to(best, (8, length))


def absorb(queries, block, state):
    heads, _, length = queries[0].shape
    shapes = tuple(jax.ShapeDtypeStruct((heads, rows, 2 * length), F32) for rows in (HEAD + 16, 8))
    first = state is None
    return pl.pallas_call(
        functools.partial(absorb_kernel, first),
        out_shape=shapes,
        in_specs=[VMEM] * (3 if first else 5),
        out_specs=(VMEM, VMEM),
        input_output_aliases={} if first else {3: 0, 4: 1},
        compiler_params=PARAMS,
        name="absorb",
    )(*queries, block, *(() if first else state))


def closing_kernel(side, queries, block, carried, carried_top, folded, context, share):
    length = context.shape[1]
    where = slice(side * length, (side + 1) * length)
    for head in range(queries.shape[0]):
        running, _ = attend(queries[head], block[head], carried[head, :, where], carried_top[head, 0:1, where])
        context[head * HEAD : (head + 1) * HEAD, :] = (running[:HEAD] / running[HEAD : HEAD + 1]).astype(BF16)
    whole = context[...]
    share[...] = sum(dot(part, whole) for part in split3(folded[...]))


def closing(side, queries, block, state, folded):
    heads, _, length = queries[side].shape
    return pl.pallas_call(
        functools.partial(closing_kernel, side),
        out_shape=(
            jax.ShapeDtypeStruct((heads * HEAD, length), BF16),
            jax.ShapeDtypeStruct((folded.shape[0], length), F32),
        ),
        in_specs=[VMEM] * 5,
        out_specs=(VMEM, VMEM),
        compiler_params=PARAMS,
        name="closing",
    )(queries[side], block, *state, folded)


def arrange_kernel(weight, forward, backward):
    channels = weight.shape[1]
    for layer in range(weight.shape[0]):
        taps = weight[layer]
        turned_taps = taps.astype(F32).T
        for row in range(3):
            forward[layer, row] = taps[:, row * 3 * channels : (row + 1) * 3 * channels]
            at = [((2 - row) * 3 + 2 - column) * channels for column in range(3)]
            backward[layer, row] = jnp.concatenate(
                [turned_taps[start : start + channels, :] for start in at], axis=1
            ).astype(BF16)


def arrange(weight):
    layers, channels, wide = weight.shape
    shape = jax.ShapeDtypeStruct((layers, 3, channels, wide // 3), BF16)
    return pl.pallas_call(
        arrange_kernel,
        out_shape=(shape, shape),
        in_specs=[VMEM],
        out_specs=(VMEM, VMEM),
        compiler_params=PARAMS,
        name="arrange",
    )(weight)


def turned(values, step):
    return pltpu.roll(values, step % values.shape[1], 1)


def three_columns(values, cols):
    cells = values.shape[1]
    column = lax.rem(lax.broadcasted_iota(jnp.int32, (1, cells), 1), cols)
    wide = values.astype(F32)
    left = jnp.where(column == 0, 0.0, turned(wide, 1)).astype(BF16)
    right = jnp.where(column == cols - 1, 0.0, turned(wide, -1)).astype(BF16)
    return jnp.concatenate([left, values.astype(BF16), right], axis=0)


def three_rows(weights, columns, cols):
    cells = columns.shape[1] - 2 * cols
    return sum(dot(weights[a], columns[:, a * cols : a * cols + cells]) for a in range(3))


def network_kernel(
    cols, frame_rows, place, chip_map, near, far, forward, backward, head, own_context, their_context, holo, sums,
    gradient, hidden, pre_one, pre_two, grads,
):
    core, half, row_at = place[0], place[1], place[2]
    own = chip_map.shape[1]
    cells = hidden.shape[1]
    rim = (cells - own) // 2
    row_count = cells // cols
    above = rim // cols
    first_row = row_at - above
    piece = own // 2
    down = (core == place[3]).astype(jnp.int32)
    for source, base, lead in ((chip_map, own, core), (near, 2 * own * down, core), (far, 2 * own * (1 - down), 1 - core)):
        for side in range(2):
            start = pl.multiple_of(base + lax.rem(lead + side, 2) * piece, 128)
            hidden[:, pl.ds(start, piece)] = source[:, side * piece : (side + 1) * piece]

    def inside(start_row, rows):
        lane = lax.broadcasted_iota(jnp.int32, (1, rows * cols), 1)
        frame_lane = lane + (first_row + start_row) * cols
        return jnp.logical_and(frame_lane >= 0, frame_lane < frame_rows * cols)

    channels, outputs = forward.shape[2], head.shape[0]
    columns_zero = three_columns(jnp.where(inside(0, row_count), hidden[:channels, :].astype(F32), 0.0), cols)
    first = three_rows(forward[0], columns_zero, cols)
    rows_one = row_count - 2
    sigmoid_first = jax.nn.sigmoid(first)
    one = jnp.where(inside(1, rows_one), first * sigmoid_first, 0.0)
    columns_one = three_columns(one, cols)
    second = three_rows(forward[1], columns_one, cols)
    rows_two = row_count - 4
    sigmoid_two = jax.nn.sigmoid(second)
    two = (second * sigmoid_two).astype(BF16)
    holo[...] = dot(head[...], two[:, rim - 2 * cols : rim - 2 * cols + own])
    pieces = hidden[channels:, 2 * cols : cells - 2 * cols].astype(F32)
    cotangent = pieces[:outputs] + pieces[outputs : 2 * outputs] + pieces[2 * outputs : 3 * outputs]
    wide_head = head[...].astype(F32).T
    grad_two = sum(wide_head[:, at : at + 1] * cotangent[at : at + 1, :] for at in range(outputs)).astype(BF16)
    slope = grad_two.astype(F32) * sigmoid_two * (1.0 + second * (1.0 - sigmoid_two))
    pre_grad_two = jnp.where(inside(2, rows_two), slope, 0.0)
    grad_one = three_rows(backward[1], three_columns(pre_grad_two, cols), cols).astype(BF16)
    rows_grad = row_count - 6
    middle = first[:, 2 * cols : 2 * cols + rows_grad * cols]
    sigmoid_one = sigmoid_first[:, 2 * cols : 2 * cols + rows_grad * cols]
    slope = grad_one.astype(F32) * sigmoid_one * (1.0 + middle * (1.0 - sigmoid_one))
    pre_grad_one = jnp.where(inside(3, rows_grad), slope, 0.0)
    grad_zero = three_rows(backward[0], three_columns(pre_grad_one, cols), cols).astype(BF16)
    pre_one[...] = pre_grad_one[:, rim - 3 * cols : rim - 3 * cols + own].astype(BF16)
    pre_two[...] = pre_grad_two[:, rim - 2 * cols : rim - 2 * cols + own].astype(BF16)

    share = sums.shape[0]
    taps = 9 * channels
    for layer, (pre, columns, offset) in enumerate(((pre_one, columns_zero, rim), (pre_two, columns_one, rim - cols))):

        @pl.when(core == layer)
        def _(pre=pre, columns=columns, offset=offset):
            stacked = jnp.concatenate(
                [columns[:, offset + (a - 1) * cols : offset + (a - 1) * cols + own] for a in range(3)], axis=0
            )
            rows = pre[pl.ds(pl.multiple_of(half * share, 16), share), :]
            sums[:, :taps] = lax.dot_general(rows, stacked, NT, preferred_element_type=F32)

    grads[...] = grad_zero
    gradient[...] = sum(
        lax.dot_general(
            grads[:, pl.ds(pl.multiple_of(at * piece, 128), piece)], seen[...], NT, preferred_element_type=F32
        )
        for at, seen in ((core, own_context), (1 - core, their_context))
    )


def network(place, maps, forward, backward, head, own_context, their_context, cols, frame_rows, col_count):
    own = maps[0].shape[1]
    channels = forward.shape[2]
    return pl.pallas_call(
        functools.partial(network_kernel, cols, frame_rows),
        out_shape=(
            jax.ShapeDtypeStruct((head.shape[0], own), F32),
            jax.ShapeDtypeStruct((channels // col_count, 9 * channels), F32),
            jax.ShapeDtypeStruct((channels, own_context.shape[0]), F32),
        ),
        in_specs=[SMEM] + [VMEM] * 8,
        out_specs=(VMEM,) * 3,
        scratch_shapes=[pltpu.VMEM((maps[0].shape[0], 3 * own), BF16)] + [pltpu.VMEM((channels, own), BF16)] * 3,
        compiler_params=PARAMS,
        name="network",
    )(place, *maps, forward, backward, head, own_context, their_context)


def swapped(values, axis):
    size = lax.axis_size(axis)
    return lax.ppermute(values, axis, [(i, i ^ 1) for i in range(size)])


def passed(values, axis, step, wrap):
    size = lax.axis_size(axis)
    pairs = [(i, (i + step) % size) for i in range(size) if wrap or 0 <= i + step < size]
    return lax.ppermute(values, axis, pairs)


def beside(values):
    size, cols = lax.axis_size("tok"), lax.axis_size("col")
    pairs = []
    for at in range(size // 2):
        for core, other in ((0, at ^ 1), (1, ((at + 1) ^ 1) - 1)):
            inside = 0 <= other < size // 2
            for col in range(cols):
                target = (other if inside else at, col if inside or cols == 1 else col ^ 1)
                pairs.append(((2 * at + core) * cols + col, (2 * target[0] + core) * cols + target[1]))
    return lax.ppermute(values, ("tok", "col"), pairs)


def round_ring(values):
    size = lax.axis_size("tok")
    chips = size // 2
    order = [at for at in range(chips) if at == 0 or at % 2 == 1] + [
        at for at in reversed(range(chips)) if at and at % 2 == 0
    ]
    following = {order[at]: order[(at + 1) % chips] for at in range(chips)}
    return lax.ppermute(values, "tok", [(i, 2 * following[i // 2] + i % 2) for i in range(size)])


def everyone(values, axis, stride, count):
    sent = values.astype(BF16)
    terms = [(passed(sent, axis, stride * step, True) if step else sent).astype(F32) for step in range(count)]
    while len(terms) > 1:
        apart = len(terms) // 2
        terms = [terms[at] + terms[at + apart] for at in range(apart)]
    return terms[0]


def sum_frames(values, across):
    size, cols = lax.axis_size("dp"), lax.axis_size("col")
    sent = values.astype(BF16)
    terms = []
    for step in range(size):
        pairs = []
        for i in range(size):
            other = i ^ step if size & (size - 1) == 0 else (i + step) % size
            pairs += [(i * cols + j, other * cols + (j ^ 1 if across else j)) for j in range(cols)]
        moved = lax.ppermute(sent, ("dp", "col"), pairs) if step or across else sent
        terms.append(moved.astype(F32))
    while len(terms) > 1:
        terms = [sum(terms[at : at + 2][1:], terms[at]) for at in range(0, len(terms), 2)]
    return terms[0]


def in_order(core, mine, theirs, axis):
    return jnp.where(
        core == 0, jnp.concatenate([mine, theirs], axis=axis), jnp.concatenate([theirs, mine], axis=axis)
    )


def step(
    tokens, ln_gain, qkv_weight, out_weight, readout_weight, conv_weight, head_weight, holo_cot
):
    frame_rows = tokens[0]
    cotangent = holo_cot[0]
    rows_dev, cols_dev = cotangent.shape[1:]
    tok_count, col_count = lax.axis_size("tok"), lax.axis_size("col")
    chips = tok_count // 2
    tok_at, half = lax.axis_index("tok"), lax.axis_index("col")
    core = lax.rem(tok_at, 2)
    chip_row = (tok_at - core) * rows_dev
    place = jnp.stack([core, half, chip_row, lax.rem(tok_at // 2, 2)]).astype(jnp.int32)
    cols = cols_dev * col_count

    gain, qkv_weight, out_weight = lax.optimization_barrier(
        (ln_gain.astype(F32).reshape(1, -1), qkv_weight, out_weight)
    )
    normed = normalize(frame_rows, gain)
    own_keyed = project_side((1, 2), False, place, normed, qkv_weight)
    own_keyed, normed = lax.optimization_barrier((own_keyed, normed))
    their_keyed = project_side((1, 2), True, place, normed, qkv_weight)
    their_keyed, normed = lax.optimization_barrier((their_keyed, normed))
    got_keyed = swapped(their_keyed, "tok")
    own_queries, their_queries = project((0,), place, normed, qkv_weight)
    queries = (own_queries, swapped(their_queries, "tok"))
    kept = own_keyed.shape[0] * HEAD

    def prepare(conv_weight, out_weight, readout_weight, frame_rows):
        forward, backward = arrange(conv_weight)
        own_out = lax.dynamic_slice_in_dim(out_weight, core * kept, kept, 0)
        folded = lax.dot_general(readout_weight, own_out, (((0,), (1,)), ((), ())), preferred_element_type=F32)
        direct = lax.dot_general(readout_weight, frame_rows, (((0,), (1,)), ((), ())), preferred_element_type=F32)
        return (forward, backward, folded, direct)

    def exact_rows(other_cot):
        wide_cot = in_order(half, cotangent, other_cot, 2)
        exact_cot = jnp.concatenate(split3(wide_cot.reshape(wide_cot.shape[0], -1)), axis=0)
        return jnp.pad(exact_cot, ((0, -exact_cot.shape[0] % 16), (0, 0)))

    state, blocks = None, [own_keyed, got_keyed]
    for turn in range(chips):
        arriving = []
        if turn < chips - 1:
            for block in blocks:
                arriving.append(round_ring(block))
        for at, block in enumerate(blocks):
            if turn == chips - 1 and at == 1:
                break
            state = absorb(queries, block, state)
            if at == 0 and turn == chips - 2:
                state, given, own_cot = lax.optimization_barrier(
                    (state, (conv_weight, out_weight, readout_weight, frame_rows), cotangent)
                )
                prepared, other_cot = prepare(*given), swapped(own_cot, "col")
            if at == 1 and turn == chips - 2:
                state, other_cot = lax.optimization_barrier((state, other_cot))
                exact_cot = exact_rows(other_cot)
            if at == 0 and turn == chips - 1:
                state, prepared, exact_cot = lax.optimization_barrier((state, prepared, exact_cot))
            if turn < chips - 2:
                arriving[at], state = lax.optimization_barrier((arriving[at], state))
        blocks = arriving if turn < chips - 1 else blocks
    forward, backward, folded, direct = prepared

    their_context, their_share = closing(1, queries, blocks[1], state, folded)
    own_context, own_share = closing(0, queries, blocks[1], state, folded)
    partial = own_share + swapped(their_share, "tok")
    partial = (partial + jnp.where(half == 0, direct, 0.0)).astype(BF16)
    own_map = (partial.astype(F32) + swapped(partial, "col").astype(F32)).astype(BF16)
    own_map = jnp.concatenate([own_map, exact_cot], axis=0)
    chip_map = jnp.concatenate([own_map, swapped(own_map, "tok")], axis=1)
    near = beside(chip_map)
    rows_chip = 2 * rows_dev
    maps = (chip_map, near, swapped(near, "tok"))
    holo, sums, gradient = network(
        place, maps, forward, backward, head_weight, own_context, their_context, cols, tok_count * rows_dev, col_count
    )
    holo = holo.reshape(-1, rows_chip, cols)
    hologram = lax.dynamic_slice(
        holo, (0, core * rows_dev, half * cols_dev), (holo.shape[0], rows_dev, cols_dev)
    )

    taps_wide = sums.shape[1]
    lanes = 128 * ((taps_wide + 127) // 128)
    rows = sums.shape[0]
    pieces = gradient.shape[0] // rows
    folded_gradient = [gradient[at * rows : (at + 1) * rows] for at in range(pieces)]
    sent = jnp.concatenate([jnp.pad(sums, ((0, 0), (0, lanes - taps_wide))), *folded_gradient], axis=1)
    summed = everyone(sent, "tok", 2, chips)
    own_terms = sum_frames(summed, False)
    far_terms = sum_frames(summed[:, :taps_wide], True)
    wide = gradient.shape[1]
    own_small = jnp.concatenate(
        [own_terms[:, lanes + at * wide : lanes + (at + 1) * wide] for at in range(pieces)], axis=0
    )
    small = in_order(core, own_small, swapped(own_small, "tok"), 1)
    out_grad = lax.dot_general(
        small, readout_weight.astype(F32), (((0,), (1,)), ((), ())), precision=lax.Precision.HIGHEST
    )
    layer_grad = in_order(half, own_terms[:, :taps_wide], far_terms, 0)
    conv_grad = in_order(core, layer_grad[None], swapped(layer_grad, "tok")[None], 0)
    return (hologram[None], conv_grad, out_grad)


def solution(mesh):
    in_specs = (
        P("dp", "tok", None),
        P(),
        P(None, None, "col"),
        P("col", None),
        P(),
        P(),
        P(),
        P("dp", None, "tok", "col"),
    )
    out_specs = (P("dp", None, "tok", "col"), P(), P("col", None))
    return jax.shard_map(step, mesh=mesh, in_specs=in_specs, out_specs=out_specs, check_vma=False)
```

```python
import functools

import jax
import jax.numpy as jnp
from jax import lax
from jax.experimental import pallas as pl
from jax.experimental.pallas import tpu as pltpu
from jax.sharding import PartitionSpec as P


HEAD = 64
EPSILON = 1e-05
BF16 = jnp.bfloat16
F32 = jnp.float32
VMEM = pl.BlockSpec(memory_space=pltpu.VMEM)
SMEM = pl.BlockSpec(memory_space=pltpu.SMEM)
PARAMS = pltpu.CompilerParams(vmem_limit_bytes=16 * 2**20)
NT = (((1,), (1,)), ((), ()))


def dot(a, b):
    return jnp.dot(a, b, preferred_element_type=F32)


def split3(values):
    high = values.astype(BF16)
    rest = values - high.astype(F32)
    mid = rest.astype(BF16)
    low = (rest - mid.astype(F32)).astype(BF16)
    return high, mid, low


def normalize_kernel(tokens, gain, normed):
    values = tokens[...].astype(F32)
    center = values - jnp.mean(values, axis=-1, keepdims=True)
    spread = jnp.mean(center * center, axis=-1, keepdims=True)
    normed[...] = (center * lax.rsqrt(spread + EPSILON) * gain[...]).astype(BF16)


def normalize(tokens, gain):
    return pl.pallas_call(
        normalize_kernel,
        out_shape=jax.ShapeDtypeStruct(tokens.shape, BF16),
        in_specs=[VMEM, VMEM],
        out_specs=VMEM,
        compiler_params=PARAMS,
        name="normalize",
    )(tokens, gain)


def project_kernel(members, place, normed, weight, mine, theirs, turned):
    core = place[0]
    kept = mine.shape[0] * HEAD
    rows = normed[...]
    for at, member in enumerate(members):
        product = dot(rows, weight[member]).astype(BF16)
        if member == 0:
            product = product * jnp.asarray(1.0 / HEAD**0.5, BF16)
        turned[at] = product.T
        for which, out in ((1 - core, theirs), (core, mine)):
            for head in range(mine.shape[0]):
                start = pl.multiple_of(which * kept + head * HEAD, HEAD)
                out[head, at * HEAD : (at + 1) * HEAD, :] = turned[at, pl.ds(start, HEAD), :]


def project(members, place, normed, weight):
    count, length = weight.shape[2] // HEAD // 2, normed.shape[0]
    shape = jax.ShapeDtypeStruct((count, len(members) * HEAD, length), BF16)
    return pl.pallas_call(
        functools.partial(project_kernel, members),
        out_shape=(shape, shape),
        in_specs=[SMEM, VMEM, VMEM],
        out_specs=(VMEM,) * 2,
        scratch_shapes=[pltpu.VMEM((len(members), weight.shape[2], length), BF16)],
        compiler_params=PARAMS,
        name="project",
    )(place, normed, weight)


def attend(queries, block, running, best):
    length = block.shape[1]
    keys = block[:HEAD].T
    values = jnp.concatenate([block[HEAD:], jnp.ones((16, length), BF16)], axis=0)
    depth = min(512, length)
    for below in range(0, length, depth):
        scores = dot(keys[below : below + depth], queries)
        raised_top = jnp.max(scores, axis=0, keepdims=True)
        if best is not None:
            raised_top = jnp.maximum(best, raised_top)
        weights = jnp.exp(scores - raised_top).astype(BF16)
        added = dot(values[:, below : below + depth], weights)
        running = added if best is None else running * jnp.exp(best - raised_top) + added
        best = raised_top
    return running, best


def absorb_kernel(first, own, got, block, *refs):
    carried, carried_top = (None, None) if first else refs[:2]
    out, top = refs[-2:]
    length = own.shape[2]
    for head in range(own.shape[0]):
        for side, queries in enumerate((own, got)):
            where = slice(side * length, (side + 1) * length)
            running = None if first else carried[head, :, where]
            best = None if first else carried_top[head, 0:1, where]
            running, best = attend(queries[head], block[head], running, best)
            out[head, :, where] = running
            top[head, :, where] = jnp.broadcast_to(best, (8, length))


def absorb(queries, block, state):
    heads, _, length = queries[0].shape
    shapes = tuple(jax.ShapeDtypeStruct((heads, rows, 2 * length), F32) for rows in (HEAD + 16, 8))
    first = state is None
    return pl.pallas_call(
        functools.partial(absorb_kernel, first),
        out_shape=shapes,
        in_specs=[VMEM] * (3 if first else 5),
        out_specs=(VMEM, VMEM),
        input_output_aliases={} if first else {3: 0, 4: 1},
        compiler_params=PARAMS,
        name="absorb",
    )(*queries, block, *(() if first else state))


def closing_kernel(side, queries, block, carried, carried_top, folded, context, share):
    length = context.shape[1]
    where = slice(side * length, (side + 1) * length)
    for head in range(queries.shape[0]):
        running, _ = attend(queries[head], block[head], carried[head, :, where], carried_top[head, 0:1, where])
        context[head * HEAD : (head + 1) * HEAD, :] = (running[:HEAD] / running[HEAD : HEAD + 1]).astype(BF16)
    whole = context[...]
    share[...] = sum(dot(part, whole) for part in split3(folded[...]))


def closing(side, queries, block, state, folded):
    heads, _, length = queries[side].shape
    return pl.pallas_call(
        functools.partial(closing_kernel, side),
        out_shape=(
            jax.ShapeDtypeStruct((heads * HEAD, length), BF16),
            jax.ShapeDtypeStruct((folded.shape[0], length), F32),
        ),
        in_specs=[VMEM] * 5,
        out_specs=(VMEM, VMEM),
        compiler_params=PARAMS,
        name="closing",
    )(queries[side], block, *state, folded)


def arrange_kernel(weight, forward, backward):
    channels = weight.shape[1]
    for layer in range(weight.shape[0]):
        taps = weight[layer]
        turned_taps = taps.astype(F32).T
        for row in range(3):
            forward[layer, row] = taps[:, row * 3 * channels : (row + 1) * 3 * channels]
            at = [((2 - row) * 3 + 2 - column) * channels for column in range(3)]
            backward[layer, row] = jnp.concatenate(
                [turned_taps[start : start + channels, :] for start in at], axis=1
            ).astype(BF16)


def arrange(weight):
    layers, channels, wide = weight.shape
    shape = jax.ShapeDtypeStruct((layers, 3, channels, wide // 3), BF16)
    return pl.pallas_call(
        arrange_kernel,
        out_shape=(shape, shape),
        in_specs=[VMEM],
        out_specs=(VMEM, VMEM),
        compiler_params=PARAMS,
        name="arrange",
    )(weight)


def turned(values, step):
    return pltpu.roll(values, step % values.shape[1], 1)


def three_columns(values, cols):
    cells = values.shape[1]
    column = lax.rem(lax.broadcasted_iota(jnp.int32, (1, cells), 1), cols)
    wide = values.astype(F32)
    left = jnp.where(column == 0, 0.0, turned(wide, 1)).astype(BF16)
    right = jnp.where(column == cols - 1, 0.0, turned(wide, -1)).astype(BF16)
    return jnp.concatenate([left, values.astype(BF16), right], axis=0)


def three_rows(weights, columns, cols):
    cells = columns.shape[1] - 2 * cols
    return sum(dot(weights[a], columns[:, a * cols : a * cols + cells]) for a in range(3))


def network_kernel(
    cols, frame_rows, place, chip_map, near, far, forward, backward, head, own_context, their_context, holo, sums,
    gradient, hidden, pre_one, pre_two, grads,
):
    core, half, row_at = place[0], place[1], place[2]
    own = chip_map.shape[1]
    cells = hidden.shape[1]
    rim = (cells - own) // 2
    row_count = cells // cols
    above = rim // cols
    first_row = row_at - above
    piece = own // 2
    down = (core == place[3]).astype(jnp.int32)
    for source, base, lead in ((chip_map, own, core), (near, 2 * own * down, core), (far, 2 * own * (1 - down), 1 - core)):
        for side in range(2):
            start = pl.multiple_of(base + lax.rem(lead + side, 2) * piece, 128)
            hidden[:, pl.ds(start, piece)] = source[:, side * piece : (side + 1) * piece]

    def inside(start_row, rows):
        lane = lax.broadcasted_iota(jnp.int32, (1, rows * cols), 1)
        frame_lane = lane + (first_row + start_row) * cols
        return jnp.logical_and(frame_lane >= 0, frame_lane < frame_rows * cols)

    channels, outputs = forward.shape[2], head.shape[0]
    columns_zero = three_columns(jnp.where(inside(0, row_count), hidden[:channels, :].astype(F32), 0.0), cols)
    first = three_rows(forward[0], columns_zero, cols)
    rows_one = row_count - 2
    sigmoid_first = jax.nn.sigmoid(first)
    one = jnp.where(inside(1, rows_one), first * sigmoid_first, 0.0)
    columns_one = three_columns(one, cols)
    second = three_rows(forward[1], columns_one, cols)
    rows_two = row_count - 4
    sigmoid_two = jax.nn.sigmoid(second)
    two = (second * sigmoid_two).astype(BF16)
    holo[...] = dot(head[...], two[:, rim - 2 * cols : rim - 2 * cols + own])
    pieces = hidden[channels:, 2 * cols : cells - 2 * cols].astype(F32)
    cotangent = pieces[:outputs] + pieces[outputs : 2 * outputs] + pieces[2 * outputs : 3 * outputs]
    wide_head = head[...].astype(F32).T
    grad_two = sum(wide_head[:, at : at + 1] * cotangent[at : at + 1, :] for at in range(outputs)).astype(BF16)
    slope = grad_two.astype(F32) * sigmoid_two * (1.0 + second * (1.0 - sigmoid_two))
    pre_grad_two = jnp.where(inside(2, rows_two), slope, 0.0)
    grad_one = three_rows(backward[1], three_columns(pre_grad_two, cols), cols).astype(BF16)
    rows_grad = row_count - 6
    middle = first[:, 2 * cols : 2 * cols + rows_grad * cols]
    sigmoid_one = sigmoid_first[:, 2 * cols : 2 * cols + rows_grad * cols]
    slope = grad_one.astype(F32) * sigmoid_one * (1.0 + middle * (1.0 - sigmoid_one))
    pre_grad_one = jnp.where(inside(3, rows_grad), slope, 0.0)
    grad_zero = three_rows(backward[0], three_columns(pre_grad_one, cols), cols).astype(BF16)
    pre_one[...] = pre_grad_one[:, rim - 3 * cols : rim - 3 * cols + own].astype(BF16)
    pre_two[...] = pre_grad_two[:, rim - 2 * cols : rim - 2 * cols + own].astype(BF16)

    share = sums.shape[0]
    taps = 9 * channels
    for layer, (pre, columns, offset) in enumerate(((pre_one, columns_zero, rim), (pre_two, columns_one, rim - cols))):

        @pl.when(core == layer)
        def _(pre=pre, columns=columns, offset=offset):
            stacked = jnp.concatenate(
                [columns[:, offset + (a - 1) * cols : offset + (a - 1) * cols + own] for a in range(3)], axis=0
            )
            rows = pre[pl.ds(pl.multiple_of(half * share, 16), share), :]
            sums[:, :taps] = lax.dot_general(rows, stacked, NT, preferred_element_type=F32)

    grads[...] = grad_zero
    gradient[...] = sum(
        lax.dot_general(
            grads[:, pl.ds(pl.multiple_of(at * piece, 128), piece)], seen[...], NT, preferred_element_type=F32
        )
        for at, seen in ((core, own_context), (1 - core, their_context))
    )


def network(place, maps, forward, backward, head, own_context, their_context, cols, frame_rows, col_count):
    own = maps[0].shape[1]
    channels = forward.shape[2]
    return pl.pallas_call(
        functools.partial(network_kernel, cols, frame_rows),
        out_shape=(
            jax.ShapeDtypeStruct((head.shape[0], own), F32),
            jax.ShapeDtypeStruct((channels // col_count, 9 * channels), F32),
            jax.ShapeDtypeStruct((channels, own_context.shape[0]), F32),
        ),
        in_specs=[SMEM] + [VMEM] * 8,
        out_specs=(VMEM,) * 3,
        scratch_shapes=[pltpu.VMEM((maps[0].shape[0], 3 * own), BF16)] + [pltpu.VMEM((channels, own), BF16)] * 3,
        compiler_params=PARAMS,
        name="network",
    )(place, *maps, forward, backward, head, own_context, their_context)


def swapped(values, axis):
    size = lax.axis_size(axis)
    return lax.ppermute(values, axis, [(i, i ^ 1) for i in range(size)])


def passed(values, axis, step, wrap):
    size = lax.axis_size(axis)
    pairs = [(i, (i + step) % size) for i in range(size) if wrap or 0 <= i + step < size]
    return lax.ppermute(values, axis, pairs)


def beside(values):
    size, cols = lax.axis_size("tok"), lax.axis_size("col")
    pairs = []
    for at in range(size // 2):
        for core, other in ((0, at ^ 1), (1, ((at + 1) ^ 1) - 1)):
            inside = 0 <= other < size // 2
            for col in range(cols):
                target = (other if inside else at, col if inside or cols == 1 else col ^ 1)
                pairs.append(((2 * at + core) * cols + col, (2 * target[0] + core) * cols + target[1]))
    return lax.ppermute(values, ("tok", "col"), pairs)


def round_ring(values):
    size = lax.axis_size("tok")
    chips = size // 2
    order = [at for at in range(chips) if at == 0 or at % 2 == 1] + [
        at for at in reversed(range(chips)) if at and at % 2 == 0
    ]
    following = {order[at]: order[(at + 1) % chips] for at in range(chips)}
    return lax.ppermute(values, "tok", [(i, 2 * following[i // 2] + i % 2) for i in range(size)])


def everyone(values, axis, stride, count):
    sent = values.astype(BF16)
    terms = [sent.astype(F32)]
    for step in range(1, count):
        terms.append(passed(sent, axis, stride * step, True).astype(F32))
    while len(terms) > 1:
        apart = len(terms) // 2
        terms = [terms[at] + terms[at + apart] for at in range(apart)]
    return terms[0]


def sum_frames(values, across):
    size, cols = lax.axis_size("dp"), lax.axis_size("col")
    sent = values.astype(BF16)
    terms = []
    for step in range(size):
        pairs = []
        for i in range(size):
            other = i ^ step if size & (size - 1) == 0 else (i + step) % size
            pairs += [(i * cols + j, other * cols + (j ^ 1 if across else j)) for j in range(cols)]
        moved = lax.ppermute(sent, ("dp", "col"), pairs) if step or across else sent
        terms.append(moved.astype(F32))
    while len(terms) > 1:
        terms = [sum(terms[at : at + 2][1:], terms[at]) for at in range(0, len(terms), 2)]
    return terms[0]


def in_order(core, mine, theirs, axis):
    return jnp.where(
        core == 0, jnp.concatenate([mine, theirs], axis=axis), jnp.concatenate([theirs, mine], axis=axis)
    )


def step(
    tokens, ln_gain, qkv_weight, out_weight, readout_weight, conv_weight, head_weight, holo_cot
):
    frame_rows = tokens[0]
    cotangent = holo_cot[0]
    rows_dev, cols_dev = cotangent.shape[1:]
    tok_count, col_count = lax.axis_size("tok"), lax.axis_size("col")
    chips = tok_count // 2
    tok_at, half = lax.axis_index("tok"), lax.axis_index("col")
    core = lax.rem(tok_at, 2)
    chip_row = (tok_at - core) * rows_dev
    place = jnp.stack([core, half, chip_row, lax.rem(tok_at // 2, 2)]).astype(jnp.int32)
    cols = cols_dev * col_count

    gain, qkv_weight, out_weight = lax.optimization_barrier(
        (ln_gain.astype(F32).reshape(1, -1), qkv_weight, out_weight)
    )
    normed = normalize(frame_rows, gain)
    own_keyed, their_keyed = project((1, 2), place, normed, qkv_weight)
    own_keyed, their_keyed, normed = lax.optimization_barrier((own_keyed, their_keyed, normed))
    got_keyed = swapped(their_keyed, "tok")
    own_queries, their_queries = project((0,), place, normed, qkv_weight)
    queries = (own_queries, swapped(their_queries, "tok"))
    kept = own_keyed.shape[0] * HEAD

    def prepare(conv_weight, out_weight, readout_weight, frame_rows):
        forward, backward = arrange(conv_weight)
        own_out = lax.dynamic_slice_in_dim(out_weight, core * kept, kept, 0)
        folded = lax.dot_general(readout_weight, own_out, (((0,), (1,)), ((), ())), preferred_element_type=F32)
        direct = lax.dot_general(readout_weight, frame_rows, (((0,), (1,)), ((), ())), preferred_element_type=F32)
        return (forward, backward, folded, direct)

    def exact_rows(other_cot):
        wide_cot = in_order(half, cotangent, other_cot, 2)
        exact_cot = jnp.concatenate(split3(wide_cot.reshape(wide_cot.shape[0], -1)), axis=0)
        return jnp.pad(exact_cot, ((0, -exact_cot.shape[0] % 16), (0, 0)))

    state, blocks = None, [own_keyed, got_keyed]
    for turn in range(chips):
        arriving = []
        if turn < chips - 1:
            for block in blocks:
                arriving.append(round_ring(block))
        for at, block in enumerate(blocks):
            if turn == chips - 1 and at == 1:
                break
            state = absorb(queries, block, state)
            if at == 0 and turn == chips - 2:
                state, given, own_cot = lax.optimization_barrier(
                    (state, (conv_weight, out_weight, readout_weight, frame_rows), cotangent)
                )
                prepared, other_cot = prepare(*given), swapped(own_cot, "col")
            if at == 1 and turn == chips - 2:
                state, other_cot = lax.optimization_barrier((state, other_cot))
                exact_cot = exact_rows(other_cot)
            if at == 0 and turn == chips - 1:
                state, prepared, exact_cot = lax.optimization_barrier((state, prepared, exact_cot))
            if turn < chips - 2:
                arriving[at], state = lax.optimization_barrier((arriving[at], state))
        blocks = arriving if turn < chips - 1 else blocks
    forward, backward, folded, direct = prepared

    their_context, their_share = closing(1, queries, blocks[1], state, folded)
    own_context, own_share = closing(0, queries, blocks[1], state, folded)
    partial = own_share + swapped(their_share, "tok")
    partial = (partial + jnp.where(half == 0, direct, 0.0)).astype(BF16)
    own_map = (partial.astype(F32) + swapped(partial, "col").astype(F32)).astype(BF16)
    own_map = jnp.concatenate([own_map, exact_cot], axis=0)
    chip_map = jnp.concatenate([own_map, swapped(own_map, "tok")], axis=1)
    near = beside(chip_map)
    rows_chip = 2 * rows_dev
    maps = (chip_map, near, swapped(near, "tok"))
    holo, sums, gradient = network(
        place, maps, forward, backward, head_weight, own_context, their_context, cols, tok_count * rows_dev, col_count
    )
    holo = holo.reshape(-1, rows_chip, cols)
    hologram = lax.dynamic_slice(
        holo, (0, core * rows_dev, half * cols_dev), (holo.shape[0], rows_dev, cols_dev)
    )

    taps_wide = sums.shape[1]
    lanes = 128 * ((taps_wide + 127) // 128)
    rows = sums.shape[0]
    pieces = gradient.shape[0] // rows
    folded_gradient = [gradient[at * rows : (at + 1) * rows] for at in range(pieces)]
    sent = jnp.concatenate([jnp.pad(sums, ((0, 0), (0, lanes - taps_wide))), *folded_gradient], axis=1)
    summed = everyone(sent, "tok", 2, chips)
    own_terms = sum_frames(summed, False)
    far_terms = sum_frames(summed[:, :taps_wide], True)
    wide = gradient.shape[1]
    own_small = jnp.concatenate(
        [own_terms[:, lanes + at * wide : lanes + (at + 1) * wide] for at in range(pieces)], axis=0
    )
    small = in_order(core, own_small, swapped(own_small, "tok"), 1)
    out_grad = lax.dot_general(
        small, readout_weight.astype(F32), (((0,), (1,)), ((), ())), precision=lax.Precision.HIGHEST
    )
    layer_grad = in_order(half, own_terms[:, :taps_wide], far_terms, 0)
    conv_grad = in_order(core, layer_grad[None], swapped(layer_grad, "tok")[None], 0)
    return (hologram[None], conv_grad, out_grad)


def solution(mesh):
    in_specs = (
        P("dp", "tok", None),
        P(),
        P(None, None, "col"),
        P("col", None),
        P(),
        P(),
        P(),
        P("dp", None, "tok", "col"),
    )
    out_specs = (P("dp", None, "tok", "col"), P(), P("col", None))
    return jax.shard_map(step, mesh=mesh, in_specs=in_specs, out_specs=out_specs, check_vma=False)
```
